32 devices in a mesh: row: 8 (over y, x, core), col: 4 (over z).
Axes of the slice: x: 2, y: 2, z: 4, core: 2. Of those that a mesh axis runs over, the one named last changes fastest.
Arguments:
- alignment: float32 [32, 384, 64], P('col', 'row'), may hold values from -6 to 6
- pair_rep: float32 [384, 384, 128], P('row', 'col'), may hold values from -6 to 6
- seq_mask: int32 [32], P('col'), may hold values 0 or 1
- res_mask: int32 [384], P('row'), may hold values 0 or 1
- left_weight: float32 [64, 32], replicated, may hold values from -0.75 to 0.75
- right_weight: float32 [64, 32], replicated, may hold values from -0.75 to 0.75
- w_outer: float32 [1024, 128], replicated, may hold values from -4 to 4
- w_logits: float32 [128, 8], replicated, may hold values from -45 to 45
- value_weight: float32 [64, 256], replicated, may hold values from -0.75 to 0.75
- gate_weight: float32 [64, 256], replicated, may hold values from -0.75 to 0.75
- output_weight: float32 [256, 64], replicated, may hold values from -6 to 6
Outputs:
- alignment_out: float32 [32, 384, 64], P('col', 'row')
- pair_out: float32 [384, 384, 128], P('row', 'col')
The draws below stay inside these ranges and needn't reach their ends.
All inputs are finite; a program needn't handle non-finite values. No bound on the sum of `seq_mask` or of `res_mask` on one device may be relied on, other than what follows from the above.
Results may differ from the reference program's by a relative error of at most 0.0003.
Values sent between devices are 32-bit elements; how exact they have to be, the bound alone decides.
A program may use at most 128 MiB of HBM per device.

```python
import jax
import jax.numpy as jnp
from jax import lax

ALIGNED_WIDTH = 64
FACTOR_WIDTH = 32
PAIR_W = 128
AVERAGE_HEADS = 8
HEAD_CHANNELS = 32
RES_DEV = 48
SEQUENCE_COUNT = 32
RESIDUE_COUNT = 384
OUTER = 1024
N_ROW = 8


def draw_w_logits(key, part):
    first_key, second_key = jax.random.split(jax.random.fold_in(key, 11))
    normal_part = jnp.clip(jax.random.normal(first_key, (PAIR_W, AVERAGE_HEADS), jnp.float32), -5.0, 5.0)
    base = normal_part / PAIR_W ** 0.5
    levels = jnp.exp(jnp.linspace(jnp.log(0.5), jnp.log(2.0), AVERAGE_HEADS))
    shuffled = jax.random.permutation(second_key, AVERAGE_HEADS)
    return base * levels[shuffled][None, :]


def plant(array, key, smallest, top_value):
    extent = array.shape
    index_at = [jax.random.randint(jax.random.fold_in(key, axis), (), 0, extent[axis]) for axis in range(len(extent))]
    array = array.at[tuple(index_at)].set(smallest)
    longest = extent.index(max(extent))
    index_at[longest] = (index_at[longest] + 1) % extent[longest]
    return array.at[tuple(index_at)].set(top_value)


def level_of(stream_key, shape, cuts, low, largest):
    level = 1.0
    for position, parts in cuts:
        steps = jax.random.uniform(jax.random.fold_in(jax.random.fold_in(stream_key, 6), position), (parts,), jnp.float32, low / len(cuts), largest / len(cuts))
        level = level * jnp.repeat(jnp.exp(steps), shape[position] // parts).reshape((-1,) + (1,) * (len(shape) - 1 - position))
    return level


def gaussian(rng, dims, width, bound, pieces=(), dtype=jnp.bfloat16):
    result = width * jax.random.normal(rng, dims, jnp.float32)
    if pieces:
        result = result * level_of(rng, dims, pieces, -0.22, 0.18)
    return jnp.clip(result, -bound, bound).astype(dtype)


def setup_inputs(seed: int = 0) -> dict:
    arg_keys = jax.random.split(jax.random.key(seed), 12)
    alignment = gaussian(arg_keys[0], (SEQUENCE_COUNT, RESIDUE_COUNT, ALIGNED_WIDTH), 1.0, 6.0, ((0, 4), (1, 8)), jnp.float32)
    pair_rep = gaussian(arg_keys[1], (RESIDUE_COUNT, RESIDUE_COUNT, PAIR_W), 1.0, 6.0, ((0, 8), (1, 4)), jnp.float32)
    seq_mask = plant((jax.random.randint(arg_keys[2], (SEQUENCE_COUNT,), 0, 8) < 7).astype(jnp.int32), jax.random.fold_in(arg_keys[2], 1), 0, 1)
    res_mask = plant((jax.random.randint(arg_keys[3], (RESIDUE_COUNT,), 0, 8) < 7).astype(jnp.int32), jax.random.fold_in(arg_keys[3], 1), 0, 1)
    left_weight = gaussian(arg_keys[4], (ALIGNED_WIDTH, FACTOR_WIDTH), ALIGNED_WIDTH ** -0.5, 0.75, (), jnp.float32)
    right_weight = gaussian(arg_keys[5], (ALIGNED_WIDTH, FACTOR_WIDTH), ALIGNED_WIDTH ** -0.5, 0.75, (), jnp.float32)
    w_outer = gaussian(arg_keys[6], (OUTER, PAIR_W), 0.3, 4.0, (), jnp.float32)
    w_logits = draw_w_logits(jax.random.fold_in(arg_keys[11], 71), 0)
    value_weight = gaussian(arg_keys[8], (ALIGNED_WIDTH, AVERAGE_HEADS * HEAD_CHANNELS), ALIGNED_WIDTH ** -0.5, 0.75, (), jnp.float32)
    gate_weight = gaussian(arg_keys[9], (ALIGNED_WIDTH, AVERAGE_HEADS * HEAD_CHANNELS), ALIGNED_WIDTH ** -0.5, 0.75, (), jnp.float32)
    output_weight = gaussian(arg_keys[10], (AVERAGE_HEADS * HEAD_CHANNELS, ALIGNED_WIDTH), 0.5, 6.0, (), jnp.float32)
    return {"alignment": alignment, "pair_rep": pair_rep, "seq_mask": seq_mask, "res_mask": res_mask, "left_weight": left_weight, "right_weight": right_weight, "w_outer": w_outer, "w_logits": w_logits, "value_weight": value_weight, "gate_weight": gate_weight, "output_weight": output_weight}


epsilon = 1e-05
highest = lax.Precision.HIGHEST

def layer_norm(values):
    center = lax.optimization_barrier(jnp.mean(values, axis=-1, keepdims=True))
    centred = values - center
    return centred * lax.rsqrt(lax.optimization_barrier(jnp.mean(centred * centred, axis=-1, keepdims=True)) + epsilon)

def project(values, weight):
    return jnp.einsum('...c,cv->...v', values, weight, precision=highest)

def outer_block(left_rows, right_rows, w_outer):
    outer = jnp.einsum('sia,sjb->ijab', left_rows, right_rows, precision=highest)
    flat = outer.reshape(outer.shape[0] * outer.shape[1], outer.shape[2] * outer.shape[3])
    mapped = jnp.dot(flat, w_outer, precision=highest, preferred_element_type=jnp.float32)
    return mapped.reshape(outer.shape[0], outer.shape[1], w_outer.shape[1])

def reference(alignment, pair_rep, seq_mask, res_mask, left_weight, right_weight, w_outer, w_logits, value_weight, gate_weight, output_weight):
    normed = layer_norm(alignment)
    seq_live = seq_mask.astype(jnp.float32)
    res_live = res_mask.astype(jnp.float32)
    live = (seq_live[:, None] * res_live[None, :])[:, :, None]
    left_proj = project(normed, left_weight) * live
    right_proj = project(normed, right_weight) * live
    left_blocks = left_proj.reshape(SEQUENCE_COUNT, N_ROW, RES_DEV, FACTOR_WIDTH).transpose(1, 0, 2, 3)
    outer_sums = lax.map(lambda row_block: outer_block(row_block, right_proj, w_outer), left_blocks)
    outer_sums = outer_sums.reshape(RESIDUE_COUNT, RESIDUE_COUNT, PAIR_W)
    pair_count = jnp.maximum(res_live[:, None] * res_live[None, :] * jnp.sum(seq_live), 1.0)
    pair_out = pair_rep + outer_sums / pair_count[:, :, None]
    pair_normed = layer_norm(pair_out)
    logits = jnp.einsum('ijz,zh->hij', pair_normed, w_logits, precision=highest)
    logits = logits + ((res_live - 1.0) * 1000000000.0)[None, None, :]
    row_max = lax.optimization_barrier(jnp.max(logits, axis=2, keepdims=True))
    expo_terms = jnp.exp(logits - row_max)
    weights = expo_terms / lax.optimization_barrier(jnp.sum(expo_terms, axis=2, keepdims=True))
    values = project(normed, value_weight).reshape(SEQUENCE_COUNT, RESIDUE_COUNT, AVERAGE_HEADS, HEAD_CHANNELS)
    averaged = jnp.einsum('hij,sjhv->sihv', weights, values, precision=highest)
    averaged = averaged.reshape(SEQUENCE_COUNT, RESIDUE_COUNT, AVERAGE_HEADS * HEAD_CHANNELS)
    gate_open = jax.nn.sigmoid(project(normed, gate_weight))
    alignment_out = alignment + project(gate_open * averaged, output_weight)
    return (alignment_out, pair_out)
```

```python
import functools

import jax
import jax.numpy as jnp
from jax import lax
from jax.experimental import pallas as pl
from jax.experimental.pallas import tpu as pltpu
from jax.sharding import PartitionSpec as P

MESH = pl.DeviceIdType.MESH
F32 = jnp.float32
BF16 = jnp.bfloat16
epsilon = 1e-05
PAIR_VMEM = 48 * 1024 * 1024
AVERAGE_VMEM = 24 * 1024 * 1024
MIX_BYTES = 30 * 1024 * 1024
LANES = 128


def layer_norm(values):
    center = jnp.mean(values, axis=-1, keepdims=True)
    centred = values - center
    return centred * lax.rsqrt(jnp.mean(centred * centred, axis=-1, keepdims=True) + epsilon)


def split(values):
    high = values.astype(BF16)
    return high, (values - high.astype(F32)).astype(BF16)


def dot(left, right):
    return jnp.dot(left, right, preferred_element_type=F32)


def dot_t(left, right):
    return lax.dot_general(left, right, (((1,), (1,)), ((), ())), preferred_element_type=F32)


def t_dot(left, right):
    return lax.dot_general(left, right, (((0,), (0,)), ((), ())), preferred_element_type=F32)


def dot_split(left, right_high, right_low, multiply=dot):
    high, low = split(left)
    return multiply(high, right_high) + (multiply(low, right_high) + multiply(high, right_low))


def iota(shape, axis):
    return lax.broadcasted_iota(jnp.int32, shape, axis)


def stacked_dot(values, weights):
    count, half = values.shape[0], weights.shape[1] // 2
    high, low = split(values)
    out = dot(jnp.concatenate([high, low], axis=0), weights)
    out = out[:, :half] + out[:, half:]
    return out[:count] + out[count:]


def spread_heads(weight, heads, group, store):
    width, channels = weight.shape
    head_width = channels // heads
    both = jnp.concatenate(split(weight), axis=0)
    rows, lanes = iota((channels, LANES), 0), iota((channels, LANES), 1)
    own = iota((group * width, LANES), 0) // width == iota((group * width, LANES), 1) // head_width
    for h in range(heads):
        pick = jnp.where(rows == h * head_width + lanes % head_width, 1.0, 0.0).astype(BF16)
        tiled = dot(both, pick)
        parts = []
        for t in range(2):
            piece = jnp.concatenate([tiled[t * width : (t + 1) * width]] * group, axis=0)
            parts.append(jnp.where(own, piece, 0.0))
        store(h, jnp.concatenate(parts, axis=1).astype(BF16))


def pair_kernel(
    n_row,
    n_col,
    here,
    seq_in,
    res_in,
    align_in,
    left_w_in,
    right_w_in,
    outer_in,
    logits_w_in,
    value_w_in,
    gate_w_in,
    output_w_in,
    pair_in,
    pair_out,
    slots,
    norm_all,
    gate_out,
    value_bd,
    output_bd,
    align_ref,
    seq_ref,
    res_ref,
    left_w_ref,
    right_w_ref,
    outer_ref,
    logits_w_ref,
    value_w_ref,
    gate_w_ref,
    output_w_ref,
    rows_buf,
    masked_buf,
    block_buf,
    right_buf,
    left_ref,
    right_ref,
    gate_bd,
    wl_buf,
    w_buf,
    l_buf,
    r_buf,
    mask_buf,
    high_buf,
    low_buf,
    load_sem,
    left_send,
    left_recv,
    turn_sem,
    right_send,
    right_recv,
    share_send,
    share_recv,
    logits_send,
    logits_recv,
    norm_send,
    norm_recv,
    relay_send,
    relay_recv,
):
    row, col = lax.axis_index("row"), lax.axis_index("col")
    n = n_row * n_col
    me = row * n_col + col
    barrier = pltpu.get_barrier_semaphore()
    loads = [
        pltpu.make_async_copy(source, target, load_sem.at[at])
        for at, (source, target) in enumerate(
            [
                (align_in, align_ref),
                (seq_in, seq_ref),
                (res_in, res_ref),
                (right_w_in, right_w_ref),
                (left_w_in, left_w_ref),
                (outer_in, outer_ref),
                (gate_w_in, gate_w_ref),
                (value_w_in, value_w_ref),
                (logits_w_in, logits_w_ref),
                (output_w_in, output_w_ref),
                (pair_in, pair_out),
            ]
        )
    ]
    for load in loads:
        load.start()

    def greet(step, carry):
        other = lax.rem(me + step, n)
        pl.semaphore_signal(
            barrier,
            inc=1,
            device_id=(other // n_col, lax.rem(other, n_col)),
            device_id_type=MESH,
        )
        return carry

    lax.fori_loop(1, n, greet, 0)

    seqs, rows, width = align_ref.shape
    factor = right_w_ref.shape[0]
    ratio, k_col = n_row // n_col, factor * seqs
    half = n_row // 2
    chip, core = row // 2, lax.rem(row, 2)
    partner = 2 * chip + 1 - core
    cols, pair_width = pair_out.shape[1], pair_out.shape[2]
    heads = logits_w_ref.shape[0]
    quarter = rows * seqs // 4
    steps = rows // here
    parts = LANES // (here * heads)
    jrows = cols // parts
    group = LANES * heads // value_w_ref.shape[1]
    premixed = high_buf.shape[0] == rows
    depth = n_col * k_col

    def peer_row(k):
        return 2 * lax.rem(chip + k, half) + core

    relayed = n_col >= 4
    at_high, at_low = col == n_col - 2, col == 1
    relay = at_high | at_low
    far_src = jnp.where(at_low, n_col - 1, 0)
    far_dest = jnp.where(at_low, 0, n_col - 1)

    def is_far(other):
        return (other - col == n_col - 1) | (col - other == n_col - 1)

    def near(other, action):
        if relayed:
            pl.when(jnp.logical_not(is_far(other)))(action)
        else:
            action()

    def unless_relayed(src, action):
        if relayed:
            pl.when(jnp.logical_not(relay & (src == far_src)))(action)
        else:
            action()

    for at in range(5):
        loads[at].wait()
    res_row = res_ref[...].astype(F32)
    diag = iota((rows, rows), 0) == iota((rows, rows), 1)

    def column(values):
        return jnp.sum(
            jnp.where(diag, jnp.broadcast_to(values, (rows, rows)), 0.0), axis=1, keepdims=True
        )

    res_col = column(res_row)
    spread = jnp.broadcast_to(right_w_ref[...][:, None, :], (factor, seqs, width))
    row_seq = iota((factor, seqs, width), 1)
    seq_sum = 0.0
    for s in range(seqs):
        normed = layer_norm(align_ref[s])
        norm_all[row, :, s * width : (s + 1) * width] = normed
        live = seq_ref[s].astype(F32)
        seq_sum = seq_sum + live
        masked = normed * (res_col * live)
        masked_buf[:, s * width : (s + 1) * width] = masked
        rows_buf[pl.ds(s, rows, stride=seqs), :] = masked
        block_buf[:, s * width : (s + 1) * width] = jnp.where(row_seq == s, spread, 0.0).reshape(
            factor * seqs, width
        )
    wr_high, wr_low = split(block_buf[...])
    right_buf[0:rows, :] = dot_split(masked_buf[...], wr_high, wr_low, dot_t)
    right_buf[rows : rows + 8, 0:rows] = jnp.broadcast_to(res_row, (8, rows))
    right_buf[rows : rows + 8, rows:] = jnp.zeros((8, right_buf.shape[1] - rows), F32)
    wl_high, wl_low = split(left_w_ref[...])
    left = dot_split(rows_buf[...], wl_high, wl_low, dot_t)
    for g in range(4):
        left_ref[col, 0:quarter, g * factor : (g + 1) * factor] = left[
            g * quarter : (g + 1) * quarter
        ]
    left_ref[col, quarter : quarter + 8, :] = jnp.full((8, left_ref.shape[2]), seq_sum, F32)

    pl.semaphore_wait(barrier, n - 1)
    dest = row // ratio
    spot = col * ratio + lax.rem(row, ratio)
    away = dest != col
    turn = pltpu.make_async_remote_copy(
        right_buf,
        right_ref.at[spot],
        turn_sem.at[0],
        turn_sem.at[1],
        device_id=(spot, dest),
        device_id_type=MESH,
    )
    stay = pltpu.make_async_copy(right_buf, right_ref.at[spot], turn_sem.at[1])

    @pl.when(away)
    def _():
        turn.start()

    @pl.when(jnp.logical_not(away))
    def _():
        stay.start()

    def left_copy(k):
        return pltpu.make_async_remote_copy(
            left_ref.at[col],
            left_ref.at[col],
            left_send.at[k],
            left_recv.at[col],
            device_id=(row, lax.rem(col + k, n_col)),
            device_id_type=MESH,
        )

    def left_forward():
        return pltpu.make_async_remote_copy(
            left_ref.at[far_src],
            left_ref.at[far_src],
            left_send.at[0],
            left_recv.at[far_src],
            device_id=(row, far_dest),
            device_id_type=MESH,
        )

    def left_wait(src):
        pltpu.make_async_copy(left_ref.at[src], left_ref.at[src], left_recv.at[src]).wait()

    for k in range(1, n_col):
        near(lax.rem(col + k, n_col), left_copy(k).start)

    def right_copy(k):
        return pltpu.make_async_remote_copy(
            right_ref.at[row],
            right_ref.at[row],
            right_send.at[k],
            right_recv.at[half - k],
            device_id=(peer_row(k), col),
            device_id_type=MESH,
        )

    def share_copy(k):
        src = peer_row(k)
        return pltpu.make_async_remote_copy(
            right_ref.at[src],
            right_ref.at[src],
            share_send.at[k],
            share_recv.at[k],
            device_id=(partner, col),
            device_id_type=MESH,
        )

    def norm_copy(k):
        return pltpu.make_async_remote_copy(
            norm_all.at[row],
            norm_all.at[row],
            norm_send.at[k],
            norm_recv.at[half - k],
            device_id=(peer_row(k), col),
            device_id_type=MESH,
        )

    def relay_copy(k):
        return pltpu.make_async_remote_copy(
            norm_all.at[peer_row(k)],
            norm_all.at[peer_row(k)],
            relay_send.at[k],
            relay_recv.at[k],
            device_id=(partner, col),
            device_id_type=MESH,
        )

    loads[5].wait()
    for b in range(factor):
        high, low = split(outer_ref[pl.ds(b, factor, stride=factor), :])
        lanes = slice(b * pair_width, (b + 1) * pair_width)
        w_buf[0:factor, lanes] = high
        w_buf[factor : 2 * factor, lanes] = low
        w_buf[2 * factor : 3 * factor, lanes] = high

    def left_rows(c, at):
        packed = left_ref[c, 0:quarter, :]
        high = packed.astype(BF16).astype(F32)
        low = packed - high
        for g in range(4):
            lanes = slice(g * factor, (g + 1) * factor)
            pieces = [high[:, lanes], high[:, lanes], low[:, lanes]]
            l_buf[at, g * quarter : (g + 1) * quarter, :] = jnp.concatenate(
                pieces, axis=1
            ).astype(BF16)

    def mix(l_rows, c, count):
        for nb in range(factor // 2):
            mixed = dot(l_rows, w_buf[:, nb * 2 * pair_width : (nb + 1) * 2 * pair_width])
            tiles = jnp.concatenate(
                [
                    mixed[:, :pair_width].reshape(count, seqs, pair_width),
                    mixed[:, pair_width:].reshape(count, seqs, pair_width),
                ],
                axis=1,
            )
            high, low = split(tiles)
            high_buf[:, c, nb] = high
            low_buf[:, c, nb] = low

    def prepare():
        for at in range(6, 11):
            loads[at].wait()

        def keep_value(h, block):
            value_bd[h] = block

        def keep_gate(h, block):
            gate_bd[h] = block

        spread_heads(gate_w_ref[...], heads, group, keep_gate)
        spread_heads(value_w_ref[...], heads, group, keep_value)
        for g in range(seqs // group):
            own = norm_all[row, :, g * group * width : (g + 1) * group * width]
            for h in range(heads):
                gate_out[g, h] = jax.nn.sigmoid(stacked_dot(own, gate_bd[h]))
        channels = output_w_ref.shape[1]
        head_width = channels // heads
        lanes = iota((width, group * width), 1)
        pick = jnp.where(iota((width, group * width), 0) == lanes % width, 1.0, 0.0).astype(BF16)
        own = (iota((2 * group * head_width, group * width), 0) // head_width) % group == iota(
            (2 * group * head_width, group * width), 1
        ) // width
        for t, half_w in enumerate(split(output_w_ref[...])):
            tiled = t_dot(half_w, pick)
            for hp in range(heads // 2):
                pieces = []
                for hh in range(2):
                    first = (2 * hp + hh) * head_width
                    pieces += [tiled[first : first + head_width]] * group
                output_bd[t, hp] = jnp.where(own, jnp.concatenate(pieces, axis=0), 0.0).astype(BF16)
        lanes = iota((heads, 2 * LANES), 1)
        low_half = iota((pair_width, 2 * LANES), 1) >= LANES
        w_high, w_low = split(logits_w_ref[...])
        for i in range(here):
            pick = jnp.where(
                ((lanes // here) % heads == iota((heads, 2 * LANES), 0)) & (lanes % here == i),
                1.0,
                0.0,
            ).astype(BF16)
            block = jnp.where(low_half, t_dot(w_low, pick), t_dot(w_high, pick))
            wl_buf[i // 2, (i % 2) * pair_width : (i % 2 + 1) * pair_width, :] = block.astype(BF16)

    low_end = col < (n_col + 1) // 2
    spot_in = jnp.where(low_end, col, n_col - 1 - col)

    def stage(k, carry):
        order = jnp.where(k - 1 < spot_in, k - 1, k)
        src = jnp.where(low_end, order, n_col - 1 - order)
        src = jnp.where(k == 0, col, src)

        @pl.when(k == 1)
        def _():
            prepare()
            pltpu.make_async_copy(right_buf, right_ref.at[row], turn_sem.at[1]).wait()
            for k2 in range(1, half):
                right_copy(k2).start()
            share_copy(0).start()
            if relayed:

                @pl.when(relay)
                def _():
                    left_wait(far_src)
                    left_forward().start()

        @pl.when(k == n_col - 1)
        def _():
            for k2 in range(1, half):
                pltpu.make_async_copy(
                    right_buf, right_ref.at[peer_row(k2)], right_recv.at[k2]
                ).wait()
                share_copy(k2).start()
            relay_copy(0).start()
            for k2 in range(1, half):
                norm_copy(k2).start()

        @pl.when(k > 0)
        def _():
            unless_relayed(src, lambda: left_wait(src))

        at = 0 if premixed else src
        left_rows(src, at)
        if premixed:
            mix(l_buf[0], src, rows)
        return carry

    lax.fori_loop(0, n_col, stage, 0)
    for k in range(half):
        src = 2 * lax.rem(chip + k, half) + 1 - core
        pltpu.make_async_copy(right_buf, right_ref.at[src], share_recv.at[k]).wait()
    count = left_ref[0, quarter : quarter + 1, 0:1]
    for c in range(1, n_col):
        count = count + left_ref[c, quarter : quarter + 1, 0:1]
    scale = 1.0 / jnp.maximum(count, 1.0)
    for c in range(n_col):
        for t in range(ratio):
            high_r, low_r = split(right_ref[c * ratio + t, 0:rows, :])
            lanes = slice(c * k_col, (c + 1) * k_col)
            r_buf[t * rows : (t + 1) * rows, lanes] = high_r
            r_buf[cols + t * rows : cols + (t + 1) * rows, lanes] = low_r
    res_cols = jnp.concatenate(
        [column(right_ref[t, rows : rows + 1, 0:rows]) for t in range(ratio)], axis=0
    )
    part_of = iota((jrows, LANES), 1) // (here * heads)
    mask = jnp.zeros((jrows, LANES), F32)
    for p in range(parts):
        dead = (res_cols[p * jrows : (p + 1) * jrows] - 1.0) * 1000000000.0
        mask = jnp.where(part_of == p, dead, mask)
    mask_buf[...] = mask

    def chunk(at):
        return pl.ds(pl.multiple_of(at * jrows, jrows), jrows)

    def logits_copy(k, at):
        return pltpu.make_async_remote_copy(
            slots.at[col, chunk(at)],
            slots.at[col, chunk(at)],
            logits_send.at[k, at],
            logits_recv.at[col, at],
            device_id=(row, lax.rem(col + k, n_col)),
            device_id_type=MESH,
        )

    def logits_forward(at):
        return pltpu.make_async_remote_copy(
            slots.at[far_src, chunk(at)],
            slots.at[far_src, chunk(at)],
            logits_send.at[0, at],
            logits_recv.at[far_src, at],
            device_id=(row, far_dest),
            device_id_type=MESH,
        )

    def logits_wait(src, at):
        pltpu.make_async_copy(
            slots.at[src, chunk(at)], slots.at[src, chunk(at)], logits_recv.at[src, at]
        ).wait()

    def pass_on(at):
        @pl.when(relay)
        def _():
            logits_wait(far_src, at)
            logits_forward(at).start()

    lag = 2

    def body(step, carry):
        first_row = pl.multiple_of(step * here, here)
        if not premixed:
            size = here * seqs
            for c in range(n_col):
                mix(l_buf[c, pl.ds(pl.multiple_of(step * size, size), size), :], c, here)
        r_both = r_buf[...]
        total = None
        for p in range(here // 2):
            at = [2 * p + t + (first_row if premixed else 0) for t in range(2)]
            right_high = jnp.concatenate(
                [high_buf[i].reshape(depth, pair_width) for i in at], axis=1
            )
            right_low = jnp.concatenate([low_buf[i].reshape(depth, pair_width) for i in at], axis=1)
            first = dot(r_both, right_high)
            sums = first[:cols] + (first[cols:] + dot(r_both[:cols], right_low))
            high, low = [], []
            for t in range(2):
                i = first_row + 2 * p + t
                pair = pair_out[i] + sums[:, t * pair_width : (t + 1) * pair_width] * scale
                pair_out[i] = pair
                pieces = split(layer_norm(pair))
                high.append(pieces[0])
                low.append(pieces[1])
            both = jnp.concatenate(
                [jnp.concatenate(high, axis=1), jnp.concatenate(low, axis=1)], axis=0
            )
            out = dot(both, wl_buf[p])
            out = out[:, :LANES] + out[:, LANES:]
            out = out[:cols] + out[cols:]
            total = out if total is None else total + out
        logits = total[:jrows]
        for p in range(1, parts):
            logits = jnp.where(part_of == p, total[p * jrows : (p + 1) * jrows], logits)
        slots[col, chunk(step), :] = logits + mask_buf[...]
        for k in range(1, n_col):
            near(lax.rem(col + k, n_col), logits_copy(k, step).start)
        if relayed:

            @pl.when(step >= lag)
            def _():
                pass_on(step - lag)

        @pl.when(step == steps // 2)
        def _():
            for k in range(1, half):
                pltpu.make_async_copy(
                    norm_all.at[row], norm_all.at[peer_row(k)], norm_recv.at[k]
                ).wait()
                relay_copy(k).start()

        return carry

    lax.fori_loop(0, steps, body, 0)
    if relayed:
        for at in range(steps - lag, steps):
            pass_on(at)
    for k in range(half):
        other = 2 * lax.rem(chip + k, half) + 1 - core
        pltpu.make_async_copy(norm_all.at[row], norm_all.at[other], relay_recv.at[k]).wait()
        relay_copy(k).wait_send()
        share_copy(k).wait_send()
    for k in range(1, half):
        norm_copy(k).wait_send()
        right_copy(k).wait_send()
    for k in range(1, n_col):
        near(lax.rem(col + k, n_col), left_copy(k).wait_send)

    @pl.when(away)
    def _():
        turn.wait_send()

    if relayed:

        @pl.when(relay)
        def _():
            left_forward().wait_send()

    def drain(at, carry):
        for k in range(1, n_col):
            other = lax.rem(col + k, n_col)
            near(other, logits_copy(k, at).wait_send)
            unless_relayed(other, lambda: logits_wait(other, at))
        if relayed:

            @pl.when(relay)
            def _():
                logits_forward(at).wait_send()

        return carry

    lax.fori_loop(0, steps, drain, 0)


def average_kernel(
    here,
    slots,
    norm_ref,
    gate_ref,
    value_bd,
    output_bd,
    align_ref,
    pair_ref,
    out_any,
    pair_any,
    out_buf,
    sems,
):
    place = pltpu.make_async_copy(pair_ref, pair_any, sems.at[0])
    place.start()
    seqs, rows, width = align_ref.shape
    n_col, total_rows, _ = slots.shape
    groups, heads = gate_ref.shape[0], gate_ref.shape[1]
    group = seqs // groups
    steps = rows // here
    jrows = total_rows // steps
    wide = here * heads
    parts = LANES // wide
    norm_high, norm_low = split(norm_ref[...])
    part_of = iota((jrows, LANES), 1) // wide

    def over_parts(values, combine):
        out = values
        for p in range(1, parts):
            out = combine(out, pltpu.roll(values, p * wide, 1))
        return out

    weights = []
    for t in range(steps):
        pieces = [slots[c, t * jrows : (t + 1) * jrows, :] for c in range(n_col)]
        top = pieces[0]
        for piece in pieces[1:]:
            top = jnp.maximum(top, piece)
        top = over_parts(jnp.max(top, axis=0, keepdims=True), jnp.maximum)
        pieces = [jnp.exp(piece - top) for piece in pieces]
        total = pieces[0]
        for piece in pieces[1:]:
            total = total + piece
        inverse = 1.0 / over_parts(jnp.sum(total, axis=0, keepdims=True), jnp.add)
        weights.append([piece * inverse for piece in pieces])
    turned = []
    for t in range(0, steps, parts):
        blocks = []
        for c in range(n_col):
            for p in range(parts):
                block = None
                for q in range(parts):
                    value = weights[t + q][c]
                    shift = (q - p) % parts * wide
                    if shift:
                        value = pltpu.roll(value, shift, 1)
                    block = value if block is None else jnp.where(part_of == q, value, block)
                blocks.append(block)
        turned.append(jnp.concatenate(blocks, axis=0).T)
    mixed = dot_split(jnp.concatenate(turned, axis=0), norm_high, norm_low)
    for g in range(groups):
        gated = []
        for h in range(heads):
            own = jnp.concatenate(
                [
                    mixed[
                        t * wide + h * here : t * wide + (h + 1) * here,
                        g * group * width : (g + 1) * group * width,
                    ]
                    for t in range(steps)
                ],
                axis=0,
            )
            gated.append(stacked_dot(own, value_bd[h]) * gate_ref[g, h])
        out = None
        for hp in range(heads // 2):
            part = dot_split(
                jnp.concatenate(gated[2 * hp : 2 * hp + 2], axis=1),
                output_bd[0, hp],
                output_bd[1, hp],
            )
            out = part if out is None else out + part
        for s in range(group):
            at = g * group + s
            out_buf[at] = align_ref[at] + out[:, s * width : (s + 1) * width]
        pltpu.make_async_copy(
            out_buf.at[pl.ds(g * group, group)],
            out_any.at[pl.ds(g * group, group)],
            sems.at[1 + g],
        ).start()
    for g in range(groups):
        pltpu.make_async_copy(
            out_buf.at[pl.ds(g * group, group)],
            out_any.at[pl.ds(g * group, group)],
            sems.at[1 + g],
        ).wait()
    place.wait()


def per_device(
    n_row,
    n_col,
    alignment,
    pair_rep,
    seq_mask,
    res_mask,
    left_weight,
    right_weight,
    w_outer,
    w_logits,
    value_weight,
    gate_weight,
    output_weight,
):
    seqs, rows, width = alignment.shape
    cols, pair_width = pair_rep.shape[1], pair_rep.shape[2]
    factor = left_weight.shape[1]
    heads = w_logits.shape[1]
    channels = value_weight.shape[1]
    k_col = factor * seqs
    quarter = rows * seqs // 4
    half = n_row // 2
    here = 8
    steps = rows // here
    jrows = cols * here * heads // LANES
    group = LANES * heads // channels
    groups = seqs // group
    vmem = pl.BlockSpec(memory_space=pltpu.VMEM)
    anywhere = pl.BlockSpec(memory_space=pl.ANY)
    dma = pltpu.SemaphoreType.DMA
    left_shape = (quarter + 8, 4 * factor)
    right_shape = (rows + 8, k_col)
    mix_row = (n_col, factor // 2, 2 * seqs, pair_width)
    row_bytes = 4 * n_col * k_col * pair_width
    premixed = rows * row_bytes <= MIX_BYTES
    held = rows if premixed else here
    pair_new, slots, norm_all, gate, value_bd, output_bd, align = pl.pallas_call(
        functools.partial(pair_kernel, n_row, n_col, here),
        out_shape=(
            pltpu.VMEM(pair_rep.shape, F32),
            pltpu.VMEM((n_col, steps * jrows, LANES), F32),
            pltpu.VMEM((n_row, rows, seqs * width), F32),
            pltpu.VMEM((groups, heads, rows, LANES), F32),
            pltpu.VMEM((heads, group * width, 2 * LANES), BF16),
            pltpu.VMEM((2, heads // 2, 2 * LANES, group * width), BF16),
            pltpu.VMEM(alignment.shape, F32),
        ),
        in_specs=[anywhere] * 11,
        out_specs=(vmem,) * 7,
        scratch_shapes=[
            pltpu.SMEM((seqs,), jnp.int32),
            pltpu.VMEM((1, rows), jnp.int32),
            pltpu.VMEM((factor, width), F32),
            pltpu.VMEM((factor, width), F32),
            pltpu.VMEM(w_outer.shape, F32),
            pltpu.VMEM((heads, pair_width), F32),
            pltpu.VMEM(value_weight.shape, F32),
            pltpu.VMEM(gate_weight.shape, F32),
            pltpu.VMEM((width, channels), F32),
            pltpu.VMEM((rows * seqs, width), F32),
            pltpu.VMEM((rows, seqs * width), F32),
            pltpu.VMEM((k_col, seqs * width), F32),
            pltpu.VMEM(right_shape, F32),
            pltpu.VMEM((n_col,) + left_shape, F32),
            pltpu.VMEM((n_row,) + right_shape, F32),
            pltpu.VMEM((heads, group * width, 2 * LANES), BF16),
            pltpu.VMEM((here // 2, 2 * pair_width, 2 * LANES), BF16),
            pltpu.VMEM((3 * factor, factor * pair_width), BF16),
            pltpu.VMEM((1 if premixed else n_col, rows * seqs, 3 * factor), BF16),
            pltpu.VMEM((2 * cols, n_col * k_col), BF16),
            pltpu.VMEM((jrows, LANES), F32),
            pltpu.VMEM((held,) + mix_row, BF16),
            pltpu.VMEM((held,) + mix_row, BF16),
            dma((11,)),
            dma((n_col,)),
            dma((n_col,)),
            dma((2,)),
            dma((half,)),
            dma((half,)),
            dma((half,)),
            dma((half,)),
            dma((n_col, steps)),
            dma((n_col, steps)),
            dma((half,)),
            dma((half,)),
            dma((half,)),
            dma((half,)),
        ],
        compiler_params=pltpu.CompilerParams(
            collective_id=0, has_side_effects=True, vmem_limit_bytes=PAIR_VMEM
        ),
        name="pair",
    )(
        seq_mask,
        res_mask.reshape(1, rows),
        alignment,
        left_weight.T,
        right_weight.T,
        w_outer,
        w_logits.T,
        value_weight,
        gate_weight,
        output_weight.T,
        pair_rep,
    )
    alignment_out, pair_final = pl.pallas_call(
        functools.partial(average_kernel, here),
        out_shape=(
            jax.ShapeDtypeStruct(alignment.shape, F32),
            jax.ShapeDtypeStruct(pair_rep.shape, F32),
        ),
        in_specs=[vmem] * 7,
        out_specs=(anywhere, anywhere),
        scratch_shapes=[pltpu.VMEM(alignment.shape, F32), dma((1 + groups,))],
        compiler_params=pltpu.CompilerParams(vmem_limit_bytes=AVERAGE_VMEM),
        name="average",
    )(
        slots,
        norm_all.reshape(n_row * rows, seqs * width),
        gate,
        value_bd,
        output_bd,
        align,
        pair_new,
    )
    return (alignment_out, pair_final)


def solution(mesh):
    in_specs = (P("col", "row", None), P("row", "col", None), P("col"), P("row")) + (P(),) * 7
    out_specs = (P("col", "row", None), P("row", "col", None))
    return jax.shard_map(
        functools.partial(per_device, mesh.shape["row"], mesh.shape["col"]),
        mesh=mesh,
        in_specs=in_specs,
        out_specs=out_specs,
        check_vma=False,
    )
```

```python
import functools

import jax
import jax.numpy as jnp
from jax import lax
from jax.experimental import pallas as pl
from jax.experimental.pallas import tpu as pltpu
from jax.sharding import PartitionSpec as P

MESH = pl.DeviceIdType.MESH
F32 = jnp.float32
BF16 = jnp.bfloat16
epsilon = 1e-05
PAIR_VMEM = 48 * 1024 * 1024
AVERAGE_VMEM = 24 * 1024 * 1024
MIX_BYTES = 30 * 1024 * 1024
LANES = 128


def layer_norm(values):
    center = jnp.mean(values, axis=-1, keepdims=True)
    centred = values - center
    return centred * lax.rsqrt(jnp.mean(centred * centred, axis=-1, keepdims=True) + epsilon)


def split(values):
    high = values.astype(BF16)
    return high, (values - high.astype(F32)).astype(BF16)


def dot(left, right):
    return jnp.dot(left, right, preferred_element_type=F32)


def dot_t(left, right):
    return lax.dot_general(left, right, (((1,), (1,)), ((), ())), preferred_element_type=F32)


def t_dot(left, right):
    return lax.dot_general(left, right, (((0,), (0,)), ((), ())), preferred_element_type=F32)


def dot_split(left, right_high, right_low, multiply=dot):
    high, low = split(left)
    return multiply(high, right_high) + (multiply(low, right_high) + multiply(high, right_low))


def iota(shape, axis):
    return lax.broadcasted_iota(jnp.int32, shape, axis)


def stacked_dot(values, weights):
    count, half = values.shape[0], weights.shape[1] // 2
    high, low = split(values)
    out = dot(jnp.concatenate([high, low], axis=0), weights)
    out = out[:, :half] + out[:, half:]
    return out[:count] + out[count:]


def spread_heads(weight, heads, group, store):
    width, channels = weight.shape
    head_width = channels // heads
    both = jnp.concatenate(split(weight), axis=0)
    rows, lanes = iota((channels, LANES), 0), iota((channels, LANES), 1)
    own = iota((group * width, LANES), 0) // width == iota((group * width, LANES), 1) // head_width
    for h in range(heads):
        pick = jnp.where(rows == h * head_width + lanes % head_width, 1.0, 0.0).astype(BF16)
        tiled = dot(both, pick)
        parts = []
        for t in range(2):
            piece = jnp.concatenate([tiled[t * width : (t + 1) * width]] * group, axis=0)
            parts.append(jnp.where(own, piece, 0.0))
        store(h, jnp.concatenate(parts, axis=1).astype(BF16))


def pair_kernel(
    n_row,
    n_col,
    here,
    seq_in,
    res_in,
    align_in,
    left_w_in,
    right_w_in,
    outer_in,
    logits_w_in,
    value_w_in,
    gate_w_in,
    output_w_in,
    pair_in,
    pair_out,
    slots,
    norm_all,
    gate_out,
    value_bd,
    output_bd,
    align_ref,
    seq_ref,
    res_ref,
    left_w_ref,
    right_w_ref,
    outer_ref,
    logits_w_ref,
    value_w_ref,
    gate_w_ref,
    output_w_ref,
    rows_buf,
    masked_buf,
    block_buf,
    right_buf,
    left_ref,
    right_ref,
    gate_bd,
    wl_buf,
    w_buf,
    l_buf,
    r_buf,
    mask_buf,
    high_buf,
    low_buf,
    pair_ref,
    load_sem,
    left_send,
    left_recv,
    turn_sem,
    right_send,
    right_recv,
    share_send,
    share_recv,
    logits_send,
    logits_recv,
    norm_send,
    norm_recv,
    relay_send,
    relay_recv,
):
    row, col = lax.axis_index("row"), lax.axis_index("col")
    n = n_row * n_col
    me = row * n_col + col
    barrier = pltpu.get_barrier_semaphore()
    loads = [
        pltpu.make_async_copy(source, target, load_sem.at[at])
        for at, (source, target) in enumerate(
            [
                (align_in, align_ref),
                (seq_in, seq_ref),
                (res_in, res_ref),
                (right_w_in, right_w_ref),
                (left_w_in, left_w_ref),
                (outer_in, outer_ref),
                (gate_w_in, gate_w_ref),
                (value_w_in, value_w_ref),
                (logits_w_in, logits_w_ref),
                (output_w_in, output_w_ref),
                (pair_in, pair_ref),
            ]
        )
    ]
    for load in loads:
        load.start()

    def greet(step, carry):
        other = lax.rem(me + step, n)
        pl.semaphore_signal(
            barrier,
            inc=1,
            device_id=(other // n_col, lax.rem(other, n_col)),
            device_id_type=MESH,
        )
        return carry

    lax.fori_loop(1, n, greet, 0)

    seqs, rows, width = align_ref.shape
    factor = right_w_ref.shape[0]
    ratio, k_col = n_row // n_col, factor * seqs
    half = n_row // 2
    chip, core = row // 2, lax.rem(row, 2)
    partner = 2 * chip + 1 - core
    cols, pair_width = pair_out.shape[1], pair_out.shape[2]
    heads = logits_w_ref.shape[0]
    quarter = rows * seqs // 4
    steps = rows // here
    parts = LANES // (here * heads)
    jrows = cols // parts
    group = LANES * heads // value_w_ref.shape[1]
    premixed = high_buf.shape[0] == rows
    depth = n_col * k_col

    def peer_row(k):
        return 2 * lax.rem(chip + k, half) + core

    relayed = n_col >= 4
    at_high, at_low = col == n_col - 2, col == 1
    relay = at_high | at_low
    far_src = jnp.where(at_low, n_col - 1, 0)
    far_dest = jnp.where(at_low, 0, n_col - 1)

    def is_far(other):
        return (other - col == n_col - 1) | (col - other == n_col - 1)

    def near(other, action):
        if relayed:
            pl.when(jnp.logical_not(is_far(other)))(action)
        else:
            action()

    def unless_relayed(src, action):
        if relayed:
            pl.when(jnp.logical_not(relay & (src == far_src)))(action)
        else:
            action()

    for at in range(5):
        loads[at].wait()
    res_row = res_ref[...].astype(F32)
    diag = iota((rows, rows), 0) == iota((rows, rows), 1)

    def column(values):
        return jnp.sum(
            jnp.where(diag, jnp.broadcast_to(values, (rows, rows)), 0.0), axis=1, keepdims=True
        )

    res_col = column(res_row)
    spread = jnp.broadcast_to(right_w_ref[...][:, None, :], (factor, seqs, width))
    row_seq = iota((factor, seqs, width), 1)
    seq_sum = 0.0
    for s in range(seqs):
        normed = layer_norm(align_ref[s])
        norm_all[row, :, s * width : (s + 1) * width] = normed
        live = seq_ref[s].astype(F32)
        seq_sum = seq_sum + live
        masked = normed * (res_col * live)
        masked_buf[:, s * width : (s + 1) * width] = masked
        rows_buf[pl.ds(s, rows, stride=seqs), :] = masked
        block_buf[:, s * width : (s + 1) * width] = jnp.where(row_seq == s, spread, 0.0).reshape(
            factor * seqs, width
        )
    wr_high, wr_low = split(block_buf[...])
    right_buf[0:rows, :] = dot_split(masked_buf[...], wr_high, wr_low, dot_t)
    right_buf[rows : rows + 8, 0:rows] = jnp.broadcast_to(res_row, (8, rows))
    right_buf[rows : rows + 8, rows:] = jnp.zeros((8, right_buf.shape[1] - rows), F32)
    wl_high, wl_low = split(left_w_ref[...])
    left = dot_split(rows_buf[...], wl_high, wl_low, dot_t)
    for g in range(4):
        left_ref[col, 0:quarter, g * factor : (g + 1) * factor] = left[
            g * quarter : (g + 1) * quarter
        ]
    left_ref[col, quarter : quarter + 8, :] = jnp.full((8, left_ref.shape[2]), seq_sum, F32)

    pl.semaphore_wait(barrier, n - 1)
    dest = row // ratio
    spot = col * ratio + lax.rem(row, ratio)
    away = dest != col
    turn = pltpu.make_async_remote_copy(
        right_buf,
        right_ref.at[spot],
        turn_sem.at[0],
        turn_sem.at[1],
        device_id=(spot, dest),
        device_id_type=MESH,
    )
    stay = pltpu.make_async_copy(right_buf, right_ref.at[spot], turn_sem.at[1])

    @pl.when(away)
    def _():
        turn.start()

    @pl.when(jnp.logical_not(away))
    def _():
        stay.start()

    def left_copy(k):
        return pltpu.make_async_remote_copy(
            left_ref.at[col],
            left_ref.at[col],
            left_send.at[k],
            left_recv.at[col],
            device_id=(row, lax.rem(col + k, n_col)),
            device_id_type=MESH,
        )

    def left_forward():
        return pltpu.make_async_remote_copy(
            left_ref.at[far_src],
            left_ref.at[far_src],
            left_send.at[0],
            left_recv.at[far_src],
            device_id=(row, far_dest),
            device_id_type=MESH,
        )

    def left_wait(src):
        pltpu.make_async_copy(left_ref.at[src], left_ref.at[src], left_recv.at[src]).wait()

    for k in range(1, n_col):
        near(lax.rem(col + k, n_col), left_copy(k).start)

    def right_copy(k):
        return pltpu.make_async_remote_copy(
            right_ref.at[row],
            right_ref.at[row],
            right_send.at[k],
            right_recv.at[half - k],
            device_id=(peer_row(k), col),
            device_id_type=MESH,
        )

    def share_copy(k):
        src = peer_row(k)
        return pltpu.make_async_remote_copy(
            right_ref.at[src],
            right_ref.at[src],
            share_send.at[k],
            share_recv.at[k],
            device_id=(partner, col),
            device_id_type=MESH,
        )

    def norm_copy(k):
        return pltpu.make_async_remote_copy(
            norm_all.at[row],
            norm_all.at[row],
            norm_send.at[k],
            norm_recv.at[half - k],
            device_id=(peer_row(k), col),
            device_id_type=MESH,
        )

    def relay_copy(k):
        return pltpu.make_async_remote_copy(
            norm_all.at[peer_row(k)],
            norm_all.at[peer_row(k)],
            relay_send.at[k],
            relay_recv.at[k],
            device_id=(partner, col),
            device_id_type=MESH,
        )

    loads[5].wait()
    for b in range(factor):
        high, low = split(outer_ref[pl.ds(b, factor, stride=factor), :])
        lanes = slice(b * pair_width, (b + 1) * pair_width)
        w_buf[0:factor, lanes] = high
        w_buf[factor : 2 * factor, lanes] = low
        w_buf[2 * factor : 3 * factor, lanes] = high

    def left_rows(c, at):
        packed = left_ref[c, 0:quarter, :]
        high = packed.astype(BF16).astype(F32)
        low = packed - high
        for g in range(4):
            lanes = slice(g * factor, (g + 1) * factor)
            pieces = [high[:, lanes], high[:, lanes], low[:, lanes]]
            l_buf[at, g * quarter : (g + 1) * quarter, :] = jnp.concatenate(
                pieces, axis=1
            ).astype(BF16)

    def mix(l_rows, c, count):
        for nb in range(factor // 2):
            mixed = dot(l_rows, w_buf[:, nb * 2 * pair_width : (nb + 1) * 2 * pair_width])
            tiles = jnp.concatenate(
                [
                    mixed[:, :pair_width].reshape(count, seqs, pair_width),
                    mixed[:, pair_width:].reshape(count, seqs, pair_width),
                ],
                axis=1,
            )
            high, low = split(tiles)
            high_buf[:, c, nb] = high
            low_buf[:, c, nb] = low

    def prepare():
        for at in range(6, 11):
            loads[at].wait()

        def keep_value(h, block):
            value_bd[h] = block

        def keep_gate(h, block):
            gate_bd[h] = block

        spread_heads(gate_w_ref[...], heads, group, keep_gate)
        spread_heads(value_w_ref[...], heads, group, keep_value)
        for g in range(seqs // group):
            own = norm_all[row, :, g * group * width : (g + 1) * group * width]
            for h in range(heads):
                gate_out[g, h] = jax.nn.sigmoid(stacked_dot(own, gate_bd[h]))
        channels = output_w_ref.shape[1]
        head_width = channels // heads
        lanes = iota((width, group * width), 1)
        pick = jnp.where(iota((width, group * width), 0) == lanes % width, 1.0, 0.0).astype(BF16)
        own = (iota((2 * group * head_width, group * width), 0) // head_width) % group == iota(
            (2 * group * head_width, group * width), 1
        ) // width
        for t, half_w in enumerate(split(output_w_ref[...])):
            tiled = t_dot(half_w, pick)
            for hp in range(heads // 2):
                pieces = []
                for hh in range(2):
                    first = (2 * hp + hh) * head_width
                    pieces += [tiled[first : first + head_width]] * group
                output_bd[t, hp] = jnp.where(own, jnp.concatenate(pieces, axis=0), 0.0).astype(BF16)
        lanes = iota((heads, 2 * LANES), 1)
        low_half = iota((pair_width, 2 * LANES), 1) >= LANES
        w_high, w_low = split(logits_w_ref[...])
        for i in range(here):
            pick = jnp.where(
                ((lanes // here) % heads == iota((heads, 2 * LANES), 0)) & (lanes % here == i),
                1.0,
                0.0,
            ).astype(BF16)
            block = jnp.where(low_half, t_dot(w_low, pick), t_dot(w_high, pick))
            wl_buf[i // 2, (i % 2) * pair_width : (i % 2 + 1) * pair_width, :] = block.astype(BF16)

    low_end = col < (n_col + 1) // 2
    spot_in = jnp.where(low_end, col, n_col - 1 - col)

    def stage(k, carry):
        order = jnp.where(k - 1 < spot_in, k - 1, k)
        src = jnp.where(low_end, order, n_col - 1 - order)
        src = jnp.where(k == 0, col, src)

        @pl.when(k == 1)
        def _():
            prepare()
            pltpu.make_async_copy(right_buf, right_ref.at[row], turn_sem.at[1]).wait()
            for k2 in range(1, half):
                right_copy(k2).start()
            share_copy(0).start()
            if relayed:

                @pl.when(relay)
                def _():
                    left_wait(far_src)
                    left_forward().start()

        @pl.when(k == n_col - 1)
        def _():
            for k2 in range(1, half):
                pltpu.make_async_copy(
                    right_buf, right_ref.at[peer_row(k2)], right_recv.at[k2]
                ).wait()
                share_copy(k2).start()
            relay_copy(0).start()
            for k2 in range(1, half):
                norm_copy(k2).start()

        @pl.when(k > 0)
        def _():
            unless_relayed(src, lambda: left_wait(src))

        at = 0 if premixed else src
        left_rows(src, at)
        if premixed:
            mix(l_buf[0], src, rows)
        return carry

    lax.fori_loop(0, n_col, stage, 0)
    for k in range(half):
        src = 2 * lax.rem(chip + k, half) + 1 - core
        pltpu.make_async_copy(right_buf, right_ref.at[src], share_recv.at[k]).wait()
    count = left_ref[0, quarter : quarter + 1, 0:1]
    for c in range(1, n_col):
        count = count + left_ref[c, quarter : quarter + 1, 0:1]
    scale = 1.0 / jnp.maximum(count, 1.0)
    for c in range(n_col):
        for t in range(ratio):
            high_r, low_r = split(right_ref[c * ratio + t, 0:rows, :])
            lanes = slice(c * k_col, (c + 1) * k_col)
            r_buf[t * rows : (t + 1) * rows, lanes] = high_r
            r_buf[cols + t * rows : cols + (t + 1) * rows, lanes] = low_r
    res_cols = jnp.concatenate(
        [column(right_ref[t, rows : rows + 1, 0:rows]) for t in range(ratio)], axis=0
    )
    part_of = iota((jrows, LANES), 1) // (here * heads)
    mask = jnp.zeros((jrows, LANES), F32)
    for p in range(parts):
        dead = (res_cols[p * jrows : (p + 1) * jrows] - 1.0) * 1000000000.0
        mask = jnp.where(part_of == p, dead, mask)
    mask_buf[...] = mask

    def chunk(at):
        return pl.ds(pl.multiple_of(at * jrows, jrows), jrows)

    def logits_copy(k, at):
        return pltpu.make_async_remote_copy(
            slots.at[col, chunk(at)],
            slots.at[col, chunk(at)],
            logits_send.at[k, at],
            logits_recv.at[col, at],
            device_id=(row, lax.rem(col + k, n_col)),
            device_id_type=MESH,
        )

    def logits_forward(at):
        return pltpu.make_async_remote_copy(
            slots.at[far_src, chunk(at)],
            slots.at[far_src, chunk(at)],
            logits_send.at[0, at],
            logits_recv.at[far_src, at],
            device_id=(row, far_dest),
            device_id_type=MESH,
        )

    def logits_wait(src, at):
        pltpu.make_async_copy(
            slots.at[src, chunk(at)], slots.at[src, chunk(at)], logits_recv.at[src, at]
        ).wait()

    def pass_on(at):
        @pl.when(relay)
        def _():
            logits_wait(far_src, at)
            logits_forward(at).start()

    lag = 2

    def body(step, carry):
        first_row = pl.multiple_of(step * here, here)
        if not premixed:
            size = here * seqs
            for c in range(n_col):
                mix(l_buf[c, pl.ds(pl.multiple_of(step * size, size), size), :], c, here)
        r_both = r_buf[...]
        for p in range(here // 2):
            at = [2 * p + t + (first_row if premixed else 0) for t in range(2)]
            right_high = jnp.concatenate(
                [high_buf[i].reshape(depth, pair_width) for i in at], axis=1
            )
            right_low = jnp.concatenate([low_buf[i].reshape(depth, pair_width) for i in at], axis=1)
            first = dot(r_both, right_high)
            sums = first[:cols] + (first[cols:] + dot(r_both[:cols], right_low))
            for t in range(2):
                i = first_row + 2 * p + t
                pair_out[i] = pair_ref[i] + sums[:, t * pair_width : (t + 1) * pair_width] * scale
        total = None
        batch = here // 2
        for g in range(0, here, batch):
            pairs = pair_out[pl.ds(first_row + g, batch)].reshape(batch * cols, pair_width)
            high, low = split(layer_norm(pairs))
            for p in range(batch // 2):
                both = jnp.concatenate(
                    [
                        jnp.concatenate(
                            [
                                half_x[(2 * p + t) * cols : (2 * p + t + 1) * cols]
                                for t in range(2)
                            ],
                            axis=1,
                        )
                        for half_x in (high, low)
                    ],
                    axis=0,
                )
                out = dot(both, wl_buf[g // 2 + p])
                out = out[:, :LANES] + out[:, LANES:]
                out = out[:cols] + out[cols:]
                total = out if total is None else total + out
        logits = total[:jrows]
        for p in range(1, parts):
            logits = jnp.where(part_of == p, total[p * jrows : (p + 1) * jrows], logits)
        slots[col, chunk(step), :] = logits + mask_buf[...]
        for k in range(1, n_col):
            near(lax.rem(col + k, n_col), logits_copy(k, step).start)
        if relayed:

            @pl.when(step >= lag)
            def _():
                pass_on(step - lag)

        @pl.when(step == steps // 2)
        def _():
            for k in range(1, half):
                pltpu.make_async_copy(
                    norm_all.at[row], norm_all.at[peer_row(k)], norm_recv.at[k]
                ).wait()
                relay_copy(k).start()

        return carry

    lax.fori_loop(0, steps, body, 0)
    if relayed:
        for at in range(steps - lag, steps):
            pass_on(at)
    for k in range(half):
        other = 2 * lax.rem(chip + k, half) + 1 - core
        pltpu.make_async_copy(norm_all.at[row], norm_all.at[other], relay_recv.at[k]).wait()
        relay_copy(k).wait_send()
        share_copy(k).wait_send()
    for k in range(1, half):
        norm_copy(k).wait_send()
        right_copy(k).wait_send()
    for k in range(1, n_col):
        near(lax.rem(col + k, n_col), left_copy(k).wait_send)

    @pl.when(away)
    def _():
        turn.wait_send()

    if relayed:

        @pl.when(relay)
        def _():
            left_forward().wait_send()

    def drain(at, carry):
        for k in range(1, n_col):
            other = lax.rem(col + k, n_col)
            near(other, logits_copy(k, at).wait_send)
            unless_relayed(other, lambda: logits_wait(other, at))
        if relayed:

            @pl.when(relay)
            def _():
                logits_forward(at).wait_send()

        return carry

    lax.fori_loop(0, steps, drain, 0)


def average_kernel(
    here,
    slots,
    norm_ref,
    gate_ref,
    value_bd,
    output_bd,
    align_ref,
    pair_ref,
    out_any,
    pair_any,
    out_buf,
    sems,
):
    place = pltpu.make_async_copy(pair_ref, pair_any, sems.at[0])
    place.start()
    seqs, rows, width = align_ref.shape
    n_col, total_rows, _ = slots.shape
    groups, heads = gate_ref.shape[0], gate_ref.shape[1]
    group = seqs // groups
    steps = rows // here
    jrows = total_rows // steps
    wide = here * heads
    parts = LANES // wide
    norm_high, norm_low = split(norm_ref[...])
    part_of = iota((jrows, LANES), 1) // wide

    def over_parts(values, combine):
        out = values
        for p in range(1, parts):
            out = combine(out, pltpu.roll(values, p * wide, 1))
        return out

    weights = []
    for t in range(steps):
        pieces = [slots[c, t * jrows : (t + 1) * jrows, :] for c in range(n_col)]
        top = pieces[0]
        for piece in pieces[1:]:
            top = jnp.maximum(top, piece)
        top = over_parts(jnp.max(top, axis=0, keepdims=True), jnp.maximum)
        pieces = [jnp.exp(piece - top) for piece in pieces]
        total = pieces[0]
        for piece in pieces[1:]:
            total = total + piece
        inverse = 1.0 / over_parts(jnp.sum(total, axis=0, keepdims=True), jnp.add)
        weights.append([piece * inverse for piece in pieces])
    turned = []
    for t in range(0, steps, parts):
        blocks = []
        for c in range(n_col):
            for p in range(parts):
                block = None
                for q in range(parts):
                    value = weights[t + q][c]
                    shift = (q - p) % parts * wide
                    if shift:
                        value = pltpu.roll(value, shift, 1)
                    block = value if block is None else jnp.where(part_of == q, value, block)
                blocks.append(block)
        turned.append(jnp.concatenate(blocks, axis=0).T)
    mixed = dot_split(jnp.concatenate(turned, axis=0), norm_high, norm_low)
    for g in range(groups):
        gated = []
        for h in range(heads):
            own = jnp.concatenate(
                [
                    mixed[
                        t * wide + h * here : t * wide + (h + 1) * here,
                        g * group * width : (g + 1) * group * width,
                    ]
                    for t in range(steps)
                ],
                axis=0,
            )
            gated.append(stacked_dot(own, value_bd[h]) * gate_ref[g, h])
        out = None
        for hp in range(heads // 2):
            part = dot_split(
                jnp.concatenate(gated[2 * hp : 2 * hp + 2], axis=1),
                output_bd[0, hp],
                output_bd[1, hp],
            )
            out = part if out is None else out + part
        for s in range(group):
            at = g * group + s
            out_buf[at] = align_ref[at] + out[:, s * width : (s + 1) * width]
        pltpu.make_async_copy(
            out_buf.at[pl.ds(g * group, group)],
            out_any.at[pl.ds(g * group, group)],
            sems.at[1 + g],
        ).start()
    for g in range(groups):
        pltpu.make_async_copy(
            out_buf.at[pl.ds(g * group, group)],
            out_any.at[pl.ds(g * group, group)],
            sems.at[1 + g],
        ).wait()
    place.wait()


def per_device(
    n_row,
    n_col,
    alignment,
    pair_rep,
    seq_mask,
    res_mask,
    left_weight,
    right_weight,
    w_outer,
    w_logits,
    value_weight,
    gate_weight,
    output_weight,
):
    seqs, rows, width = alignment.shape
    cols, pair_width = pair_rep.shape[1], pair_rep.shape[2]
    factor = left_weight.shape[1]
    heads = w_logits.shape[1]
    channels = value_weight.shape[1]
    k_col = factor * seqs
    quarter = rows * seqs // 4
    half = n_row // 2
    here = 8
    steps = rows // here
    jrows = cols * here * heads // LANES
    group = LANES * heads // channels
    groups = seqs // group
    vmem = pl.BlockSpec(memory_space=pltpu.VMEM)
    anywhere = pl.BlockSpec(memory_space=pl.ANY)
    dma = pltpu.SemaphoreType.DMA
    left_shape = (quarter + 8, 4 * factor)
    right_shape = (rows + 8, k_col)
    mix_row = (n_col, factor // 2, 2 * seqs, pair_width)
    row_bytes = 4 * n_col * k_col * pair_width
    premixed = rows * row_bytes <= MIX_BYTES
    held = rows if premixed else here
    pair_new, slots, norm_all, gate, value_bd, output_bd, align = pl.pallas_call(
        functools.partial(pair_kernel, n_row, n_col, here),
        out_shape=(
            pltpu.VMEM(pair_rep.shape, F32),
            pltpu.VMEM((n_col, steps * jrows, LANES), F32),
            pltpu.VMEM((n_row, rows, seqs * width), F32),
            pltpu.VMEM((groups, heads, rows, LANES), F32),
            pltpu.VMEM((heads, group * width, 2 * LANES), BF16),
            pltpu.VMEM((2, heads // 2, 2 * LANES, group * width), BF16),
            pltpu.VMEM(alignment.shape, F32),
        ),
        in_specs=[anywhere] * 11,
        out_specs=(vmem,) * 7,
        scratch_shapes=[
            pltpu.SMEM((seqs,), jnp.int32),
            pltpu.VMEM((1, rows), jnp.int32),
            pltpu.VMEM((factor, width), F32),
            pltpu.VMEM((factor, width), F32),
            pltpu.VMEM(w_outer.shape, F32),
            pltpu.VMEM((heads, pair_width), F32),
            pltpu.VMEM(value_weight.shape, F32),
            pltpu.VMEM(gate_weight.shape, F32),
            pltpu.VMEM((width, channels), F32),
            pltpu.VMEM((rows * seqs, width), F32),
            pltpu.VMEM((rows, seqs * width), F32),
            pltpu.VMEM((k_col, seqs * width), F32),
            pltpu.VMEM(right_shape, F32),
            pltpu.VMEM((n_col,) + left_shape, F32),
            pltpu.VMEM((n_row,) + right_shape, F32),
            pltpu.VMEM((heads, group * width, 2 * LANES), BF16),
            pltpu.VMEM((here // 2, 2 * pair_width, 2 * LANES), BF16),
            pltpu.VMEM((3 * factor, factor * pair_width), BF16),
            pltpu.VMEM((1 if premixed else n_col, rows * seqs, 3 * factor), BF16),
            pltpu.VMEM((2 * cols, n_col * k_col), BF16),
            pltpu.VMEM((jrows, LANES), F32),
            pltpu.VMEM((held,) + mix_row, BF16),
            pltpu.VMEM((held,) + mix_row, BF16),
            pltpu.VMEM(pair_rep.shape, F32),
            dma((11,)),
            dma((n_col,)),
            dma((n_col,)),
            dma((2,)),
            dma((half,)),
            dma((half,)),
            dma((half,)),
            dma((half,)),
            dma((n_col, steps)),
            dma((n_col, steps)),
            dma((half,)),
            dma((half,)),
            dma((half,)),
            dma((half,)),
        ],
        compiler_params=pltpu.CompilerParams(
            collective_id=0, has_side_effects=True, vmem_limit_bytes=PAIR_VMEM
        ),
        name="pair",
    )(
        seq_mask,
        res_mask.reshape(1, rows),
        alignment,
        left_weight.T,
        right_weight.T,
        w_outer,
        w_logits.T,
        value_weight,
        gate_weight,
        output_weight.T,
        pair_rep,
    )
    alignment_out, pair_final = pl.pallas_call(
        functools.partial(average_kernel, here),
        out_shape=(
            jax.ShapeDtypeStruct(alignment.shape, F32),
            jax.ShapeDtypeStruct(pair_rep.shape, F32),
        ),
        in_specs=[vmem] * 7,
        out_specs=(anywhere, anywhere),
        scratch_shapes=[pltpu.VMEM(alignment.shape, F32), dma((1 + groups,))],
        compiler_params=pltpu.CompilerParams(vmem_limit_bytes=AVERAGE_VMEM),
        name="average",
    )(
        slots,
        norm_all.reshape(n_row * rows, seqs * width),
        gate,
        value_bd,
        output_bd,
        align,
        pair_new,
    )
    return (alignment_out, pair_final)


def solution(mesh):
    in_specs = (P("col", "row", None), P("row", "col", None), P("col"), P("row")) + (P(),) * 7
    out_specs = (P("col", "row", None), P("row", "col", None))
    return jax.shard_map(
        functools.partial(per_device, mesh.shape["row"], mesh.shape["col"]),
        mesh=mesh,
        in_specs=in_specs,
        out_specs=out_specs,
        check_vma=False,
    )
```

```python
import functools

import jax
import jax.numpy as jnp
from jax import lax
from jax.experimental import pallas as pl
from jax.experimental.pallas import tpu as pltpu
from jax.sharding import PartitionSpec as P

MESH = pl.DeviceIdType.MESH
F32 = jnp.float32
BF16 = jnp.bfloat16
epsilon = 1e-05
PAIR_VMEM = 48 * 1024 * 1024
AVERAGE_VMEM = 24 * 1024 * 1024
MIX_BYTES = 30 * 1024 * 1024
LANES = 128


def layer_norm(values):
    center = jnp.mean(values, axis=-1, keepdims=True)
    centred = values - center
    return centred * lax.rsqrt(jnp.mean(centred * centred, axis=-1, keepdims=True) + epsilon)


def split(values):
    high = values.astype(BF16)
    return high, (values - high.astype(F32)).astype(BF16)


def dot(left, right):
    return jnp.dot(left, right, preferred_element_type=F32)


def dot_t(left, right):
    return lax.dot_general(left, right, (((1,), (1,)), ((), ())), preferred_element_type=F32)


def t_dot(left, right):
    return lax.dot_general(left, right, (((0,), (0,)), ((), ())), preferred_element_type=F32)


def dot_split(left, right_high, right_low, multiply=dot):
    high, low = split(left)
    return multiply(high, right_high) + (multiply(low, right_high) + multiply(high, right_low))


def iota(shape, axis):
    return lax.broadcasted_iota(jnp.int32, shape, axis)


def stacked_dot(values, weights):
    count, half = values.shape[0], weights.shape[1] // 2
    high, low = split(values)
    out = dot(jnp.concatenate([high, low], axis=0), weights)
    out = out[:, :half] + out[:, half:]
    return out[:count] + out[count:]


def spread_heads(weight, heads, group, store):
    width, channels = weight.shape
    head_width = channels // heads
    both = jnp.concatenate(split(weight), axis=0)
    rows, lanes = iota((channels, LANES), 0), iota((channels, LANES), 1)
    own = iota((group * width, LANES), 0) // width == iota((group * width, LANES), 1) // head_width
    for h in range(heads):
        pick = jnp.where(rows == h * head_width + lanes % head_width, 1.0, 0.0).astype(BF16)
        tiled = dot(both, pick)
        parts = []
        for t in range(2):
            piece = jnp.concatenate([tiled[t * width : (t + 1) * width]] * group, axis=0)
            parts.append(jnp.where(own, piece, 0.0))
        store(h, jnp.concatenate(parts, axis=1).astype(BF16))


def pair_kernel(
    n_row,
    n_col,
    here,
    seq_in,
    res_in,
    align_in,
    left_w_in,
    right_w_in,
    outer_in,
    logits_w_in,
    value_w_in,
    gate_w_in,
    output_w_in,
    pair_in,
    pair_out,
    slots,
    norm_all,
    gate_out,
    value_bd,
    output_bd,
    align_ref,
    seq_ref,
    res_ref,
    left_w_ref,
    right_w_ref,
    outer_ref,
    logits_w_ref,
    value_w_ref,
    gate_w_ref,
    output_w_ref,
    rows_buf,
    masked_buf,
    block_buf,
    right_buf,
    left_ref,
    right_ref,
    gate_bd,
    wl_buf,
    w_buf,
    l_buf,
    r_buf,
    mask_buf,
    high_buf,
    low_buf,
    pair_ref,
    load_sem,
    left_send,
    left_recv,
    turn_sem,
    right_send,
    right_recv,
    share_send,
    share_recv,
    logits_send,
    logits_recv,
    norm_send,
    norm_recv,
    relay_send,
    relay_recv,
):
    row, col = lax.axis_index("row"), lax.axis_index("col")
    barrier = pltpu.get_barrier_semaphore()
    loads = [
        pltpu.make_async_copy(source, target, load_sem.at[at])
        for at, (source, target) in enumerate(
            [
                (align_in, align_ref),
                (seq_in, seq_ref),
                (res_in, res_ref),
                (right_w_in, right_w_ref),
                (left_w_in, left_w_ref),
                (outer_in, outer_ref),
                (gate_w_in, gate_w_ref),
                (value_w_in, value_w_ref),
                (logits_w_in, logits_w_ref),
                (output_w_in, output_w_ref),
                (pair_in, pair_ref),
            ]
        )
    ]
    for load in loads:
        load.start()

    seqs, rows, width = align_ref.shape
    factor = right_w_ref.shape[0]
    ratio, k_col = n_row // n_col, factor * seqs
    half = n_row // 2
    chip, core = row // 2, lax.rem(row, 2)
    partner = 2 * chip + 1 - core
    cols, pair_width = pair_out.shape[1], pair_out.shape[2]
    heads = logits_w_ref.shape[0]
    quarter = rows * seqs // 4
    steps = rows // here
    parts = LANES // (here * heads)
    jrows = cols // parts
    group = LANES * heads // value_w_ref.shape[1]
    premixed = high_buf.shape[0] == rows
    depth = n_col * k_col

    def peer_row(k):
        return 2 * lax.rem(chip + k, half) + core

    relayed = n_col >= 4
    at_high, at_low = col == n_col - 2, col == 1
    relay = at_high | at_low
    far_src = jnp.where(at_low, n_col - 1, 0)
    far_dest = jnp.where(at_low, 0, n_col - 1)

    def is_far(other):
        return (other - col == n_col - 1) | (col - other == n_col - 1)

    def near(other, action):
        if relayed:
            pl.when(jnp.logical_not(is_far(other)))(action)
        else:
            action()

    def unless_relayed(src, action):
        if relayed:
            pl.when(jnp.logical_not(relay & (src == far_src)))(action)
        else:
            action()

    dest = row // ratio
    spot = col * ratio + lax.rem(row, ratio)
    away = dest != col

    def meet(action):
        for k in range(1, n_col):
            other = lax.rem(col + k, n_col)
            near(other, functools.partial(action, row, other))
        for k in range(1, half):
            action(peer_row(k), col)
        action(partner, col)
        pl.when(away)(functools.partial(action, spot, dest))

    def greet(other_row, other_col):
        pl.semaphore_signal(
            barrier, inc=1, device_id=(other_row, other_col), device_id_type=MESH
        )

    greeters = half + n_col - 1 + jnp.where(away, 1, 0)
    if relayed:
        greeters = greeters - jnp.where((col == 0) | (col == n_col - 1), 1, 0)
    meet(greet)
    for at in range(5):
        loads[at].wait()
    res_row = res_ref[...].astype(F32)
    diag = iota((rows, rows), 0) == iota((rows, rows), 1)

    def column(values):
        return jnp.sum(
            jnp.where(diag, jnp.broadcast_to(values, (rows, rows)), 0.0), axis=1, keepdims=True
        )

    res_col = column(res_row)
    spread = jnp.broadcast_to(right_w_ref[...][:, None, :], (factor, seqs, width))
    row_seq = iota((factor, seqs, width), 1)
    seq_sum = 0.0
    for s in range(seqs):
        normed = layer_norm(align_ref[s])
        norm_all[row, :, s * width : (s + 1) * width] = normed
        live = seq_ref[s].astype(F32)
        seq_sum = seq_sum + live
        masked = normed * (res_col * live)
        masked_buf[:, s * width : (s + 1) * width] = masked
        rows_buf[pl.ds(s, rows, stride=seqs), :] = masked
        block_buf[:, s * width : (s + 1) * width] = jnp.where(row_seq == s, spread, 0.0).reshape(
            factor * seqs, width
        )
    wr_high, wr_low = split(block_buf[...])
    right_buf[0:rows, :] = dot_split(masked_buf[...], wr_high, wr_low, dot_t)
    right_buf[rows : rows + 8, 0:rows] = jnp.broadcast_to(res_row, (8, rows))
    right_buf[rows : rows + 8, rows:] = jnp.zeros((8, right_buf.shape[1] - rows), F32)
    pl.semaphore_wait(barrier, greeters)
    turn = pltpu.make_async_remote_copy(
        right_buf,
        right_ref.at[spot],
        turn_sem.at[0],
        turn_sem.at[1],
        device_id=(spot, dest),
        device_id_type=MESH,
    )
    stay = pltpu.make_async_copy(right_buf, right_ref.at[spot], turn_sem.at[1])

    @pl.when(away)
    def _():
        turn.start()

    @pl.when(jnp.logical_not(away))
    def _():
        stay.start()

    wl_high, wl_low = split(left_w_ref[...])
    left = dot_split(rows_buf[...], wl_high, wl_low, dot_t)
    for g in range(4):
        left_ref[col, 0:quarter, g * factor : (g + 1) * factor] = left[
            g * quarter : (g + 1) * quarter
        ]
    left_ref[col, quarter : quarter + 8, :] = jnp.full((8, left_ref.shape[2]), seq_sum, F32)

    def left_copy(k):
        return pltpu.make_async_remote_copy(
            left_ref.at[col],
            left_ref.at[col],
            left_send.at[k],
            left_recv.at[col],
            device_id=(row, lax.rem(col + k, n_col)),
            device_id_type=MESH,
        )

    def left_forward():
        return pltpu.make_async_remote_copy(
            left_ref.at[far_src],
            left_ref.at[far_src],
            left_send.at[0],
            left_recv.at[far_src],
            device_id=(row, far_dest),
            device_id_type=MESH,
        )

    def left_wait(src):
        pltpu.make_async_copy(left_ref.at[src], left_ref.at[src], left_recv.at[src]).wait()

    def right_copy(k):
        return pltpu.make_async_remote_copy(
            right_ref.at[row],
            right_ref.at[row],
            right_send.at[k],
            right_recv.at[half - k],
            device_id=(peer_row(k), col),
            device_id_type=MESH,
        )

    def share_copy(k):
        src = peer_row(k)
        return pltpu.make_async_remote_copy(
            right_ref.at[src],
            right_ref.at[src],
            share_send.at[k],
            share_recv.at[k],
            device_id=(partner, col),
            device_id_type=MESH,
        )

    def norm_copy(k):
        return pltpu.make_async_remote_copy(
            norm_all.at[row],
            norm_all.at[row],
            norm_send.at[k],
            norm_recv.at[half - k],
            device_id=(peer_row(k), col),
            device_id_type=MESH,
        )

    def relay_copy(k):
        return pltpu.make_async_remote_copy(
            norm_all.at[peer_row(k)],
            norm_all.at[peer_row(k)],
            relay_send.at[k],
            relay_recv.at[k],
            device_id=(partner, col),
            device_id_type=MESH,
        )

    loads[5].wait()
    for b in range(factor):
        high, low = split(outer_ref[pl.ds(b, factor, stride=factor), :])
        lanes = slice(b * pair_width, (b + 1) * pair_width)
        w_buf[0:factor, lanes] = high
        w_buf[factor : 2 * factor, lanes] = low
        w_buf[2 * factor : 3 * factor, lanes] = high

    def left_rows(c, at):
        packed = left_ref[c, 0:quarter, :]
        high = packed.astype(BF16).astype(F32)
        low = packed - high
        for g in range(4):
            lanes = slice(g * factor, (g + 1) * factor)
            pieces = [high[:, lanes], high[:, lanes], low[:, lanes]]
            l_buf[at, g * quarter : (g + 1) * quarter, :] = jnp.concatenate(
                pieces, axis=1
            ).astype(BF16)

    def mix(l_rows, c, count):
        for nb in range(factor // 2):
            mixed = dot(l_rows, w_buf[:, nb * 2 * pair_width : (nb + 1) * 2 * pair_width])
            tiles = jnp.concatenate(
                [
                    mixed[:, :pair_width].reshape(count, seqs, pair_width),
                    mixed[:, pair_width:].reshape(count, seqs, pair_width),
                ],
                axis=1,
            )
            high, low = split(tiles)
            high_buf[:, c, nb] = high
            low_buf[:, c, nb] = low

    def prepare():
        for at in range(6, 11):
            loads[at].wait()

        def keep_value(h, block):
            value_bd[h] = block

        def keep_gate(h, block):
            gate_bd[h] = block

        spread_heads(gate_w_ref[...], heads, group, keep_gate)
        spread_heads(value_w_ref[...], heads, group, keep_value)
        for g in range(seqs // group):
            own = norm_all[row, :, g * group * width : (g + 1) * group * width]
            for h in range(heads):
                gate_out[g, h] = jax.nn.sigmoid(stacked_dot(own, gate_bd[h]))
        channels = output_w_ref.shape[1]
        head_width = channels // heads
        lanes = iota((width, group * width), 1)
        pick = jnp.where(iota((width, group * width), 0) == lanes % width, 1.0, 0.0).astype(BF16)
        own = (iota((2 * group * head_width, group * width), 0) // head_width) % group == iota(
            (2 * group * head_width, group * width), 1
        ) // width
        for t, half_w in enumerate(split(output_w_ref[...])):
            tiled = t_dot(half_w, pick)
            for hp in range(heads // 2):
                pieces = []
                for hh in range(2):
                    first = (2 * hp + hh) * head_width
                    pieces += [tiled[first : first + head_width]] * group
                output_bd[t, hp] = jnp.where(own, jnp.concatenate(pieces, axis=0), 0.0).astype(BF16)
        lanes = iota((heads, 2 * LANES), 1)
        low_half = iota((pair_width, 2 * LANES), 1) >= LANES
        w_high, w_low = split(logits_w_ref[...])
        for i in range(here):
            pick = jnp.where(
                ((lanes // here) % heads == iota((heads, 2 * LANES), 0)) & (lanes % here == i),
                1.0,
                0.0,
            ).astype(BF16)
            block = jnp.where(low_half, t_dot(w_low, pick), t_dot(w_high, pick))
            wl_buf[i // 2, (i % 2) * pair_width : (i % 2 + 1) * pair_width, :] = block.astype(BF16)

    low_end = col < (n_col + 1) // 2
    spot_in = jnp.where(low_end, col, n_col - 1 - col)

    def stage(k, carry):
        order = jnp.where(k - 1 < spot_in, k - 1, k)
        src = jnp.where(low_end, order, n_col - 1 - order)
        src = jnp.where(k == 0, col, src)

        @pl.when(k == 1)
        def _():
            for k2 in range(1, n_col):
                near(lax.rem(col + k2, n_col), left_copy(k2).start)
            prepare()
            pltpu.make_async_copy(right_buf, right_ref.at[row], turn_sem.at[1]).wait()
            for k2 in range(1, half):
                right_copy(k2).start()
            share_copy(0).start()
            if relayed:

                @pl.when(relay)
                def _():
                    left_wait(far_src)
                    left_forward().start()

        @pl.when(k == n_col - 1)
        def _():
            for k2 in range(1, half):
                pltpu.make_async_copy(
                    right_buf, right_ref.at[peer_row(k2)], right_recv.at[k2]
                ).wait()
                share_copy(k2).start()
            relay_copy(0).start()
            for k2 in range(1, half):
                norm_copy(k2).start()

        @pl.when(k > 0)
        def _():
            unless_relayed(src, lambda: left_wait(src))

        at = 0 if premixed else src
        left_rows(src, at)
        if premixed:
            mix(l_buf[0], src, rows)
        return carry

    lax.fori_loop(0, n_col, stage, 0)
    for k in range(half):
        src = 2 * lax.rem(chip + k, half) + 1 - core
        pltpu.make_async_copy(right_buf, right_ref.at[src], share_recv.at[k]).wait()
    count = left_ref[0, quarter : quarter + 1, 0:1]
    for c in range(1, n_col):
        count = count + left_ref[c, quarter : quarter + 1, 0:1]
    scale = 1.0 / jnp.maximum(count, 1.0)
    for c in range(n_col):
        for t in range(ratio):
            high_r, low_r = split(right_ref[c * ratio + t, 0:rows, :])
            lanes = slice(c * k_col, (c + 1) * k_col)
            r_buf[t * rows : (t + 1) * rows, lanes] = high_r
            r_buf[cols + t * rows : cols + (t + 1) * rows, lanes] = low_r
    res_cols = jnp.concatenate(
        [column(right_ref[t, rows : rows + 1, 0:rows]) for t in range(ratio)], axis=0
    )
    part_of = iota((jrows, LANES), 1) // (here * heads)
    mask = jnp.zeros((jrows, LANES), F32)
    for p in range(parts):
        dead = (res_cols[p * jrows : (p + 1) * jrows] - 1.0) * 1000000000.0
        mask = jnp.where(part_of == p, dead, mask)
    mask_buf[...] = mask

    def chunk(at):
        return pl.ds(pl.multiple_of(at * jrows, jrows), jrows)

    def logits_copy(k, at):
        return pltpu.make_async_remote_copy(
            slots.at[col, chunk(at)],
            slots.at[col, chunk(at)],
            logits_send.at[k, at],
            logits_recv.at[col, at],
            device_id=(row, lax.rem(col + k, n_col)),
            device_id_type=MESH,
        )

    def logits_forward(at):
        return pltpu.make_async_remote_copy(
            slots.at[far_src, chunk(at)],
            slots.at[far_src, chunk(at)],
            logits_send.at[0, at],
            logits_recv.at[far_src, at],
            device_id=(row, far_dest),
            device_id_type=MESH,
        )

    def logits_wait(src, at):
        pltpu.make_async_copy(
            slots.at[src, chunk(at)], slots.at[src, chunk(at)], logits_recv.at[src, at]
        ).wait()

    def pass_on(at):
        @pl.when(relay)
        def _():
            logits_wait(far_src, at)
            logits_forward(at).start()

    lag, direct = 2, 1

    def body(step, carry):
        first_row = pl.multiple_of(step * here, here)
        if not premixed:
            size = here * seqs
            for c in range(n_col):
                mix(l_buf[c, pl.ds(pl.multiple_of(step * size, size), size), :], c, here)
        r_both = r_buf[...]
        for p in range(here // 2):
            at = [2 * p + t + (first_row if premixed else 0) for t in range(2)]
            right_high = jnp.concatenate(
                [high_buf[i].reshape(depth, pair_width) for i in at], axis=1
            )
            right_low = jnp.concatenate([low_buf[i].reshape(depth, pair_width) for i in at], axis=1)
            first = dot(r_both, right_high)
            sums = first[:cols] + (first[cols:] + dot(r_both[:cols], right_low))
            for t in range(2):
                i = first_row + 2 * p + t
                pair_out[i] = pair_ref[i] + sums[:, t * pair_width : (t + 1) * pair_width] * scale
        total = None
        batch = here // 2
        for g in range(0, here, batch):
            pairs = pair_out[pl.ds(first_row + g, batch)].reshape(batch * cols, pair_width)
            high, low = split(layer_norm(pairs))
            for p in range(batch // 2):
                both = jnp.concatenate(
                    [
                        jnp.concatenate(
                            [
                                half_x[(2 * p + t) * cols : (2 * p + t + 1) * cols]
                                for t in range(2)
                            ],
                            axis=1,
                        )
                        for half_x in (high, low)
                    ],
                    axis=0,
                )
                out = dot(both, wl_buf[g // 2 + p])
                out = out[:, :LANES] + out[:, LANES:]
                out = out[:cols] + out[cols:]
                total = out if total is None else total + out
        logits = total[:jrows]
        for p in range(1, parts):
            logits = jnp.where(part_of == p, total[p * jrows : (p + 1) * jrows], logits)
        slots[col, chunk(step), :] = logits + mask_buf[...]
        for k in range(1, n_col):
            other = lax.rem(col + k, n_col)
            if relayed:
                pl.when(jnp.logical_not(is_far(other)) | (step >= steps - direct))(
                    logits_copy(k, step).start
                )
            else:
                logits_copy(k, step).start()
        if relayed:

            @pl.when(step >= lag)
            def _():
                pass_on(step - lag)

        @pl.when(step == steps // 2)
        def _():
            for k in range(1, half):
                pltpu.make_async_copy(
                    norm_all.at[row], norm_all.at[peer_row(k)], norm_recv.at[k]
                ).wait()
                relay_copy(k).start()

        return carry

    lax.fori_loop(0, steps, body, 0)
    if relayed:
        for at in range(steps - lag, steps - direct):
            pass_on(at)
    for k in range(half):
        other = 2 * lax.rem(chip + k, half) + 1 - core
        pltpu.make_async_copy(norm_all.at[row], norm_all.at[other], relay_recv.at[k]).wait()
        relay_copy(k).wait_send()
        share_copy(k).wait_send()
    for k in range(1, half):
        norm_copy(k).wait_send()
        right_copy(k).wait_send()
    for k in range(1, n_col):
        near(lax.rem(col + k, n_col), left_copy(k).wait_send)

    @pl.when(away)
    def _():
        turn.wait_send()

    if relayed:

        @pl.when(relay)
        def _():
            left_forward().wait_send()

    def drain(at, carry):
        for k in range(1, n_col):
            other = lax.rem(col + k, n_col)
            near(other, logits_copy(k, at).wait_send)
            unless_relayed(other, lambda: logits_wait(other, at))
        if relayed:

            @pl.when(relay)
            def _():
                logits_forward(at).wait_send()

        return carry

    if relayed:
        lax.fori_loop(0, steps - direct, drain, 0)
    for at in range(steps - direct if relayed else 0, steps):
        for k in range(1, n_col):
            logits_copy(k, at).wait_send()
            logits_wait(lax.rem(col + k, n_col), at)


def average_kernel(
    here,
    slots,
    norm_ref,
    gate_ref,
    value_bd,
    output_bd,
    align_ref,
    pair_ref,
    out_any,
    pair_any,
    out_buf,
    sems,
):
    place = pltpu.make_async_copy(pair_ref, pair_any, sems.at[0])
    place.start()
    seqs, rows, width = align_ref.shape
    n_col, total_rows, _ = slots.shape
    groups, heads = gate_ref.shape[0], gate_ref.shape[1]
    group = seqs // groups
    steps = rows // here
    jrows = total_rows // steps
    wide = here * heads
    parts = LANES // wide
    norm_high, norm_low = split(norm_ref[...])
    part_of = iota((jrows, LANES), 1) // wide

    def over_parts(values, combine):
        out = values
        for p in range(1, parts):
            out = combine(out, pltpu.roll(values, p * wide, 1))
        return out

    weights = []
    for t in range(steps):
        pieces = [slots[c, t * jrows : (t + 1) * jrows, :] for c in range(n_col)]
        top = pieces[0]
        for piece in pieces[1:]:
            top = jnp.maximum(top, piece)
        top = over_parts(jnp.max(top, axis=0, keepdims=True), jnp.maximum)
        pieces = [jnp.exp(piece - top) for piece in pieces]
        total = pieces[0]
        for piece in pieces[1:]:
            total = total + piece
        inverse = 1.0 / over_parts(jnp.sum(total, axis=0, keepdims=True), jnp.add)
        weights.append([piece * inverse for piece in pieces])
    turned = []
    for t in range(0, steps, parts):
        blocks = []
        for c in range(n_col):
            for p in range(parts):
                block = None
                for q in range(parts):
                    value = weights[t + q][c]
                    shift = (q - p) % parts * wide
                    if shift:
                        value = pltpu.roll(value, shift, 1)
                    block = value if block is None else jnp.where(part_of == q, value, block)
                blocks.append(block)
        turned.append(jnp.concatenate(blocks, axis=0).T)
    mixed = dot_split(jnp.concatenate(turned, axis=0), norm_high, norm_low)
    for g in range(groups):
        gated = []
        for h in range(heads):
            own = jnp.concatenate(
                [
                    mixed[
                        t * wide + h * here : t * wide + (h + 1) * here,
                        g * group * width : (g + 1) * group * width,
                    ]
                    for t in range(steps)
                ],
                axis=0,
            )
            gated.append(stacked_dot(own, value_bd[h]) * gate_ref[g, h])
        out = None
        for hp in range(heads // 2):
            part = dot_split(
                jnp.concatenate(gated[2 * hp : 2 * hp + 2], axis=1),
                output_bd[0, hp],
                output_bd[1, hp],
            )
            out = part if out is None else out + part
        for s in range(group):
            at = g * group + s
            out_buf[at] = align_ref[at] + out[:, s * width : (s + 1) * width]
        pltpu.make_async_copy(
            out_buf.at[pl.ds(g * group, group)],
            out_any.at[pl.ds(g * group, group)],
            sems.at[1 + g],
        ).start()
    for g in range(groups):
        pltpu.make_async_copy(
            out_buf.at[pl.ds(g * group, group)],
            out_any.at[pl.ds(g * group, group)],
            sems.at[1 + g],
        ).wait()
    place.wait()


def per_device(
    n_row,
    n_col,
    alignment,
    pair_rep,
    seq_mask,
    res_mask,
    left_weight,
    right_weight,
    w_outer,
    w_logits,
    value_weight,
    gate_weight,
    output_weight,
):
    seqs, rows, width = alignment.shape
    cols, pair_width = pair_rep.shape[1], pair_rep.shape[2]
    factor = left_weight.shape[1]
    heads = w_logits.shape[1]
    channels = value_weight.shape[1]
    k_col = factor * seqs
    quarter = rows * seqs // 4
    half = n_row // 2
    here = 8
    steps = rows // here
    jrows = cols * here * heads // LANES
    group = LANES * heads // channels
    groups = seqs // group
    vmem = pl.BlockSpec(memory_space=pltpu.VMEM)
    anywhere = pl.BlockSpec(memory_space=pl.ANY)
    dma = pltpu.SemaphoreType.DMA
    left_shape = (quarter + 8, 4 * factor)
    right_shape = (rows + 8, k_col)
    mix_row = (n_col, factor // 2, 2 * seqs, pair_width)
    row_bytes = 4 * n_col * k_col * pair_width
    premixed = rows * row_bytes <= MIX_BYTES
    held = rows if premixed else here
    pair_new, slots, norm_all, gate, value_bd, output_bd, align = pl.pallas_call(
        functools.partial(pair_kernel, n_row, n_col, here),
        out_shape=(
            pltpu.VMEM(pair_rep.shape, F32),
            pltpu.VMEM((n_col, steps * jrows, LANES), F32),
            pltpu.VMEM((n_row, rows, seqs * width), F32),
            pltpu.VMEM((groups, heads, rows, LANES), F32),
            pltpu.VMEM((heads, group * width, 2 * LANES), BF16),
            pltpu.VMEM((2, heads // 2, 2 * LANES, group * width), BF16),
            pltpu.VMEM(alignment.shape, F32),
        ),
        in_specs=[anywhere] * 11,
        out_specs=(vmem,) * 7,
        scratch_shapes=[
            pltpu.SMEM((seqs,), jnp.int32),
            pltpu.VMEM((1, rows), jnp.int32),
            pltpu.VMEM((factor, width), F32),
            pltpu.VMEM((factor, width), F32),
            pltpu.VMEM(w_outer.shape, F32),
            pltpu.VMEM((heads, pair_width), F32),
            pltpu.VMEM(value_weight.shape, F32),
            pltpu.VMEM(gate_weight.shape, F32),
            pltpu.VMEM((width, channels), F32),
            pltpu.VMEM((rows * seqs, width), F32),
            pltpu.VMEM((rows, seqs * width), F32),
            pltpu.VMEM((k_col, seqs * width), F32),
            pltpu.VMEM(right_shape, F32),
            pltpu.VMEM((n_col,) + left_shape, F32),
            pltpu.VMEM((n_row,) + right_shape, F32),
            pltpu.VMEM((heads, group * width, 2 * LANES), BF16),
            pltpu.VMEM((here // 2, 2 * pair_width, 2 * LANES), BF16),
            pltpu.VMEM((3 * factor, factor * pair_width), BF16),
            pltpu.VMEM((1 if premixed else n_col, rows * seqs, 3 * factor), BF16),
            pltpu.VMEM((2 * cols, n_col * k_col), BF16),
            pltpu.VMEM((jrows, LANES), F32),
            pltpu.VMEM((held,) + mix_row, BF16),
            pltpu.VMEM((held,) + mix_row, BF16),
            pltpu.VMEM(pair_rep.shape, F32),
            dma((11,)),
            dma((n_col,)),
            dma((n_col,)),
            dma((2,)),
            dma((half,)),
            dma((half,)),
            dma((half,)),
            dma((half,)),
            dma((n_col, steps)),
            dma((n_col, steps)),
            dma((half,)),
            dma((half,)),
            dma((half,)),
            dma((half,)),
        ],
        compiler_params=pltpu.CompilerParams(
            collective_id=0, has_side_effects=True, vmem_limit_bytes=PAIR_VMEM
        ),
        name="pair",
    )(
        seq_mask,
        res_mask.reshape(1, rows),
        alignment,
        left_weight.T,
        right_weight.T,
        w_outer,
        w_logits.T,
        value_weight,
        gate_weight,
        output_weight.T,
        pair_rep,
    )
    alignment_out, pair_final = pl.pallas_call(
        functools.partial(average_kernel, here),
        out_shape=(
            jax.ShapeDtypeStruct(alignment.shape, F32),
            jax.ShapeDtypeStruct(pair_rep.shape, F32),
        ),
        in_specs=[vmem] * 7,
        out_specs=(anywhere, anywhere),
        scratch_shapes=[pltpu.VMEM(alignment.shape, F32), dma((1 + groups,))],
        compiler_params=pltpu.CompilerParams(vmem_limit_bytes=AVERAGE_VMEM),
        name="average",
    )(
        slots,
        norm_all.reshape(n_row * rows, seqs * width),
        gate,
        value_bd,
        output_bd,
        align,
        pair_new,
    )
    return (alignment_out, pair_final)


def solution(mesh):
    in_specs = (P("col", "row", None), P("row", "col", None), P("col"), P("row")) + (P(),) * 7
    out_specs = (P("col", "row", None), P("row", "col", None))
    return jax.shard_map(
        functools.partial(per_device, mesh.shape["row"], mesh.shape["col"]),
        mesh=mesh,
        in_specs=in_specs,
        out_specs=out_specs,
        check_vma=False,
    )
```

```python
import functools

import jax
import jax.numpy as jnp
from jax import lax
from jax.experimental import pallas as pl
from jax.experimental.pallas import tpu as pltpu
from jax.sharding import PartitionSpec as P

MESH = pl.DeviceIdType.MESH
F32 = jnp.float32
BF16 = jnp.bfloat16
epsilon = 1e-05
PAIR_VMEM = 48 * 1024 * 1024
AVERAGE_VMEM = 24 * 1024 * 1024
MIX_BYTES = 30 * 1024 * 1024
LANES = 128


def layer_norm(values):
    center = jnp.mean(values, axis=-1, keepdims=True)
    centred = values - center
    return centred * lax.rsqrt(jnp.mean(centred * centred, axis=-1, keepdims=True) + epsilon)


def split(values):
    high = values.astype(BF16)
    return high, (values - high.astype(F32)).astype(BF16)


def dot(left, right):
    return jnp.dot(left, right, preferred_element_type=F32)


def dot_t(left, right):
    return lax.dot_general(left, right, (((1,), (1,)), ((), ())), preferred_element_type=F32)


def t_dot(left, right):
    return lax.dot_general(left, right, (((0,), (0,)), ((), ())), preferred_element_type=F32)


def dot_split(left, right_high, right_low, multiply=dot):
    high, low = split(left)
    return multiply(high, right_high) + (multiply(low, right_high) + multiply(high, right_low))


def iota(shape, axis):
    return lax.broadcasted_iota(jnp.int32, shape, axis)


def stacked_dot(values, weights):
    count, half = values.shape[0], weights.shape[1] // 2
    high, low = split(values)
    out = dot(jnp.concatenate([high, low], axis=0), weights)
    out = out[:, :half] + out[:, half:]
    return out[:count] + out[count:]


def spread_heads(weight, heads, group, store):
    width, channels = weight.shape
    head_width = channels // heads
    both = jnp.concatenate(split(weight), axis=0)
    rows, lanes = iota((channels, LANES), 0), iota((channels, LANES), 1)
    own = iota((group * width, LANES), 0) // width == iota((group * width, LANES), 1) // head_width
    for h in range(heads):
        pick = jnp.where(rows == h * head_width + lanes % head_width, 1.0, 0.0).astype(BF16)
        tiled = dot(both, pick)
        parts = []
        for t in range(2):
            piece = jnp.concatenate([tiled[t * width : (t + 1) * width]] * group, axis=0)
            parts.append(jnp.where(own, piece, 0.0))
        store(h, jnp.concatenate(parts, axis=1).astype(BF16))


def pair_kernel(
    n_row,
    n_col,
    here,
    early,
    seq_in,
    res_in,
    align_in,
    left_w_in,
    right_w_in,
    outer_in,
    logits_w_in,
    value_w_in,
    gate_w_in,
    output_w_in,
    pair_in,
    pair_out,
    slots,
    norm_high,
    norm_low,
    gate_out,
    value_bd,
    output_bd,
    align_ref,
    early_out,
    seq_ref,
    res_ref,
    left_w_ref,
    right_w_ref,
    outer_ref,
    logits_w_ref,
    value_w_ref,
    gate_w_ref,
    output_w_ref,
    norm_all,
    rows_buf,
    masked_buf,
    block_buf,
    block_high,
    block_low,
    right_buf,
    left_ref,
    right_ref,
    gate_bd,
    wl_buf,
    w_buf,
    l_buf,
    r_buf,
    mask_buf,
    high_buf,
    low_buf,
    pair_ref,
    load_sem,
    left_send,
    left_recv,
    turn_sem,
    right_send,
    right_recv,
    share_send,
    share_recv,
    logits_send,
    logits_recv,
    norm_send,
    norm_recv,
    relay_send,
    relay_recv,
):
    row, col = lax.axis_index("row"), lax.axis_index("col")
    barrier = pltpu.get_barrier_semaphore()
    loads = [
        pltpu.make_async_copy(source, target, load_sem.at[at])
        for at, (source, target) in enumerate(
            [
                (right_w_in, right_w_ref),
                (res_in, res_ref),
                (left_w_in, left_w_ref),
                (seq_in, seq_ref),
                (align_in, align_ref),
                (outer_in, outer_ref),
                (gate_w_in, gate_w_ref),
                (value_w_in, value_w_ref),
                (logits_w_in, logits_w_ref),
                (output_w_in, output_w_ref),
                (pair_in, pair_ref),
            ]
        )
    ]
    for load in loads:
        load.start()

    seqs, rows, width = align_ref.shape
    factor = right_w_ref.shape[0]
    ratio, k_col = n_row // n_col, factor * seqs
    half = n_row // 2
    chip, core = row // 2, lax.rem(row, 2)
    partner = 2 * chip + 1 - core
    cols, pair_width = pair_out.shape[1], pair_out.shape[2]
    heads = logits_w_ref.shape[0]
    quarter = rows * seqs // 4
    steps = rows // here
    parts = LANES // (here * heads)
    jrows = cols // parts
    group = LANES * heads // value_w_ref.shape[1]
    premixed = high_buf.shape[0] == rows
    depth = n_col * k_col

    def peer_row(k):
        return 2 * lax.rem(chip + k, half) + core

    relayed = n_col >= 4
    at_high, at_low = col == n_col - 2, col == 1
    relay = at_high | at_low
    far_src = jnp.where(at_low, n_col - 1, 0)
    far_dest = jnp.where(at_low, 0, n_col - 1)

    def is_far(other):
        return (other - col == n_col - 1) | (col - other == n_col - 1)

    def near(other, action):
        if relayed:
            pl.when(jnp.logical_not(is_far(other)))(action)
        else:
            action()

    def unless_relayed(src, action):
        if relayed:
            pl.when(jnp.logical_not(relay & (src == far_src)))(action)
        else:
            action()

    dest = row // ratio
    spot = col * ratio + lax.rem(row, ratio)
    away = dest != col

    def meet(action):
        for k in range(1, n_col):
            other = lax.rem(col + k, n_col)
            near(other, functools.partial(action, row, other))
        for k in range(1, half):
            action(peer_row(k), col)
        action(partner, col)
        pl.when(away)(functools.partial(action, spot, dest))

    def greet(other_row, other_col):
        pl.semaphore_signal(
            barrier, inc=1, device_id=(other_row, other_col), device_id_type=MESH
        )

    greeters = half + n_col - 1 + jnp.where(away, 1, 0)
    if relayed:
        greeters = greeters - jnp.where((col == 0) | (col == n_col - 1), 1, 0)
    meet(greet)
    for at in range(4):
        loads[at].wait()
    res_row = res_ref[...].astype(F32)
    diag = iota((rows, rows), 0) == iota((rows, rows), 1)

    def column(values):
        return jnp.sum(
            jnp.where(diag, jnp.broadcast_to(values, (rows, rows)), 0.0), axis=1, keepdims=True
        )

    res_col = column(res_row)
    spread = jnp.broadcast_to(right_w_ref[...][:, None, :], (factor, seqs, width))
    row_seq = iota((factor, seqs, width), 1)
    for s in range(seqs):
        block_buf[:, s * width : (s + 1) * width] = jnp.where(row_seq == s, spread, 0.0).reshape(
            factor * seqs, width
        )
    wr_high, wr_low = split(block_buf[...])
    block_high[...] = wr_high
    block_low[...] = wr_low
    wl_high, wl_low = split(left_w_ref[...])
    right_buf[rows : rows + 8, 0:rows] = jnp.broadcast_to(res_row, (8, rows))
    right_buf[rows : rows + 8, rows:] = jnp.zeros((8, right_buf.shape[1] - rows), F32)
    loads[4].wait()
    seq_sum = 0.0
    for s in range(seqs):
        normed = layer_norm(align_ref[s])
        norm_all[row, :, s * width : (s + 1) * width] = normed
        live = seq_ref[s].astype(F32)
        seq_sum = seq_sum + live
        masked_buf[:, s * width : (s + 1) * width] = normed * (res_col * live)
    right_buf[0:rows, :] = dot_split(masked_buf[...], block_high[...], block_low[...], dot_t)
    pl.semaphore_wait(barrier, greeters)
    turn = pltpu.make_async_remote_copy(
        right_buf,
        right_ref.at[spot],
        turn_sem.at[0],
        turn_sem.at[1],
        device_id=(spot, dest),
        device_id_type=MESH,
    )
    stay = pltpu.make_async_copy(right_buf, right_ref.at[spot], turn_sem.at[1])

    @pl.when(away)
    def _():
        turn.start()

    @pl.when(jnp.logical_not(away))
    def _():
        stay.start()

    for s in range(seqs):
        rows_buf[pl.ds(s, rows, stride=seqs), :] = masked_buf[:, s * width : (s + 1) * width]
    left = dot_split(rows_buf[...], wl_high, wl_low, dot_t)
    for g in range(4):
        left_ref[col, 0:quarter, g * factor : (g + 1) * factor] = left[
            g * quarter : (g + 1) * quarter
        ]
    left_ref[col, quarter : quarter + 8, :] = jnp.full((8, left_ref.shape[2]), seq_sum, F32)

    def left_copy(k):
        return pltpu.make_async_remote_copy(
            left_ref.at[col],
            left_ref.at[col],
            left_send.at[k],
            left_recv.at[col],
            device_id=(row, lax.rem(col + k, n_col)),
            device_id_type=MESH,
        )

    def left_forward():
        return pltpu.make_async_remote_copy(
            left_ref.at[far_src],
            left_ref.at[far_src],
            left_send.at[0],
            left_recv.at[far_src],
            device_id=(row, far_dest),
            device_id_type=MESH,
        )

    def left_wait(src):
        pltpu.make_async_copy(left_ref.at[src], left_ref.at[src], left_recv.at[src]).wait()

    def right_copy(k):
        return pltpu.make_async_remote_copy(
            right_ref.at[row],
            right_ref.at[row],
            right_send,
            right_recv.at[half - k - 1],
            device_id=(peer_row(k), col),
            device_id_type=MESH,
        )

    def share_copy(k):
        src = peer_row(k)
        return pltpu.make_async_remote_copy(
            right_ref.at[src],
            right_ref.at[src],
            share_send,
            share_recv,
            device_id=(partner, col),
            device_id_type=MESH,
        )

    def norm_copy(k):
        return pltpu.make_async_remote_copy(
            norm_all.at[row],
            norm_all.at[row],
            norm_send,
            norm_recv,
            device_id=(peer_row(k), col),
            device_id_type=MESH,
        )

    def relay_copy(k):
        return pltpu.make_async_remote_copy(
            norm_all.at[peer_row(k)],
            norm_all.at[peer_row(k)],
            relay_send,
            relay_recv,
            device_id=(partner, col),
            device_id_type=MESH,
        )

    loads[5].wait()
    for b in range(factor):
        high, low = split(outer_ref[pl.ds(b, factor, stride=factor), :])
        lanes = slice(b * pair_width, (b + 1) * pair_width)
        w_buf[0:factor, lanes] = high
        w_buf[factor : 2 * factor, lanes] = low
        w_buf[2 * factor : 3 * factor, lanes] = high

    def left_rows(c, at):
        packed = left_ref[c, 0:quarter, :]
        high = packed.astype(BF16).astype(F32)
        low = packed - high
        for g in range(4):
            lanes = slice(g * factor, (g + 1) * factor)
            pieces = [high[:, lanes], high[:, lanes], low[:, lanes]]
            l_buf[at, g * quarter : (g + 1) * quarter, :] = jnp.concatenate(
                pieces, axis=1
            ).astype(BF16)

    def mix(l_rows, c, count):
        for nb in range(factor // 2):
            mixed = dot(l_rows, w_buf[:, nb * 2 * pair_width : (nb + 1) * 2 * pair_width])
            tiles = jnp.concatenate(
                [
                    mixed[:, :pair_width].reshape(count, seqs, pair_width),
                    mixed[:, pair_width:].reshape(count, seqs, pair_width),
                ],
                axis=1,
            )
            high, low = split(tiles)
            high_buf[:, c, nb] = high
            low_buf[:, c, nb] = low

    def prepare():
        for at in range(6, 11):
            loads[at].wait()

        def keep_value(h, block):
            value_bd[h] = block

        def keep_gate(h, block):
            gate_bd[h] = block

        spread_heads(gate_w_ref[...], heads, group, keep_gate)
        spread_heads(value_w_ref[...], heads, group, keep_value)
        for g in range(seqs // group):
            own = norm_all[row, :, g * group * width : (g + 1) * group * width]
            for h in range(heads):
                gate_out[g, h] = jax.nn.sigmoid(stacked_dot(own, gate_bd[h]))
        channels = output_w_ref.shape[1]
        head_width = channels // heads
        lanes = iota((width, group * width), 1)
        pick = jnp.where(iota((width, group * width), 0) == lanes % width, 1.0, 0.0).astype(BF16)
        own = (iota((2 * group * head_width, group * width), 0) // head_width) % group == iota(
            (2 * group * head_width, group * width), 1
        ) // width
        for t, half_w in enumerate(split(output_w_ref[...])):
            tiled = t_dot(half_w, pick)
            for hp in range(heads // 2):
                pieces = []
                for hh in range(2):
                    first = (2 * hp + hh) * head_width
                    pieces += [tiled[first : first + head_width]] * group
                output_bd[t, hp] = jnp.where(own, jnp.concatenate(pieces, axis=0), 0.0).astype(BF16)
        lanes = iota((heads, 2 * LANES), 1)
        low_half = iota((pair_width, 2 * LANES), 1) >= LANES
        w_high, w_low = split(logits_w_ref[...])
        for i in range(here):
            pick = jnp.where(
                ((lanes // here) % heads == iota((heads, 2 * LANES), 0)) & (lanes % here == i),
                1.0,
                0.0,
            ).astype(BF16)
            block = jnp.where(low_half, t_dot(w_low, pick), t_dot(w_high, pick))
            wl_buf[i // 2, (i % 2) * pair_width : (i % 2 + 1) * pair_width, :] = block.astype(BF16)

    low_end = col < (n_col + 1) // 2
    spot_in = jnp.where(low_end, col, n_col - 1 - col)

    def stage(k, carry):
        order = jnp.where(k - 1 < spot_in, k - 1, k)
        src = jnp.where(low_end, order, n_col - 1 - order)
        src = jnp.where(k == 0, col, src)

        @pl.when(k == 1)
        def _():
            for k2 in sorted(range(1, n_col), key=lambda d: min(d, n_col - d)):
                near(lax.rem(col + k2, n_col), left_copy(k2).start)
            prepare()
            pltpu.make_async_copy(right_buf, right_ref.at[row], turn_sem.at[1]).wait()
            for k2 in range(1, half):
                right_copy(k2).start()
            share_copy(0).start()
            if relayed:

                @pl.when(relay)
                def _():
                    left_wait(far_src)
                    left_forward().start()

        @pl.when(k == n_col - 1)
        def _():
            for k2 in range(1, half):
                pltpu.make_async_copy(
                    right_buf, right_ref.at[peer_row(k2)], right_recv.at[k2 - 1]
                ).wait()
                share_copy(k2).start()

        @pl.when(k > 0)
        def _():
            unless_relayed(src, lambda: left_wait(src))

        at = 0 if premixed else src
        left_rows(src, at)
        if premixed:
            mix(l_buf[0], src, rows)
        return carry

    lax.fori_loop(0, n_col, stage, 0)
    def blocks(ref, number, sem):
        pltpu.make_async_copy(ref.at[pl.ds(0, number)], ref.at[pl.ds(0, number)], sem).wait()

    blocks(right_ref, half, share_recv)
    count = left_ref[0, quarter : quarter + 1, 0:1]
    for c in range(1, n_col):
        count = count + left_ref[c, quarter : quarter + 1, 0:1]
    scale = 1.0 / jnp.maximum(count, 1.0)
    for c in range(n_col):
        for t in range(ratio):
            high_r, low_r = split(right_ref[c * ratio + t, 0:rows, :])
            lanes = slice(c * k_col, (c + 1) * k_col)
            r_buf[t * rows : (t + 1) * rows, lanes] = high_r
            r_buf[cols + t * rows : cols + (t + 1) * rows, lanes] = low_r
    res_cols = jnp.concatenate(
        [column(right_ref[t, rows : rows + 1, 0:rows]) for t in range(ratio)], axis=0
    )
    part_of = iota((jrows, LANES), 1) // (here * heads)
    mask = jnp.zeros((jrows, LANES), F32)
    for p in range(parts):
        dead = (res_cols[p * jrows : (p + 1) * jrows] - 1.0) * 1000000000.0
        mask = jnp.where(part_of == p, dead, mask)
    mask_buf[...] = mask

    def chunk(at):
        return pl.ds(pl.multiple_of(at * jrows, jrows), jrows)

    lag, direct = 2, 2
    first = steps - direct

    def logits_copy(k, at):
        other = lax.rem(col + k, n_col)
        sem = jnp.where(at < early, col, n_col + col)
        if relayed:
            passed = (at < first) & (
                ((col == 0) & (other == n_col - 2)) | ((col == n_col - 1) & (other == 1))
            )
            sem = jnp.where(passed, 2 * n_col + at, sem)
        return pltpu.make_async_remote_copy(
            slots.at[col, chunk(at)],
            slots.at[col, chunk(at)],
            logits_send.at[k],
            logits_recv.at[sem],
            device_id=(row, other),
            device_id_type=MESH,
        )

    def logits_forward(at):
        return pltpu.make_async_remote_copy(
            slots.at[far_src, chunk(at)],
            slots.at[far_src, chunk(at)],
            logits_send.at[0],
            logits_recv.at[jnp.where(at < early, far_src, n_col + far_src)],
            device_id=(row, far_dest),
            device_id_type=MESH,
        )

    def chunks(src, number, sem):
        part = slots.at[src, pl.ds(0, number * jrows)]
        pltpu.make_async_copy(part, part, sem).wait()

    def pass_on(at):
        @pl.when(relay)
        def _():
            chunks(far_src, 1, logits_recv.at[2 * n_col + at])
            logits_forward(at).start()

    def body(step, carry):
        first_row = pl.multiple_of(step * here, here)
        if not premixed:
            size = here * seqs
            for c in range(n_col):
                mix(l_buf[c, pl.ds(pl.multiple_of(step * size, size), size), :], c, here)
        r_both = r_buf[...]
        for p in range(here // 2):
            at = [2 * p + t + (first_row if premixed else 0) for t in range(2)]
            right_high = jnp.concatenate(
                [high_buf[i].reshape(depth, pair_width) for i in at], axis=1
            )
            right_low = jnp.concatenate([low_buf[i].reshape(depth, pair_width) for i in at], axis=1)
            first = dot(r_both, right_high)
            sums = first[:cols] + (first[cols:] + dot(r_both[:cols], right_low))
            for t in range(2):
                i = first_row + 2 * p + t
                pair_out[i] = pair_ref[i] + sums[:, t * pair_width : (t + 1) * pair_width] * scale
        total = None
        batch = here // 2
        for g in range(0, here, batch):
            pairs = pair_out[pl.ds(first_row + g, batch)].reshape(batch * cols, pair_width)
            high, low = split(layer_norm(pairs))
            for p in range(batch // 2):
                both = jnp.concatenate(
                    [
                        jnp.concatenate(
                            [
                                half_x[(2 * p + t) * cols : (2 * p + t + 1) * cols]
                                for t in range(2)
                            ],
                            axis=1,
                        )
                        for half_x in (high, low)
                    ],
                    axis=0,
                )
                out = dot(both, wl_buf[g // 2 + p])
                out = out[:, :LANES] + out[:, LANES:]
                out = out[:cols] + out[cols:]
                total = out if total is None else total + out
        logits = total[:jrows]
        for p in range(1, parts):
            logits = jnp.where(part_of == p, total[p * jrows : (p + 1) * jrows], logits)
        slots[col, chunk(step), :] = logits + mask_buf[...]
        for k in range(1, n_col):
            other = lax.rem(col + k, n_col)
            if relayed:
                pl.when(jnp.logical_not(is_far(other)) | (step >= steps - direct))(
                    logits_copy(k, step).start
                )
            else:
                logits_copy(k, step).start()
        if relayed:

            @pl.when(step >= lag)
            def _():
                pass_on(step - lag)

        @pl.when(step == 1)
        def _():
            relay_copy(0).start()
            for k in range(1, half):
                norm_copy(k).start()

        return carry

    lax.fori_loop(0, steps, body, 0)
    if relayed:
        for at in range(steps - lag, first):
            pass_on(at)
    blocks(norm_all, half - 1, norm_recv)
    for k in range(1, half):
        relay_copy(k).start()
    blocks(right_ref, half, share_send)
    blocks(right_ref, half - 1, right_send)
    for k in range(1, n_col):
        near(lax.rem(col + k, n_col), left_copy(k).wait_send)

    @pl.when(away)
    def _():
        turn.wait_send()

    if relayed:

        @pl.when(relay)
        def _():
            left_forward().wait_send()
            chunks(far_src, first, logits_send.at[0])

    blocks(norm_all, half, relay_recv)
    for r in range(n_row):
        high, low = split(norm_all[r])
        norm_high[r] = high
        norm_low[r] = low
    for k in range(1, n_col):
        other = lax.rem(col + k, n_col)
        unless_relayed(other, lambda: chunks(other, early, logits_recv.at[other]))

    def keep(s, values):
        early_out[s] = values

    average_rows(
        here,
        range(early),
        slots,
        norm_high[...].reshape(n_row * rows, seqs * width),
        norm_low[...].reshape(n_row * rows, seqs * width),
        gate_out,
        value_bd,
        output_bd,
        align_ref,
        keep,
    )
    blocks(norm_all, half - 1, norm_send)
    blocks(norm_all, half, relay_send)
    for k in range(1, n_col):
        other = lax.rem(col + k, n_col)
        if relayed:
            near(other, lambda: chunks(col, steps, logits_send.at[k]))
            pl.when(is_far(other))(lambda: chunks(col, direct, logits_send.at[k]))
        else:
            chunks(col, steps, logits_send.at[k])
        last = logits_recv.at[n_col + other]
        unless_relayed(other, lambda: chunks(other, steps - early, last))
        if relayed:
            pl.when(relay & (other == far_src))(lambda: chunks(other, direct, last))


def average_rows(
    here, taken, slots, norm_high, norm_low, gate_ref, value_bd, output_bd, align_ref, store
):
    seqs, rows, width = align_ref.shape
    n_col, total_rows, _ = slots.shape
    groups, heads = gate_ref.shape[0], gate_ref.shape[1]
    group = seqs // groups
    jrows = total_rows // (rows // here)
    wide = here * heads
    parts = LANES // wide
    own_rows = slice(taken[0] * here, (taken[-1] + 1) * here)
    part_of = iota((jrows, LANES), 1) // wide

    def over_parts(values, combine):
        out = values
        for p in range(1, parts):
            out = combine(out, pltpu.roll(values, p * wide, 1))
        return out

    weights = []
    for t in taken:
        pieces = [slots[c, t * jrows : (t + 1) * jrows, :] for c in range(n_col)]
        top = pieces[0]
        for piece in pieces[1:]:
            top = jnp.maximum(top, piece)
        top = over_parts(jnp.max(top, axis=0, keepdims=True), jnp.maximum)
        pieces = [jnp.exp(piece - top) for piece in pieces]
        total = pieces[0]
        for piece in pieces[1:]:
            total = total + piece
        inverse = 1.0 / over_parts(jnp.sum(total, axis=0, keepdims=True), jnp.add)
        weights.append([piece * inverse for piece in pieces])
    turned = []
    for t in range(0, len(taken), parts):
        blocks = []
        for c in range(n_col):
            for p in range(parts):
                block = None
                for q in range(parts):
                    value = weights[t + q][c]
                    shift = (q - p) % parts * wide
                    if shift:
                        value = pltpu.roll(value, shift, 1)
                    block = value if block is None else jnp.where(part_of == q, value, block)
                blocks.append(block)
        turned.append(jnp.concatenate(blocks, axis=0).T)
    mixed = dot_split(jnp.concatenate(turned, axis=0), norm_high, norm_low)
    for g in range(groups):
        gated = []
        for h in range(heads):
            own = jnp.concatenate(
                [
                    mixed[
                        t * wide + h * here : t * wide + (h + 1) * here,
                        g * group * width : (g + 1) * group * width,
                    ]
                    for t in range(len(taken))
                ],
                axis=0,
            )
            gated.append(stacked_dot(own, value_bd[h]) * gate_ref[g, h, own_rows, :])
        out = None
        for hp in range(heads // 2):
            part = dot_split(
                jnp.concatenate(gated[2 * hp : 2 * hp + 2], axis=1),
                output_bd[0, hp],
                output_bd[1, hp],
            )
            out = part if out is None else out + part
        for s in range(group):
            at = g * group + s
            store(at, align_ref[at, own_rows, :] + out[:, s * width : (s + 1) * width])


def average_kernel(
    here,
    early,
    slots,
    norm_high,
    norm_low,
    gate_ref,
    value_bd,
    output_bd,
    align_ref,
    early_ref,
    pair_ref,
    out_any,
    pair_any,
    out_buf,
    sems,
):
    rows = align_ref.shape[1]
    steps = rows // here
    first = early * here
    copies = [
        pltpu.make_async_copy(pair_ref, pair_any, sems.at[0]),
        pltpu.make_async_copy(early_ref, out_any.at[:, pl.ds(0, first), :], sems.at[1]),
        pltpu.make_async_copy(out_buf, out_any.at[:, pl.ds(first, rows - first), :], sems.at[2]),
    ]
    copies[0].start()
    copies[1].start()

    def keep(s, values):
        out_buf[s] = values

    average_rows(
        here,
        range(early, steps),
        slots,
        norm_high[...],
        norm_low[...],
        gate_ref,
        value_bd,
        output_bd,
        align_ref,
        keep,
    )
    copies[2].start()
    for copy in copies:
        copy.wait()


def per_device(
    n_row,
    n_col,
    alignment,
    pair_rep,
    seq_mask,
    res_mask,
    left_weight,
    right_weight,
    w_outer,
    w_logits,
    value_weight,
    gate_weight,
    output_weight,
):
    seqs, rows, width = alignment.shape
    cols, pair_width = pair_rep.shape[1], pair_rep.shape[2]
    factor = left_weight.shape[1]
    heads = w_logits.shape[1]
    channels = value_weight.shape[1]
    k_col = factor * seqs
    quarter = rows * seqs // 4
    half = n_row // 2
    here = 8
    steps = rows // here
    early = LANES // (here * heads)
    jrows = cols * here * heads // LANES
    group = LANES * heads // channels
    groups = seqs // group
    vmem = pl.BlockSpec(memory_space=pltpu.VMEM)
    anywhere = pl.BlockSpec(memory_space=pl.ANY)
    dma = pltpu.SemaphoreType.DMA
    left_shape = (quarter + 8, 4 * factor)
    right_shape = (rows + 8, k_col)
    mix_row = (n_col, factor // 2, 2 * seqs, pair_width)
    row_bytes = 4 * n_col * k_col * pair_width
    premixed = rows * row_bytes <= MIX_BYTES
    held = rows if premixed else here
    pair_new, slots, norm_high, norm_low, gate, value_bd, output_bd, align, started = pl.pallas_call(
        functools.partial(pair_kernel, n_row, n_col, here, early),
        out_shape=(
            pltpu.VMEM(pair_rep.shape, F32),
            pltpu.VMEM((n_col, steps * jrows, LANES), F32),
            pltpu.VMEM((n_row, rows, seqs * width), BF16),
            pltpu.VMEM((n_row, rows, seqs * width), BF16),
            pltpu.VMEM((groups, heads, rows, LANES), F32),
            pltpu.VMEM((heads, group * width, 2 * LANES), BF16),
            pltpu.VMEM((2, heads // 2, 2 * LANES, group * width), BF16),
            pltpu.VMEM(alignment.shape, F32),
            pltpu.VMEM((seqs, early * here, width), F32),
        ),
        in_specs=[anywhere] * 11,
        out_specs=(vmem,) * 9,
        scratch_shapes=[
            pltpu.SMEM((seqs,), jnp.int32),
            pltpu.VMEM((1, rows), jnp.int32),
            pltpu.VMEM((factor, width), F32),
            pltpu.VMEM((factor, width), F32),
            pltpu.VMEM(w_outer.shape, F32),
            pltpu.VMEM((heads, pair_width), F32),
            pltpu.VMEM(value_weight.shape, F32),
            pltpu.VMEM(gate_weight.shape, F32),
            pltpu.VMEM((width, channels), F32),
            pltpu.VMEM((n_row, rows, seqs * width), F32),
            pltpu.VMEM((rows * seqs, width), F32),
            pltpu.VMEM((rows, seqs * width), F32),
            pltpu.VMEM((k_col, seqs * width), F32),
            pltpu.VMEM((k_col, seqs * width), BF16),
            pltpu.VMEM((k_col, seqs * width), BF16),
            pltpu.VMEM(right_shape, F32),
            pltpu.VMEM((n_col,) + left_shape, F32),
            pltpu.VMEM((n_row,) + right_shape, F32),
            pltpu.VMEM((heads, group * width, 2 * LANES), BF16),
            pltpu.VMEM((here // 2, 2 * pair_width, 2 * LANES), BF16),
            pltpu.VMEM((3 * factor, factor * pair_width), BF16),
            pltpu.VMEM((1 if premixed else n_col, rows * seqs, 3 * factor), BF16),
            pltpu.VMEM((2 * cols, n_col * k_col), BF16),
            pltpu.VMEM((jrows, LANES), F32),
            pltpu.VMEM((held,) + mix_row, BF16),
            pltpu.VMEM((held,) + mix_row, BF16),
            pltpu.VMEM(pair_rep.shape, F32),
            dma((11,)),
            dma((n_col,)),
            dma((n_col,)),
            dma((2,)),
            dma,
            dma((half - 1,)),
            dma,
            dma,
            dma((n_col,)),
            dma((2 * n_col + steps,)),
            dma,
            dma,
            dma,
            dma,
        ],
        compiler_params=pltpu.CompilerParams(
            collective_id=0, has_side_effects=True, vmem_limit_bytes=PAIR_VMEM
        ),
        name="pair",
    )(
        seq_mask,
        res_mask.reshape(1, rows),
        alignment,
        left_weight.T,
        right_weight.T,
        w_outer,
        w_logits.T,
        value_weight,
        gate_weight,
        output_weight.T,
        pair_rep,
    )
    alignment_out, pair_final = pl.pallas_call(
        functools.partial(average_kernel, here, early),
        out_shape=(
            jax.ShapeDtypeStruct(alignment.shape, F32),
            jax.ShapeDtypeStruct(pair_rep.shape, F32),
        ),
        in_specs=[vmem] * 9,
        out_specs=(anywhere, anywhere),
        scratch_shapes=[pltpu.VMEM((seqs, (steps - early) * here, width), F32), dma((3,))],
        compiler_params=pltpu.CompilerParams(vmem_limit_bytes=AVERAGE_VMEM),
        name="average",
    )(
        slots,
        norm_high.reshape(n_row * rows, seqs * width),
        norm_low.reshape(n_row * rows, seqs * width),
        gate,
        value_bd,
        output_bd,
        align,
        started,
        pair_new,
    )
    return (alignment_out, pair_final)


def solution(mesh):
    in_specs = (P("col", "row", None), P("row", "col", None), P("col"), P("row")) + (P(),) * 7
    out_specs = (P("col", "row", None), P("row", "col", None))
    return jax.shard_map(
        functools.partial(per_device, mesh.shape["row"], mesh.shape["col"]),
        mesh=mesh,
        in_specs=in_specs,
        out_specs=out_specs,
        check_vma=False,
    )
```

```python
import functools

import jax
import jax.numpy as jnp
from jax import lax
from jax.experimental import pallas as pl
from jax.experimental.pallas import tpu as pltpu
from jax.sharding import PartitionSpec as P

MESH = pl.DeviceIdType.MESH
F32 = jnp.float32
BF16 = jnp.bfloat16
epsilon = 1e-05
PAIR_VMEM = 48 * 1024 * 1024
AVERAGE_VMEM = 24 * 1024 * 1024
MIX_BYTES = 30 * 1024 * 1024
LANES = 128


def layer_norm(values):
    center = jnp.mean(values, axis=-1, keepdims=True)
    centred = values - center
    return centred * lax.rsqrt(jnp.mean(centred * centred, axis=-1, keepdims=True) + epsilon)


def split(values):
    high = values.astype(BF16)
    return high, (values - high.astype(F32)).astype(BF16)


def dot(left, right):
    return jnp.dot(left, right, preferred_element_type=F32)


def dot_t(left, right):
    return lax.dot_general(left, right, (((1,), (1,)), ((), ())), preferred_element_type=F32)


def t_dot(left, right):
    return lax.dot_general(left, right, (((0,), (0,)), ((), ())), preferred_element_type=F32)


def dot_split(left, right_high, right_low, multiply=dot):
    high, low = split(left)
    return multiply(high, right_high) + (multiply(low, right_high) + multiply(high, right_low))


def iota(shape, axis):
    return lax.broadcasted_iota(jnp.int32, shape, axis)


def stacked_dot(values, weights):
    count, half = values.shape[0], weights.shape[1] // 2
    high, low = split(values)
    out = dot(jnp.concatenate([high, low], axis=0), weights)
    out = out[:, :half] + out[:, half:]
    return out[:count] + out[count:]


def spread_heads(weight, heads, group, store):
    width, channels = weight.shape
    head_width = channels // heads
    both = jnp.concatenate(split(weight), axis=0)
    rows, lanes = iota((channels, LANES), 0), iota((channels, LANES), 1)
    own = iota((group * width, LANES), 0) // width == iota((group * width, LANES), 1) // head_width
    for h in range(heads):
        pick = jnp.where(rows == h * head_width + lanes % head_width, 1.0, 0.0).astype(BF16)
        tiled = dot(both, pick)
        parts = []
        for t in range(2):
            piece = jnp.concatenate([tiled[t * width : (t + 1) * width]] * group, axis=0)
            parts.append(jnp.where(own, piece, 0.0))
        store(h, jnp.concatenate(parts, axis=1).astype(BF16))


def pair_kernel(
    n_row,
    n_col,
    here,
    early,
    seq_in,
    res_in,
    align_in,
    left_w_in,
    right_w_in,
    outer_in,
    logits_w_in,
    value_w_in,
    gate_w_in,
    output_w_in,
    pair_in,
    pair_out,
    slots,
    mask_out,
    norm_high,
    norm_low,
    gate_out,
    value_bd,
    output_bd,
    align_ref,
    early_out,
    seq_ref,
    res_ref,
    left_w_ref,
    right_w_ref,
    outer_ref,
    logits_w_ref,
    value_w_ref,
    gate_w_ref,
    output_w_ref,
    norm_all,
    rows_buf,
    masked_buf,
    block_buf,
    block_high,
    block_low,
    right_buf,
    left_ref,
    right_ref,
    gate_bd,
    wl_buf,
    w_buf,
    l_buf,
    r_buf,
    high_buf,
    low_buf,
    pair_ref,
    load_sem,
    left_send,
    left_recv,
    turn_sem,
    right_send,
    right_recv,
    share_send,
    share_recv,
    logits_send,
    logits_recv,
    norm_send,
    norm_recv,
    relay_send,
    relay_recv,
):
    row, col = lax.axis_index("row"), lax.axis_index("col")
    barrier = pltpu.get_barrier_semaphore()
    loads = [
        pltpu.make_async_copy(source, target, load_sem.at[at])
        for at, (source, target) in enumerate(
            [
                (right_w_in, right_w_ref),
                (res_in, res_ref),
                (left_w_in, left_w_ref),
                (seq_in, seq_ref),
                (align_in, align_ref),
                (outer_in, outer_ref),
                (gate_w_in, gate_w_ref),
                (value_w_in, value_w_ref),
                (logits_w_in, logits_w_ref),
                (output_w_in, output_w_ref),
                (pair_in, pair_ref),
            ]
        )
    ]
    for load in loads:
        load.start()

    seqs, rows, width = align_ref.shape
    factor = right_w_ref.shape[0]
    ratio, k_col = n_row // n_col, factor * seqs
    half = n_row // 2
    chip, core = row // 2, lax.rem(row, 2)
    partner = 2 * chip + 1 - core
    cols, pair_width = pair_out.shape[1], pair_out.shape[2]
    heads = logits_w_ref.shape[0]
    quarter = rows * seqs // 4
    steps = rows // here
    parts = LANES // (here * heads)
    jrows = cols // parts
    group = LANES * heads // value_w_ref.shape[1]
    premixed = high_buf.shape[0] == rows
    depth = n_col * k_col

    def peer_row(k):
        return 2 * lax.rem(chip + k, half) + core

    relayed = n_col >= 4
    at_high, at_low = col == n_col - 2, col == 1
    relay = at_high | at_low
    far_src = jnp.where(at_low, n_col - 1, 0)
    far_dest = jnp.where(at_low, 0, n_col - 1)

    def is_far(other):
        return (other - col == n_col - 1) | (col - other == n_col - 1)

    def near(other, action):
        if relayed:
            pl.when(jnp.logical_not(is_far(other)))(action)
        else:
            action()

    def unless_relayed(src, action):
        if relayed:
            pl.when(jnp.logical_not(relay & (src == far_src)))(action)
        else:
            action()

    dest = row // ratio
    spot = col * ratio + lax.rem(row, ratio)
    away = dest != col

    def meet(action):
        for k in range(1, n_col):
            other = lax.rem(col + k, n_col)
            near(other, functools.partial(action, row, other))
        for k in range(1, half):
            action(peer_row(k), col)
        action(partner, col)
        pl.when(away)(functools.partial(action, spot, dest))

    def greet(other_row, other_col):
        pl.semaphore_signal(
            barrier, inc=1, device_id=(other_row, other_col), device_id_type=MESH
        )

    greeters = half + n_col - 1 + jnp.where(away, 1, 0)
    if relayed:
        greeters = greeters - jnp.where((col == 0) | (col == n_col - 1), 1, 0)
    meet(greet)
    for at in range(4):
        loads[at].wait()
    res_row = res_ref[...].astype(F32)
    diag = iota((rows, rows), 0) == iota((rows, rows), 1)

    def column(values):
        return jnp.sum(
            jnp.where(diag, jnp.broadcast_to(values, (rows, rows)), 0.0), axis=1, keepdims=True
        )

    res_col = column(res_row)
    spread = jnp.broadcast_to(right_w_ref[...][:, None, :], (factor, seqs, width))
    row_seq = iota((factor, seqs, width), 1)
    for s in range(seqs):
        block_buf[:, s * width : (s + 1) * width] = jnp.where(row_seq == s, spread, 0.0).reshape(
            factor * seqs, width
        )
    wr_high, wr_low = split(block_buf[...])
    block_high[...] = wr_high
    block_low[...] = wr_low
    wl_high, wl_low = split(left_w_ref[...])
    norm_all[row, rows : rows + 8, 0:rows] = jnp.broadcast_to(res_row, (8, rows))
    norm_all[row, rows : rows + 8, rows:] = jnp.zeros((8, seqs * width - rows), F32)
    loads[4].wait()
    seq_sum = 0.0
    for s in range(seqs):
        normed = layer_norm(align_ref[s])
        norm_all[row, 0:rows, s * width : (s + 1) * width] = normed
        live = seq_ref[s].astype(F32)
        seq_sum = seq_sum + live
        masked_buf[:, s * width : (s + 1) * width] = normed * (res_col * live)
    right_buf[...] = dot_split(masked_buf[...], block_high[...], block_low[...], dot_t)
    pl.semaphore_wait(barrier, greeters)
    turn = pltpu.make_async_remote_copy(
        right_buf,
        right_ref.at[spot],
        turn_sem.at[0],
        turn_sem.at[1],
        device_id=(spot, dest),
        device_id_type=MESH,
    )
    stay = pltpu.make_async_copy(right_buf, right_ref.at[spot], turn_sem.at[1])

    @pl.when(away)
    def _():
        turn.start()

    @pl.when(jnp.logical_not(away))
    def _():
        stay.start()

    for s in range(seqs):
        rows_buf[pl.ds(s, rows, stride=seqs), :] = masked_buf[:, s * width : (s + 1) * width]
    left = dot_split(rows_buf[...], wl_high, wl_low, dot_t)
    for g in range(4):
        left_ref[col, 0:quarter, g * factor : (g + 1) * factor] = left[
            g * quarter : (g + 1) * quarter
        ]
    left_ref[col, quarter : quarter + 8, :] = jnp.full((8, left_ref.shape[2]), seq_sum, F32)

    def left_copy(k):
        return pltpu.make_async_remote_copy(
            left_ref.at[col],
            left_ref.at[col],
            left_send.at[k],
            left_recv.at[col],
            device_id=(row, lax.rem(col + k, n_col)),
            device_id_type=MESH,
        )

    def left_forward():
        return pltpu.make_async_remote_copy(
            left_ref.at[far_src],
            left_ref.at[far_src],
            left_send.at[0],
            left_recv.at[far_src],
            device_id=(row, far_dest),
            device_id_type=MESH,
        )

    def left_wait(src):
        pltpu.make_async_copy(left_ref.at[src], left_ref.at[src], left_recv.at[src]).wait()

    def right_copy(k):
        return pltpu.make_async_remote_copy(
            right_ref.at[row],
            right_ref.at[row],
            right_send,
            right_recv.at[half - k - 1],
            device_id=(peer_row(k), col),
            device_id_type=MESH,
        )

    def share_copy(k):
        src = peer_row(k)
        return pltpu.make_async_remote_copy(
            right_ref.at[src],
            right_ref.at[src],
            share_send,
            share_recv,
            device_id=(partner, col),
            device_id_type=MESH,
        )

    def norm_copy(k):
        return pltpu.make_async_remote_copy(
            norm_all.at[row],
            norm_all.at[row],
            norm_send,
            norm_recv,
            device_id=(peer_row(k), col),
            device_id_type=MESH,
        )

    def relay_copy(k):
        return pltpu.make_async_remote_copy(
            norm_all.at[peer_row(k)],
            norm_all.at[peer_row(k)],
            relay_send,
            relay_recv,
            device_id=(partner, col),
            device_id_type=MESH,
        )

    loads[5].wait()
    for b in range(factor):
        high, low = split(outer_ref[pl.ds(b, factor, stride=factor), :])
        lanes = slice(b * pair_width, (b + 1) * pair_width)
        w_buf[0:factor, lanes] = high
        w_buf[factor : 2 * factor, lanes] = low
        w_buf[2 * factor : 3 * factor, lanes] = high

    def left_rows(c, at):
        packed = left_ref[c, 0:quarter, :]
        high = packed.astype(BF16).astype(F32)
        low = packed - high
        for g in range(4):
            lanes = slice(g * factor, (g + 1) * factor)
            pieces = [high[:, lanes], high[:, lanes], low[:, lanes]]
            l_buf[at, g * quarter : (g + 1) * quarter, :] = jnp.concatenate(
                pieces, axis=1
            ).astype(BF16)

    def mix(l_rows, c, count):
        for nb in range(factor // 2):
            mixed = dot(l_rows, w_buf[:, nb * 2 * pair_width : (nb + 1) * 2 * pair_width])
            tiles = jnp.concatenate(
                [
                    mixed[:, :pair_width].reshape(count, seqs, pair_width),
                    mixed[:, pair_width:].reshape(count, seqs, pair_width),
                ],
                axis=1,
            )
            high, low = split(tiles)
            high_buf[:, c, nb] = high
            low_buf[:, c, nb] = low

    def prepare():
        for at in range(6, 11):
            loads[at].wait()

        def keep_value(h, block):
            value_bd[h] = block

        def keep_gate(h, block):
            gate_bd[h] = block

        spread_heads(gate_w_ref[...], heads, group, keep_gate)
        spread_heads(value_w_ref[...], heads, group, keep_value)
        groups = seqs // group
        own = jnp.concatenate(
            [
                norm_all[row, 0:rows, g * group * width : (g + 1) * group * width]
                for g in range(groups)
            ],
            axis=0,
        )
        for h in range(heads):
            gate = jax.nn.sigmoid(stacked_dot(own, gate_bd[h]))
            for g in range(groups):
                gate_out[g, h] = gate[g * rows : (g + 1) * rows]
        channels = output_w_ref.shape[1]
        head_width = channels // heads
        lanes = iota((width, group * width), 1)
        pick = jnp.where(iota((width, group * width), 0) == lanes % width, 1.0, 0.0).astype(BF16)
        own = (iota((2 * group * head_width, group * width), 0) // head_width) % group == iota(
            (2 * group * head_width, group * width), 1
        ) // width
        for t, half_w in enumerate(split(output_w_ref[...])):
            tiled = t_dot(half_w, pick)
            for hp in range(heads // 2):
                pieces = []
                for hh in range(2):
                    first = (2 * hp + hh) * head_width
                    pieces += [tiled[first : first + head_width]] * group
                output_bd[t, hp] = jnp.where(own, jnp.concatenate(pieces, axis=0), 0.0).astype(BF16)
        lanes = iota((heads, 2 * LANES), 1)
        low_half = iota((pair_width, 2 * LANES), 1) >= LANES
        w_high, w_low = split(logits_w_ref[...])
        for i in range(here):
            pick = jnp.where(
                ((lanes // here) % heads == iota((heads, 2 * LANES), 0)) & (lanes % here == i),
                1.0,
                0.0,
            ).astype(BF16)
            block = jnp.where(low_half, t_dot(w_low, pick), t_dot(w_high, pick))
            wl_buf[i // 2, (i % 2) * pair_width : (i % 2 + 1) * pair_width, :] = block.astype(BF16)

    low_end = col < (n_col + 1) // 2
    spot_in = jnp.where(low_end, col, n_col - 1 - col)

    def stage(k, carry):
        order = jnp.where(k - 1 < spot_in, k - 1, k)
        src = jnp.where(low_end, order, n_col - 1 - order)
        src = jnp.where(k == 0, col, src)

        @pl.when(k == 1)
        def _():
            for k2 in sorted(range(1, n_col), key=lambda d: min(d, n_col - d)):
                near(lax.rem(col + k2, n_col), left_copy(k2).start)
            prepare()
            pltpu.make_async_copy(right_buf, right_ref.at[row], turn_sem.at[1]).wait()
            odd = lax.rem(chip, 2)
            right_copy(half - 1 - odd * (half - 2)).start()
            right_copy(1 + odd * (half - 2)).start()
            for k2 in range(2, half - 1):
                right_copy(k2).start()
            share_copy(0).start()
            if relayed:

                @pl.when(relay)
                def _():
                    left_wait(far_src)
                    left_forward().start()

        @pl.when(k == n_col - 1)
        def _():
            for k2 in range(1, half):
                pltpu.make_async_copy(
                    right_buf, right_ref.at[peer_row(k2)], right_recv.at[k2 - 1]
                ).wait()
                share_copy(k2).start()

        @pl.when(k > 0)
        def _():
            unless_relayed(src, lambda: left_wait(src))

        at = 0 if premixed else src
        left_rows(src, at)
        if premixed:
            mix(l_buf[0], src, rows)
        return carry

    lax.fori_loop(0, n_col, stage, 0)
    def blocks(ref, number, sem):
        pltpu.make_async_copy(ref.at[pl.ds(0, number)], ref.at[pl.ds(0, number)], sem).wait()

    blocks(right_ref, half, share_recv)
    count = left_ref[0, quarter : quarter + 1, 0:1]
    for c in range(1, n_col):
        count = count + left_ref[c, quarter : quarter + 1, 0:1]
    scale = 1.0 / jnp.maximum(count, 1.0)
    for c in range(n_col):
        for t in range(ratio):
            high_r, low_r = split(right_ref[c * ratio + t])
            lanes = slice(c * k_col, (c + 1) * k_col)
            r_buf[t * rows : (t + 1) * rows, lanes] = high_r
            r_buf[cols + t * rows : cols + (t + 1) * rows, lanes] = low_r
    part_of = iota((jrows, LANES), 1) // (here * heads)

    def chunk(at):
        return pl.ds(pl.multiple_of(at * jrows, jrows), jrows)

    lag, direct = 2, 2
    first = steps - direct

    def logits_copy(k, at):
        other = lax.rem(col + k, n_col)
        sem = jnp.where(at < early, col, n_col + col)
        if relayed:
            passed = (at < first) & (
                ((col == 0) & (other == n_col - 2)) | ((col == n_col - 1) & (other == 1))
            )
            sem = jnp.where(passed, 2 * n_col + at, sem)
        return pltpu.make_async_remote_copy(
            slots.at[col, chunk(at)],
            slots.at[col, chunk(at)],
            logits_send.at[k],
            logits_recv.at[sem],
            device_id=(row, other),
            device_id_type=MESH,
        )

    def logits_forward(at):
        return pltpu.make_async_remote_copy(
            slots.at[far_src, chunk(at)],
            slots.at[far_src, chunk(at)],
            logits_send.at[0],
            logits_recv.at[jnp.where(at < early, far_src, n_col + far_src)],
            device_id=(row, far_dest),
            device_id_type=MESH,
        )

    def chunks(src, number, sem):
        part = slots.at[src, pl.ds(0, number * jrows)]
        pltpu.make_async_copy(part, part, sem).wait()

    def pass_on(at):
        @pl.when(relay)
        def _():
            chunks(far_src, 1, logits_recv.at[2 * n_col + at])
            logits_forward(at).start()

    def body(step, carry):
        first_row = pl.multiple_of(step * here, here)
        if not premixed:
            size = here * seqs
            for c in range(n_col):
                mix(l_buf[c, pl.ds(pl.multiple_of(step * size, size), size), :], c, here)
        r_both = r_buf[...]
        for p in range(here // 2):
            at = [2 * p + t + (first_row if premixed else 0) for t in range(2)]
            right_high = jnp.concatenate(
                [high_buf[i].reshape(depth, pair_width) for i in at], axis=1
            )
            right_low = jnp.concatenate([low_buf[i].reshape(depth, pair_width) for i in at], axis=1)
            product = dot(r_both, right_high)
            sums = product[:cols] + (product[cols:] + dot(r_both[:cols], right_low))
            for t in range(2):
                i = first_row + 2 * p + t
                pair_out[i] = pair_ref[i] + sums[:, t * pair_width : (t + 1) * pair_width] * scale
        total = None
        batch = here // 2
        for g in range(0, here, batch):
            pairs = pair_out[pl.ds(first_row + g, batch)].reshape(batch * cols, pair_width)
            high, low = split(layer_norm(pairs))
            for p in range(batch // 2):
                both = jnp.concatenate(
                    [
                        jnp.concatenate(
                            [
                                half_x[(2 * p + t) * cols : (2 * p + t + 1) * cols]
                                for t in range(2)
                            ],
                            axis=1,
                        )
                        for half_x in (high, low)
                    ],
                    axis=0,
                )
                out = dot(both, wl_buf[g // 2 + p])
                out = out[:, :LANES] + out[:, LANES:]
                out = out[:cols] + out[cols:]
                total = out if total is None else total + out
        logits = total[:jrows]
        for p in range(1, parts):
            logits = jnp.where(part_of == p, total[p * jrows : (p + 1) * jrows], logits)
        slots[col, chunk(step), :] = logits
        for k in range(1, n_col):
            other = lax.rem(col + k, n_col)
            if relayed:
                pl.when(jnp.logical_not(is_far(other)) | (step >= steps - direct))(
                    logits_copy(k, step).start
                )
            else:
                logits_copy(k, step).start()
        if relayed:

            @pl.when(step >= lag)
            def _():
                pass_on(step - lag)

        @pl.when(step == 1)
        def _():
            relay_copy(0).start()
            for k in range(1, half):
                norm_copy(k).start()

        return carry

    lax.fori_loop(0, steps, body, 0)
    if relayed:
        for at in range(steps - lag, first):
            pass_on(at)
    blocks(norm_all, half - 1, norm_recv)
    for k in range(1, half):
        relay_copy(k).start()
    blocks(right_ref, half, share_send)
    blocks(right_ref, half - 1, right_send)
    for k in range(1, n_col):
        near(lax.rem(col + k, n_col), left_copy(k).wait_send)

    @pl.when(away)
    def _():
        turn.wait_send()

    if relayed:

        @pl.when(relay)
        def _():
            left_forward().wait_send()
            chunks(far_src, first, logits_send.at[0])

    blocks(norm_all, half, relay_recv)
    for r in range(n_row):
        high, low = split(norm_all[r, 0:rows, :])
        norm_high[r] = high
        norm_low[r] = low
    for c in range(n_col):
        res_cols = jnp.concatenate(
            [column(norm_all[c * ratio + t, rows : rows + 1, 0:rows]) for t in range(ratio)],
            axis=0,
        )
        mask = jnp.zeros((jrows, LANES), F32)
        for p in range(parts):
            dead = (res_cols[p * jrows : (p + 1) * jrows] - 1.0) * 1000000000.0
            mask = jnp.where(part_of == p, dead, mask)
        mask_out[c] = mask
    for k in range(1, n_col):
        other = lax.rem(col + k, n_col)
        unless_relayed(other, lambda: chunks(other, early, logits_recv.at[other]))

    def keep(s, values):
        early_out[s] = values

    average_rows(
        here,
        range(early),
        slots,
        mask_out,
        norm_high[...].reshape(n_row * rows, seqs * width),
        norm_low[...].reshape(n_row * rows, seqs * width),
        gate_out,
        value_bd,
        output_bd,
        align_ref,
        keep,
    )
    blocks(norm_all, half - 1, norm_send)
    blocks(norm_all, half, relay_send)
    for k in range(1, n_col):
        other = lax.rem(col + k, n_col)
        if relayed:
            near(other, lambda: chunks(col, steps, logits_send.at[k]))
            pl.when(is_far(other))(lambda: chunks(col, direct, logits_send.at[k]))
        else:
            chunks(col, steps, logits_send.at[k])
        last = logits_recv.at[n_col + other]
        unless_relayed(other, lambda: chunks(other, steps - early, last))
        if relayed:
            pl.when(relay & (other == far_src))(lambda: chunks(other, direct, last))


def average_rows(
    here, taken, slots, mask_ref, norm_high, norm_low, gate_ref, value_bd, output_bd, align_ref, store
):
    seqs, rows, width = align_ref.shape
    n_col, total_rows, _ = slots.shape
    groups, heads = gate_ref.shape[0], gate_ref.shape[1]
    group = seqs // groups
    jrows = total_rows // (rows // here)
    wide = here * heads
    parts = LANES // wide
    own_rows = slice(taken[0] * here, (taken[-1] + 1) * here)
    part_of = iota((jrows, LANES), 1) // wide

    def over_parts(values, combine):
        out = values
        for p in range(1, parts):
            out = combine(out, pltpu.roll(values, p * wide, 1))
        return out

    weights = []
    for t in taken:
        pieces = [
            slots[c, t * jrows : (t + 1) * jrows, :] + mask_ref[c] for c in range(n_col)
        ]
        top = pieces[0]
        for piece in pieces[1:]:
            top = jnp.maximum(top, piece)
        top = over_parts(jnp.max(top, axis=0, keepdims=True), jnp.maximum)
        pieces = [jnp.exp(piece - top) for piece in pieces]
        total = pieces[0]
        for piece in pieces[1:]:
            total = total + piece
        inverse = 1.0 / over_parts(jnp.sum(total, axis=0, keepdims=True), jnp.add)
        weights.append([piece * inverse for piece in pieces])
    turned = []
    for t in range(0, len(taken), parts):
        blocks = []
        for c in range(n_col):
            for p in range(parts):
                block = None
                for q in range(parts):
                    value = weights[t + q][c]
                    shift = (q - p) % parts * wide
                    if shift:
                        value = pltpu.roll(value, shift, 1)
                    block = value if block is None else jnp.where(part_of == q, value, block)
                blocks.append(block)
        turned.append(jnp.concatenate(blocks, axis=0).T)
    mixed = dot_split(jnp.concatenate(turned, axis=0), norm_high, norm_low)
    count = len(taken) * here
    gated = []
    for h in range(heads):
        own = jnp.concatenate(
            [
                mixed[
                    t * wide + h * here : t * wide + (h + 1) * here,
                    g * group * width : (g + 1) * group * width,
                ]
                for g in range(groups)
                for t in range(len(taken))
            ],
            axis=0,
        )
        gate = jnp.concatenate([gate_ref[g, h, own_rows, :] for g in range(groups)], axis=0)
        gated.append(stacked_dot(own, value_bd[h]) * gate)
    out = None
    for hp in range(heads // 2):
        part = dot_split(
            jnp.concatenate(gated[2 * hp : 2 * hp + 2], axis=1),
            output_bd[0, hp],
            output_bd[1, hp],
        )
        out = part if out is None else out + part
    for g in range(groups):
        for s in range(group):
            at = g * group + s
            change = out[g * count : (g + 1) * count, s * width : (s + 1) * width]
            store(at, align_ref[at, own_rows, :] + change)


def average_kernel(
    here,
    early,
    slots,
    mask_ref,
    norm_high,
    norm_low,
    gate_ref,
    value_bd,
    output_bd,
    align_ref,
    early_ref,
    pair_ref,
    out_any,
    pair_any,
    out_buf,
    sems,
):
    rows = align_ref.shape[1]
    steps = rows // here
    first = early * here
    copies = [
        pltpu.make_async_copy(pair_ref, pair_any, sems.at[0]),
        pltpu.make_async_copy(early_ref, out_any.at[:, pl.ds(0, first), :], sems.at[1]),
        pltpu.make_async_copy(out_buf, out_any.at[:, pl.ds(first, rows - first), :], sems.at[2]),
    ]
    copies[0].start()
    copies[1].start()

    def keep(s, values):
        out_buf[s] = values

    average_rows(
        here,
        range(early, steps),
        slots,
        mask_ref,
        norm_high[...],
        norm_low[...],
        gate_ref,
        value_bd,
        output_bd,
        align_ref,
        keep,
    )
    copies[2].start()
    for copy in copies:
        copy.wait()


def per_device(
    n_row,
    n_col,
    alignment,
    pair_rep,
    seq_mask,
    res_mask,
    left_weight,
    right_weight,
    w_outer,
    w_logits,
    value_weight,
    gate_weight,
    output_weight,
):
    seqs, rows, width = alignment.shape
    cols, pair_width = pair_rep.shape[1], pair_rep.shape[2]
    factor = left_weight.shape[1]
    heads = w_logits.shape[1]
    channels = value_weight.shape[1]
    k_col = factor * seqs
    quarter = rows * seqs // 4
    half = n_row // 2
    here = 8
    steps = rows // here
    early = LANES // (here * heads)
    jrows = cols * here * heads // LANES
    group = LANES * heads // channels
    groups = seqs // group
    vmem = pl.BlockSpec(memory_space=pltpu.VMEM)
    anywhere = pl.BlockSpec(memory_space=pl.ANY)
    dma = pltpu.SemaphoreType.DMA
    left_shape = (quarter + 8, 4 * factor)
    right_shape = (rows, k_col)
    mix_row = (n_col, factor // 2, 2 * seqs, pair_width)
    row_bytes = 4 * n_col * k_col * pair_width
    premixed = rows * row_bytes <= MIX_BYTES
    held = rows if premixed else here
    pair_new, slots, mask, norm_high, norm_low, gate, value_bd, output_bd, align, started = pl.pallas_call(
        functools.partial(pair_kernel, n_row, n_col, here, early),
        out_shape=(
            pltpu.VMEM(pair_rep.shape, F32),
            pltpu.VMEM((n_col, steps * jrows, LANES), F32),
            pltpu.VMEM((n_col, jrows, LANES), F32),
            pltpu.VMEM((n_row, rows, seqs * width), BF16),
            pltpu.VMEM((n_row, rows, seqs * width), BF16),
            pltpu.VMEM((groups, heads, rows, LANES), F32),
            pltpu.VMEM((heads, group * width, 2 * LANES), BF16),
            pltpu.VMEM((2, heads // 2, 2 * LANES, group * width), BF16),
            pltpu.VMEM(alignment.shape, F32),
            pltpu.VMEM((seqs, early * here, width), F32),
        ),
        in_specs=[anywhere] * 11,
        out_specs=(vmem,) * 10,
        scratch_shapes=[
            pltpu.SMEM((seqs,), jnp.int32),
            pltpu.VMEM((1, rows), jnp.int32),
            pltpu.VMEM((factor, width), F32),
            pltpu.VMEM((factor, width), F32),
            pltpu.VMEM(w_outer.shape, F32),
            pltpu.VMEM((heads, pair_width), F32),
            pltpu.VMEM(value_weight.shape, F32),
            pltpu.VMEM(gate_weight.shape, F32),
            pltpu.VMEM((width, channels), F32),
            pltpu.VMEM((n_row, rows + 8, seqs * width), F32),
            pltpu.VMEM((rows * seqs, width), F32),
            pltpu.VMEM((rows, seqs * width), F32),
            pltpu.VMEM((k_col, seqs * width), F32),
            pltpu.VMEM((k_col, seqs * width), BF16),
            pltpu.VMEM((k_col, seqs * width), BF16),
            pltpu.VMEM(right_shape, F32),
            pltpu.VMEM((n_col,) + left_shape, F32),
            pltpu.VMEM((n_row,) + right_shape, F32),
            pltpu.VMEM((heads, group * width, 2 * LANES), BF16),
            pltpu.VMEM((here // 2, 2 * pair_width, 2 * LANES), BF16),
            pltpu.VMEM((3 * factor, factor * pair_width), BF16),
            pltpu.VMEM((1 if premixed else n_col, rows * seqs, 3 * factor), BF16),
            pltpu.VMEM((2 * cols, n_col * k_col), BF16),
            pltpu.VMEM((held,) + mix_row, BF16),
            pltpu.VMEM((held,) + mix_row, BF16),
            pltpu.VMEM(pair_rep.shape, F32),
            dma((11,)),
            dma((n_col,)),
            dma((n_col,)),
            dma((2,)),
            dma,
            dma((half - 1,)),
            dma,
            dma,
            dma((n_col,)),
            dma((2 * n_col + steps,)),
            dma,
            dma,
            dma,
            dma,
        ],
        compiler_params=pltpu.CompilerParams(
            collective_id=0, has_side_effects=True, vmem_limit_bytes=PAIR_VMEM
        ),
        name="pair",
    )(
        seq_mask,
        res_mask.reshape(1, rows),
        alignment,
        left_weight.T,
        right_weight.T,
        w_outer,
        w_logits.T,
        value_weight,
        gate_weight,
        output_weight.T,
        pair_rep,
    )
    alignment_out, pair_final = pl.pallas_call(
        functools.partial(average_kernel, here, early),
        out_shape=(
            jax.ShapeDtypeStruct(alignment.shape, F32),
            jax.ShapeDtypeStruct(pair_rep.shape, F32),
        ),
        in_specs=[vmem] * 10,
        out_specs=(anywhere, anywhere),
        scratch_shapes=[pltpu.VMEM((seqs, (steps - early) * here, width), F32), dma((3,))],
        compiler_params=pltpu.CompilerParams(vmem_limit_bytes=AVERAGE_VMEM),
        name="average",
    )(
        slots,
        mask,
        norm_high.reshape(n_row * rows, seqs * width),
        norm_low.reshape(n_row * rows, seqs * width),
        gate,
        value_bd,
        output_bd,
        align,
        started,
        pair_new,
    )
    return (alignment_out, pair_final)


def solution(mesh):
    in_specs = (P("col", "row", None), P("row", "col", None), P("col"), P("row")) + (P(),) * 7
    out_specs = (P("col", "row", None), P("row", "col", None))
    return jax.shard_map(
        functools.partial(per_device, mesh.shape["row"], mesh.shape["col"]),
        mesh=mesh,
        in_specs=in_specs,
        out_specs=out_specs,
        check_vma=False,
    )
```

```python
import functools

import jax
import jax.numpy as jnp
from jax import lax
from jax.experimental import pallas as pl
from jax.experimental.pallas import tpu as pltpu
from jax.sharding import PartitionSpec as P

MESH = pl.DeviceIdType.MESH
F32 = jnp.float32
BF16 = jnp.bfloat16
epsilon = 1e-05
PAIR_VMEM = 48 * 1024 * 1024
AVERAGE_VMEM = 24 * 1024 * 1024
MIX_BYTES = 30 * 1024 * 1024
LANES = 128


def layer_norm(values):
    center = jnp.mean(values, axis=-1, keepdims=True)
    centred = values - center
    return centred * lax.rsqrt(jnp.mean(centred * centred, axis=-1, keepdims=True) + epsilon)


def split(values):
    high = values.astype(BF16)
    return high, (values - high.astype(F32)).astype(BF16)


def dot(left, right):
    return jnp.dot(left, right, preferred_element_type=F32)


def dot_t(left, right):
    return lax.dot_general(left, right, (((1,), (1,)), ((), ())), preferred_element_type=F32)


def t_dot(left, right):
    return lax.dot_general(left, right, (((0,), (0,)), ((), ())), preferred_element_type=F32)


def dot_split(left, right_high, right_low, multiply=dot):
    high, low = split(left)
    return multiply(high, right_high) + (multiply(low, right_high) + multiply(high, right_low))


def iota(shape, axis):
    return lax.broadcasted_iota(jnp.int32, shape, axis)


def stacked_dot(values, weights):
    count, half = values.shape[0], weights.shape[1] // 2
    high, low = split(values)
    out = dot(jnp.concatenate([high, low], axis=0), weights)
    out = out[:, :half] + out[:, half:]
    return out[:count] + out[count:]


def spread_heads(weight, heads, group, store):
    width, channels = weight.shape
    head_width = channels // heads
    both = jnp.concatenate(split(weight), axis=0)
    rows, lanes = iota((channels, LANES), 0), iota((channels, LANES), 1)
    own = iota((group * width, LANES), 0) // width == iota((group * width, LANES), 1) // head_width
    for h in range(heads):
        pick = jnp.where(rows == h * head_width + lanes % head_width, 1.0, 0.0).astype(BF16)
        tiled = dot(both, pick)
        parts = []
        for t in range(2):
            piece = jnp.concatenate([tiled[t * width : (t + 1) * width]] * group, axis=0)
            parts.append(jnp.where(own, piece, 0.0))
        store(h, jnp.concatenate(parts, axis=1).astype(BF16))


def pair_kernel(
    n_row,
    n_col,
    here,
    early,
    seq_in,
    res_in,
    align_in,
    left_w_in,
    right_w_in,
    outer_in,
    logits_w_in,
    value_w_in,
    gate_w_in,
    output_w_in,
    pair_in,
    pair_out,
    slots,
    mask_out,
    norm_high,
    norm_low,
    gate_out,
    value_bd,
    output_bd,
    align_ref,
    early_out,
    seq_ref,
    res_ref,
    left_w_ref,
    right_w_ref,
    outer_ref,
    logits_w_ref,
    value_w_ref,
    gate_w_ref,
    output_w_ref,
    norm_all,
    rows_buf,
    masked_buf,
    block_buf,
    block_high,
    block_low,
    right_buf,
    left_ref,
    right_ref,
    gate_bd,
    wl_buf,
    w_buf,
    l_buf,
    r_buf,
    high_buf,
    low_buf,
    pair_ref,
    load_sem,
    left_send,
    left_recv,
    turn_sem,
    right_send,
    right_recv,
    share_send,
    share_recv,
    logits_send,
    logits_recv,
    norm_send,
    norm_recv,
    relay_send,
    relay_recv,
):
    row, col = lax.axis_index("row"), lax.axis_index("col")
    barrier = pltpu.get_barrier_semaphore()
    loads = [
        pltpu.make_async_copy(source, target, load_sem.at[at])
        for at, (source, target) in enumerate(
            [
                (right_w_in, right_w_ref),
                (res_in, res_ref),
                (left_w_in, left_w_ref),
                (seq_in, seq_ref),
                (align_in, align_ref),
                (outer_in, outer_ref),
                (gate_w_in, gate_w_ref),
                (value_w_in, value_w_ref),
                (logits_w_in, logits_w_ref),
                (output_w_in, output_w_ref),
                (pair_in, pair_ref),
            ]
        )
    ]
    for load in loads:
        load.start()

    seqs, rows, width = align_ref.shape
    factor = right_w_ref.shape[0]
    ratio, k_col = n_row // n_col, factor * seqs
    half = n_row // 2
    chip, core = row // 2, lax.rem(row, 2)
    partner = 2 * chip + 1 - core
    cols, pair_width = pair_out.shape[1], pair_out.shape[2]
    heads = logits_w_ref.shape[0]
    quarter = rows * seqs // 4
    steps = rows // here
    parts = LANES // (here * heads)
    jrows = cols // parts
    group = LANES * heads // value_w_ref.shape[1]
    premixed = high_buf.shape[0] == rows
    depth = n_col * k_col

    def peer_row(k):
        return 2 * lax.rem(chip + k, half) + core

    relayed = n_col >= 4
    at_high, at_low = col == n_col - 2, col == 1
    relay = at_high | at_low
    far_src = jnp.where(at_low, n_col - 1, 0)
    far_dest = jnp.where(at_low, 0, n_col - 1)

    def is_far(other):
        return (other - col == n_col - 1) | (col - other == n_col - 1)

    def near(other, action):
        if relayed:
            pl.when(jnp.logical_not(is_far(other)))(action)
        else:
            action()

    def unless_relayed(src, action):
        if relayed:
            pl.when(jnp.logical_not(relay & (src == far_src)))(action)
        else:
            action()

    dest = row // ratio
    spot = col * ratio + lax.rem(row, ratio)
    away = dest != col

    def meet(action):
        for k in range(1, n_col):
            other = lax.rem(col + k, n_col)
            near(other, functools.partial(action, row, other))
        for k in range(1, half):
            action(peer_row(k), col)
        action(partner, col)
        pl.when(away)(functools.partial(action, spot, dest))

    def greet(other_row, other_col):
        pl.semaphore_signal(
            barrier, inc=1, device_id=(other_row, other_col), device_id_type=MESH
        )

    greeters = half + n_col - 1 + jnp.where(away, 1, 0)
    if relayed:
        greeters = greeters - jnp.where((col == 0) | (col == n_col - 1), 1, 0)
    meet(greet)
    for at in range(4):
        loads[at].wait()
    res_row = res_ref[...].astype(F32)
    diag = iota((rows, rows), 0) == iota((rows, rows), 1)

    def column(values):
        return jnp.sum(
            jnp.where(diag, jnp.broadcast_to(values, (rows, rows)), 0.0), axis=1, keepdims=True
        )

    res_col = column(res_row)
    spread = jnp.broadcast_to(right_w_ref[...][:, None, :], (factor, seqs, width))
    row_seq = iota((factor, seqs, width), 1)
    for s in range(seqs):
        block_buf[:, s * width : (s + 1) * width] = jnp.where(row_seq == s, spread, 0.0).reshape(
            factor * seqs, width
        )
    wr_high, wr_low = split(block_buf[...])
    block_high[...] = wr_high
    block_low[...] = wr_low
    wl_high, wl_low = split(left_w_ref[...])
    norm_all[row, rows : rows + 8, 0:rows] = jnp.broadcast_to(res_row, (8, rows))
    norm_all[row, rows : rows + 8, rows:] = jnp.zeros((8, seqs * width - rows), F32)
    loads[4].wait()
    seq_sum = 0.0
    for s in range(seqs):
        normed = layer_norm(align_ref[s])
        norm_all[row, 0:rows, s * width : (s + 1) * width] = normed
        live = seq_ref[s].astype(F32)
        seq_sum = seq_sum + live
        masked_buf[:, s * width : (s + 1) * width] = normed * (res_col * live)
    right_buf[...] = dot_split(masked_buf[...], block_high[...], block_low[...], dot_t)
    pl.semaphore_wait(barrier, greeters)
    turn = pltpu.make_async_remote_copy(
        right_buf,
        right_ref.at[spot],
        turn_sem.at[0],
        turn_sem.at[1],
        device_id=(spot, dest),
        device_id_type=MESH,
    )
    stay = pltpu.make_async_copy(right_buf, right_ref.at[spot], turn_sem.at[1])

    @pl.when(away)
    def _():
        turn.start()

    @pl.when(jnp.logical_not(away))
    def _():
        stay.start()

    for s in range(seqs):
        rows_buf[pl.ds(s, rows, stride=seqs), :] = masked_buf[:, s * width : (s + 1) * width]
    left = dot_split(rows_buf[...], wl_high, wl_low, dot_t)
    for g in range(4):
        left_ref[col, 0:quarter, g * factor : (g + 1) * factor] = left[
            g * quarter : (g + 1) * quarter
        ]
    left_ref[col, quarter : quarter + 8, :] = jnp.full((8, left_ref.shape[2]), seq_sum, F32)

    def left_copy(k):
        return pltpu.make_async_remote_copy(
            left_ref.at[col],
            left_ref.at[col],
            left_send.at[k],
            left_recv.at[col],
            device_id=(row, lax.rem(col + k, n_col)),
            device_id_type=MESH,
        )

    def left_forward():
        return pltpu.make_async_remote_copy(
            left_ref.at[far_src],
            left_ref.at[far_src],
            left_send.at[0],
            left_recv.at[far_src],
            device_id=(row, far_dest),
            device_id_type=MESH,
        )

    def left_wait(src):
        pltpu.make_async_copy(left_ref.at[src], left_ref.at[src], left_recv.at[src]).wait()

    def right_copy(k):
        return pltpu.make_async_remote_copy(
            right_ref.at[row],
            right_ref.at[row],
            right_send,
            right_recv.at[half - k - 1],
            device_id=(peer_row(k), col),
            device_id_type=MESH,
        )

    def share_copy(k):
        src = peer_row(k)
        return pltpu.make_async_remote_copy(
            right_ref.at[src],
            right_ref.at[src],
            share_send,
            share_recv,
            device_id=(partner, col),
            device_id_type=MESH,
        )

    def norm_copy(k):
        return pltpu.make_async_remote_copy(
            norm_all.at[row],
            norm_all.at[row],
            norm_send,
            norm_recv,
            device_id=(peer_row(k), col),
            device_id_type=MESH,
        )

    def relay_copy(k):
        return pltpu.make_async_remote_copy(
            norm_all.at[peer_row(k)],
            norm_all.at[peer_row(k)],
            relay_send,
            relay_recv,
            device_id=(partner, col),
            device_id_type=MESH,
        )

    loads[5].wait()
    for b in range(factor):
        high, low = split(outer_ref[pl.ds(b, factor, stride=factor), :])
        lanes = slice(b * pair_width, (b + 1) * pair_width)
        w_buf[0:factor, lanes] = high
        w_buf[factor : 2 * factor, lanes] = low
        w_buf[2 * factor : 3 * factor, lanes] = high

    def left_rows(c, at):
        packed = left_ref[c, 0:quarter, :]
        high = packed.astype(BF16).astype(F32)
        low = packed - high
        for g in range(4):
            lanes = slice(g * factor, (g + 1) * factor)
            pieces = [high[:, lanes], high[:, lanes], low[:, lanes]]
            l_buf[at, g * quarter : (g + 1) * quarter, :] = jnp.concatenate(
                pieces, axis=1
            ).astype(BF16)

    def mix(l_rows, c, count):
        for nb in range(factor // 2):
            mixed = dot(l_rows, w_buf[:, nb * 2 * pair_width : (nb + 1) * 2 * pair_width])
            tiles = jnp.concatenate(
                [
                    mixed[:, :pair_width].reshape(count, seqs, pair_width),
                    mixed[:, pair_width:].reshape(count, seqs, pair_width),
                ],
                axis=1,
            )
            high, low = split(tiles)
            high_buf[:, c, nb] = high
            low_buf[:, c, nb] = low

    def prepare():
        for at in range(6, 11):
            loads[at].wait()

        def keep_value(h, block):
            value_bd[h] = block

        def keep_gate(h, block):
            gate_bd[h] = block

        spread_heads(gate_w_ref[...], heads, group, keep_gate)
        spread_heads(value_w_ref[...], heads, group, keep_value)
        groups = seqs // group
        own = jnp.concatenate(
            [
                norm_all[row, 0:rows, g * group * width : (g + 1) * group * width]
                for g in range(groups)
            ],
            axis=0,
        )
        for h in range(heads):
            gate = jax.nn.sigmoid(stacked_dot(own, gate_bd[h]))
            for g in range(groups):
                gate_out[g, h] = gate[g * rows : (g + 1) * rows]
        channels = output_w_ref.shape[1]
        head_width = channels // heads
        lanes = iota((width, group * width), 1)
        pick = jnp.where(iota((width, group * width), 0) == lanes % width, 1.0, 0.0).astype(BF16)
        own = (iota((2 * group * head_width, group * width), 0) // head_width) % group == iota(
            (2 * group * head_width, group * width), 1
        ) // width
        for t, half_w in enumerate(split(output_w_ref[...])):
            tiled = t_dot(half_w, pick)
            for hp in range(heads // 2):
                pieces = []
                for hh in range(2):
                    first = (2 * hp + hh) * head_width
                    pieces += [tiled[first : first + head_width]] * group
                output_bd[t, hp] = jnp.where(own, jnp.concatenate(pieces, axis=0), 0.0).astype(BF16)
        lanes = iota((heads, 2 * LANES), 1)
        low_half = iota((pair_width, 2 * LANES), 1) >= LANES
        w_high, w_low = split(logits_w_ref[...])
        for i in range(here):
            pick = jnp.where(
                ((lanes // here) % heads == iota((heads, 2 * LANES), 0)) & (lanes % here == i),
                1.0,
                0.0,
            ).astype(BF16)
            block = jnp.where(low_half, t_dot(w_low, pick), t_dot(w_high, pick))
            wl_buf[i // 2, (i % 2) * pair_width : (i % 2 + 1) * pair_width, :] = block.astype(BF16)

    low_end = col < (n_col + 1) // 2
    spot_in = jnp.where(low_end, col, n_col - 1 - col)

    def stage(k, carry):
        order = jnp.where(k - 1 < spot_in, k - 1, k)
        src = jnp.where(low_end, order, n_col - 1 - order)
        src = jnp.where(k == 0, col, src)

        @pl.when(k == 1)
        def _():
            for k2 in sorted(range(1, n_col), key=lambda d: min(d, n_col - d)):
                near(lax.rem(col + k2, n_col), left_copy(k2).start)
            prepare()
            pltpu.make_async_copy(right_buf, right_ref.at[row], turn_sem.at[1]).wait()
            odd = lax.rem(chip, 2)
            right_copy(half - 1 - odd * (half - 2)).start()
            right_copy(1 + odd * (half - 2)).start()
            for k2 in range(2, half - 1):
                right_copy(k2).start()
            share_copy(0).start()
            if relayed:

                @pl.when(relay)
                def _():
                    left_wait(far_src)
                    left_forward().start()

        @pl.when(k == n_col - 1)
        def _():
            for k2 in range(1, half):
                pltpu.make_async_copy(
                    right_buf, right_ref.at[peer_row(k2)], right_recv.at[k2 - 1]
                ).wait()
                share_copy(k2).start()

        @pl.when(k > 0)
        def _():
            unless_relayed(src, lambda: left_wait(src))

        at = 0 if premixed else src
        left_rows(src, at)
        if premixed:
            mix(l_buf[0], src, rows)
        return carry

    lax.fori_loop(0, n_col, stage, 0)
    def blocks(ref, number, sem):
        pltpu.make_async_copy(ref.at[pl.ds(0, number)], ref.at[pl.ds(0, number)], sem).wait()

    blocks(right_ref, half, share_recv)
    count = left_ref[0, quarter : quarter + 1, 0:1]
    for c in range(1, n_col):
        count = count + left_ref[c, quarter : quarter + 1, 0:1]
    scale = 1.0 / jnp.maximum(count, 1.0)
    for c in range(n_col):
        for t in range(ratio):
            high_r, low_r = split(right_ref[c * ratio + t])
            lanes = slice(c * k_col, (c + 1) * k_col)
            r_buf[t * rows : (t + 1) * rows, lanes] = high_r
            r_buf[cols + t * rows : cols + (t + 1) * rows, lanes] = low_r
    part_of = iota((jrows, LANES), 1) // (here * heads)

    def chunk(at):
        return pl.ds(pl.multiple_of(at * jrows, jrows), jrows)

    lag, direct = 2, 1
    first = steps - direct

    def logits_copy(k, at):
        other = lax.rem(col + k, n_col)
        sem = jnp.where(at < early, col, n_col + col)
        if relayed:
            passed = (at < first) & (
                ((col == 0) & (other == n_col - 2)) | ((col == n_col - 1) & (other == 1))
            )
            sem = jnp.where(passed, 2 * n_col + at, sem)
        return pltpu.make_async_remote_copy(
            slots.at[col, chunk(at)],
            slots.at[col, chunk(at)],
            logits_send.at[k],
            logits_recv.at[sem],
            device_id=(row, other),
            device_id_type=MESH,
        )

    def logits_forward(at):
        return pltpu.make_async_remote_copy(
            slots.at[far_src, chunk(at)],
            slots.at[far_src, chunk(at)],
            logits_send.at[0],
            logits_recv.at[jnp.where(at < early, far_src, n_col + far_src)],
            device_id=(row, far_dest),
            device_id_type=MESH,
        )

    def chunks(src, number, sem):
        part = slots.at[src, pl.ds(0, number * jrows)]
        pltpu.make_async_copy(part, part, sem).wait()

    def pass_on(at):
        @pl.when(relay)
        def _():
            chunks(far_src, 1, logits_recv.at[2 * n_col + at])
            logits_forward(at).start()

    def body(step, carry):
        first_row = pl.multiple_of(step * here, here)
        if not premixed:
            size = here * seqs
            for c in range(n_col):
                mix(l_buf[c, pl.ds(pl.multiple_of(step * size, size), size), :], c, here)
        r_both = r_buf[...]
        for p in range(here // 2):
            at = [2 * p + t + (first_row if premixed else 0) for t in range(2)]
            right_high = jnp.concatenate(
                [high_buf[i].reshape(depth, pair_width) for i in at], axis=1
            )
            right_low = jnp.concatenate([low_buf[i].reshape(depth, pair_width) for i in at], axis=1)
            product = dot(r_both, right_high)
            sums = product[:cols] + (product[cols:] + dot(r_both[:cols], right_low))
            for t in range(2):
                i = first_row + 2 * p + t
                pair_out[i] = pair_ref[i] + sums[:, t * pair_width : (t + 1) * pair_width] * scale
        total = None
        batch = here // 2
        for g in range(0, here, batch):
            pairs = pair_out[pl.ds(first_row + g, batch)].reshape(batch * cols, pair_width)
            high, low = split(layer_norm(pairs))
            for p in range(batch // 2):
                both = jnp.concatenate(
                    [
                        jnp.concatenate(
                            [
                                half_x[(2 * p + t) * cols : (2 * p + t + 1) * cols]
                                for t in range(2)
                            ],
                            axis=1,
                        )
                        for half_x in (high, low)
                    ],
                    axis=0,
                )
                out = dot(both, wl_buf[g // 2 + p])
                out = out[:, :LANES] + out[:, LANES:]
                out = out[:cols] + out[cols:]
                total = out if total is None else total + out
        logits = total[:jrows]
        for p in range(1, parts):
            logits = jnp.where(part_of == p, total[p * jrows : (p + 1) * jrows], logits)
        slots[col, chunk(step), :] = logits
        for k in range(1, n_col):
            other = lax.rem(col + k, n_col)
            if relayed:
                pl.when(jnp.logical_not(is_far(other)) | (step >= steps - direct))(
                    logits_copy(k, step).start
                )
            else:
                logits_copy(k, step).start()
        if relayed:

            @pl.when(step >= lag)
            def _():
                pass_on(step - lag)

        @pl.when(step == steps - 2)
        def _():
            blocks(norm_all, half - 1, norm_recv)
            for k in range(1, half):
                relay_copy(k).start()

        return carry

    relay_copy(0).start()
    for k in range(1, half):
        norm_copy(k).start()
    lax.fori_loop(0, steps, body, 0)
    if relayed:
        for at in range(steps - lag, first):
            pass_on(at)
    blocks(norm_all, half, relay_recv)
    for r in range(n_row):
        high, low = split(norm_all[r, 0:rows, :])
        norm_high[r] = high
        norm_low[r] = low
    for c in range(n_col):
        res_cols = jnp.concatenate(
            [column(norm_all[c * ratio + t, rows : rows + 1, 0:rows]) for t in range(ratio)],
            axis=0,
        )
        mask = jnp.zeros((jrows, LANES), F32)
        for p in range(parts):
            dead = (res_cols[p * jrows : (p + 1) * jrows] - 1.0) * 1000000000.0
            mask = jnp.where(part_of == p, dead, mask)
        mask_out[c] = mask
    for k in range(1, n_col):
        other = lax.rem(col + k, n_col)
        unless_relayed(other, lambda: chunks(other, early, logits_recv.at[other]))

    def keep(s, values):
        early_out[s] = values

    average_rows(
        here,
        range(early),
        slots,
        mask_out,
        norm_high[...].reshape(n_row * rows, seqs * width),
        norm_low[...].reshape(n_row * rows, seqs * width),
        gate_out,
        value_bd,
        output_bd,
        align_ref,
        keep,
    )
    blocks(right_ref, half, share_send)
    blocks(right_ref, half - 1, right_send)
    for k in range(1, n_col):
        near(lax.rem(col + k, n_col), left_copy(k).wait_send)

    @pl.when(away)
    def _():
        turn.wait_send()

    if relayed:

        @pl.when(relay)
        def _():
            left_forward().wait_send()
            chunks(far_src, first, logits_send.at[0])

    blocks(norm_all, half - 1, norm_send)
    blocks(norm_all, half, relay_send)
    for k in range(1, n_col):
        other = lax.rem(col + k, n_col)
        if relayed:
            near(other, lambda: chunks(col, steps, logits_send.at[k]))
            pl.when(is_far(other))(lambda: chunks(col, direct, logits_send.at[k]))
        else:
            chunks(col, steps, logits_send.at[k])
        last = logits_recv.at[n_col + other]
        unless_relayed(other, lambda: chunks(other, steps - early, last))
        if relayed:
            pl.when(relay & (other == far_src))(lambda: chunks(other, direct, last))


def average_rows(
    here, taken, slots, mask_ref, norm_high, norm_low, gate_ref, value_bd, output_bd, align_ref, store
):
    seqs, rows, width = align_ref.shape
    n_col, total_rows, _ = slots.shape
    groups, heads = gate_ref.shape[0], gate_ref.shape[1]
    group = seqs // groups
    jrows = total_rows // (rows // here)
    wide = here * heads
    parts = LANES // wide
    own_rows = slice(taken[0] * here, (taken[-1] + 1) * here)
    part_of = iota((jrows, LANES), 1) // wide

    def over_parts(values, combine):
        out = values
        for p in range(1, parts):
            out = combine(out, pltpu.roll(values, p * wide, 1))
        return out

    weights = []
    for t in taken:
        pieces = [
            slots[c, t * jrows : (t + 1) * jrows, :] + mask_ref[c] for c in range(n_col)
        ]
        top = pieces[0]
        for piece in pieces[1:]:
            top = jnp.maximum(top, piece)
        top = over_parts(jnp.max(top, axis=0, keepdims=True), jnp.maximum)
        pieces = [jnp.exp(piece - top) for piece in pieces]
        total = pieces[0]
        for piece in pieces[1:]:
            total = total + piece
        inverse = 1.0 / over_parts(jnp.sum(total, axis=0, keepdims=True), jnp.add)
        weights.append([piece * inverse for piece in pieces])
    turned = []
    for t in range(0, len(taken), parts):
        blocks = []
        for c in range(n_col):
            for p in range(parts):
                block = None
                for q in range(parts):
                    value = weights[t + q][c]
                    shift = (q - p) % parts * wide
                    if shift:
                        value = pltpu.roll(value, shift, 1)
                    block = value if block is None else jnp.where(part_of == q, value, block)
                blocks.append(block)
        turned.append(jnp.concatenate(blocks, axis=0).T)
    mixed = dot_split(jnp.concatenate(turned, axis=0), norm_high, norm_low)
    count = len(taken) * here
    gated = []
    for h in range(heads):
        own = jnp.concatenate(
            [
                mixed[
                    t * wide + h * here : t * wide + (h + 1) * here,
                    g * group * width : (g + 1) * group * width,
                ]
                for g in range(groups)
                for t in range(len(taken))
            ],
            axis=0,
        )
        gate = jnp.concatenate([gate_ref[g, h, own_rows, :] for g in range(groups)], axis=0)
        gated.append(stacked_dot(own, value_bd[h]) * gate)
    out = None
    for hp in range(heads // 2):
        part = dot_split(
            jnp.concatenate(gated[2 * hp : 2 * hp + 2], axis=1),
            output_bd[0, hp],
            output_bd[1, hp],
        )
        out = part if out is None else out + part
    for g in range(groups):
        for s in range(group):
            at = g * group + s
            change = out[g * count : (g + 1) * count, s * width : (s + 1) * width]
            store(at, align_ref[at, own_rows, :] + change)


def average_kernel(
    here,
    early,
    slots,
    mask_ref,
    norm_high,
    norm_low,
    gate_ref,
    value_bd,
    output_bd,
    align_ref,
    early_ref,
    pair_ref,
    out_any,
    pair_any,
    out_buf,
    sems,
):
    rows = align_ref.shape[1]
    steps = rows // here
    first = early * here
    copies = [
        pltpu.make_async_copy(pair_ref, pair_any, sems.at[0]),
        pltpu.make_async_copy(early_ref, out_any.at[:, pl.ds(0, first), :], sems.at[1]),
        pltpu.make_async_copy(out_buf, out_any.at[:, pl.ds(first, rows - first), :], sems.at[2]),
    ]
    copies[0].start()
    copies[1].start()

    def keep(s, values):
        out_buf[s] = values

    average_rows(
        here,
        range(early, steps),
        slots,
        mask_ref,
        norm_high[...],
        norm_low[...],
        gate_ref,
        value_bd,
        output_bd,
        align_ref,
        keep,
    )
    copies[2].start()
    for copy in copies:
        copy.wait()


def per_device(
    n_row,
    n_col,
    alignment,
    pair_rep,
    seq_mask,
    res_mask,
    left_weight,
    right_weight,
    w_outer,
    w_logits,
    value_weight,
    gate_weight,
    output_weight,
):
    seqs, rows, width = alignment.shape
    cols, pair_width = pair_rep.shape[1], pair_rep.shape[2]
    factor = left_weight.shape[1]
    heads = w_logits.shape[1]
    channels = value_weight.shape[1]
    k_col = factor * seqs
    quarter = rows * seqs // 4
    half = n_row // 2
    here = 8
    steps = rows // here
    early = LANES // (here * heads)
    jrows = cols * here * heads // LANES
    group = LANES * heads // channels
    groups = seqs // group
    vmem = pl.BlockSpec(memory_space=pltpu.VMEM)
    anywhere = pl.BlockSpec(memory_space=pl.ANY)
    dma = pltpu.SemaphoreType.DMA
    left_shape = (quarter + 8, 4 * factor)
    right_shape = (rows, k_col)
    mix_row = (n_col, factor // 2, 2 * seqs, pair_width)
    row_bytes = 4 * n_col * k_col * pair_width
    premixed = rows * row_bytes <= MIX_BYTES
    held = rows if premixed else here
    pair_new, slots, mask, norm_high, norm_low, gate, value_bd, output_bd, align, started = pl.pallas_call(
        functools.partial(pair_kernel, n_row, n_col, here, early),
        out_shape=(
            pltpu.VMEM(pair_rep.shape, F32),
            pltpu.VMEM((n_col, steps * jrows, LANES), F32),
            pltpu.VMEM((n_col, jrows, LANES), F32),
            pltpu.VMEM((n_row, rows, seqs * width), BF16),
            pltpu.VMEM((n_row, rows, seqs * width), BF16),
            pltpu.VMEM((groups, heads, rows, LANES), F32),
            pltpu.VMEM((heads, group * width, 2 * LANES), BF16),
            pltpu.VMEM((2, heads // 2, 2 * LANES, group * width), BF16),
            pltpu.VMEM(alignment.shape, F32),
            pltpu.VMEM((seqs, early * here, width), F32),
        ),
        in_specs=[anywhere] * 11,
        out_specs=(vmem,) * 10,
        scratch_shapes=[
            pltpu.SMEM((seqs,), jnp.int32),
            pltpu.VMEM((1, rows), jnp.int32),
            pltpu.VMEM((factor, width), F32),
            pltpu.VMEM((factor, width), F32),
            pltpu.VMEM(w_outer.shape, F32),
            pltpu.VMEM((heads, pair_width), F32),
            pltpu.VMEM(value_weight.shape, F32),
            pltpu.VMEM(gate_weight.shape, F32),
            pltpu.VMEM((width, channels), F32),
            pltpu.VMEM((n_row, rows + 8, seqs * width), F32),
            pltpu.VMEM((rows * seqs, width), F32),
            pltpu.VMEM((rows, seqs * width), F32),
            pltpu.VMEM((k_col, seqs * width), F32),
            pltpu.VMEM((k_col, seqs * width), BF16),
            pltpu.VMEM((k_col, seqs * width), BF16),
            pltpu.VMEM(right_shape, F32),
            pltpu.VMEM((n_col,) + left_shape, F32),
            pltpu.VMEM((n_row,) + right_shape, F32),
            pltpu.VMEM((heads, group * width, 2 * LANES), BF16),
            pltpu.VMEM((here // 2, 2 * pair_width, 2 * LANES), BF16),
            pltpu.VMEM((3 * factor, factor * pair_width), BF16),
            pltpu.VMEM((1 if premixed else n_col, rows * seqs, 3 * factor), BF16),
            pltpu.VMEM((2 * cols, n_col * k_col), BF16),
            pltpu.VMEM((held,) + mix_row, BF16),
            pltpu.VMEM((held,) + mix_row, BF16),
            pltpu.VMEM(pair_rep.shape, F32),
            dma((11,)),
            dma((n_col,)),
            dma((n_col,)),
            dma((2,)),
            dma,
            dma((half - 1,)),
            dma,
            dma,
            dma((n_col,)),
            dma((2 * n_col + steps,)),
            dma,
            dma,
            dma,
            dma,
        ],
        compiler_params=pltpu.CompilerParams(
            collective_id=0, has_side_effects=True, vmem_limit_bytes=PAIR_VMEM
        ),
        name="pair",
    )(
        seq_mask,
        res_mask.reshape(1, rows),
        alignment,
        left_weight.T,
        right_weight.T,
        w_outer,
        w_logits.T,
        value_weight,
        gate_weight,
        output_weight.T,
        pair_rep,
    )
    alignment_out, pair_final = pl.pallas_call(
        functools.partial(average_kernel, here, early),
        out_shape=(
            jax.ShapeDtypeStruct(alignment.shape, F32),
            jax.ShapeDtypeStruct(pair_rep.shape, F32),
        ),
        in_specs=[vmem] * 10,
        out_specs=(anywhere, anywhere),
        scratch_shapes=[pltpu.VMEM((seqs, (steps - early) * here, width), F32), dma((3,))],
        compiler_params=pltpu.CompilerParams(vmem_limit_bytes=AVERAGE_VMEM),
        name="average",
    )(
        slots,
        mask,
        norm_high.reshape(n_row * rows, seqs * width),
        norm_low.reshape(n_row * rows, seqs * width),
        gate,
        value_bd,
        output_bd,
        align,
        started,
        pair_new,
    )
    return (alignment_out, pair_final)


def solution(mesh):
    in_specs = (P("col", "row", None), P("row", "col", None), P("col"), P("row")) + (P(),) * 7
    out_specs = (P("col", "row", None), P("row", "col", None))
    return jax.shard_map(
        functools.partial(per_device, mesh.shape["row"], mesh.shape["col"]),
        mesh=mesh,
        in_specs=in_specs,
        out_specs=out_specs,
        check_vma=False,
    )
```

```python
import functools

import jax
import jax.numpy as jnp
from jax import lax
from jax.experimental import pallas as pl
from jax.experimental.pallas import tpu as pltpu
from jax.sharding import PartitionSpec as P

MESH = pl.DeviceIdType.MESH
F32 = jnp.float32
BF16 = jnp.bfloat16
epsilon = 1e-05
PAIR_VMEM = 48 * 1024 * 1024
AVERAGE_VMEM = 24 * 1024 * 1024
MIX_BYTES = 30 * 1024 * 1024
LANES = 128


def layer_norm(values):
    center = jnp.mean(values, axis=-1, keepdims=True)
    centred = values - center
    return centred * lax.rsqrt(jnp.mean(centred * centred, axis=-1, keepdims=True) + epsilon)


def split(values):
    high = values.astype(BF16)
    return high, (values - high.astype(F32)).astype(BF16)


def dot(left, right):
    return jnp.dot(left, right, preferred_element_type=F32)


def dot_t(left, right):
    return lax.dot_general(left, right, (((1,), (1,)), ((), ())), preferred_element_type=F32)


def t_dot(left, right):
    return lax.dot_general(left, right, (((0,), (0,)), ((), ())), preferred_element_type=F32)


def dot_split(left, right_high, right_low, multiply=dot):
    count = left.shape[0]
    high, low = split(left)
    both = multiply(jnp.concatenate([high, low], axis=0), right_high)
    return both[:count] + (both[count:] + multiply(high, right_low))


def iota(shape, axis):
    return lax.broadcasted_iota(jnp.int32, shape, axis)


def stacked_dot(values, weights):
    count, half = values.shape[0], weights.shape[1] // 2
    high, low = split(values)
    out = dot(jnp.concatenate([high, low], axis=0), weights)
    out = out[:, :half] + out[:, half:]
    return out[:count] + out[count:]


def spread_heads(weight, heads, group, store):
    width, channels = weight.shape
    head_width = channels // heads
    both = jnp.concatenate(split(weight), axis=0)
    rows, lanes = iota((channels, LANES), 0), iota((channels, LANES), 1)
    own = iota((group * width, LANES), 0) // width == iota((group * width, LANES), 1) // head_width
    for h in range(heads):
        pick = jnp.where(rows == h * head_width + lanes % head_width, 1.0, 0.0).astype(BF16)
        tiled = dot(both, pick)
        parts = []
        for t in range(2):
            piece = jnp.concatenate([tiled[t * width : (t + 1) * width]] * group, axis=0)
            parts.append(jnp.where(own, piece, 0.0))
        store(h, jnp.concatenate(parts, axis=1).astype(BF16))


def pair_kernel(
    n_row,
    n_col,
    here,
    early,
    seq_in,
    res_in,
    align_in,
    left_w_in,
    right_w_in,
    outer_in,
    logits_w_in,
    value_w_in,
    gate_w_in,
    output_w_in,
    pair_in,
    pair_out,
    slots,
    mask_out,
    norm_high,
    norm_low,
    gate_out,
    value_bd,
    output_bd,
    align_ref,
    early_out,
    seq_ref,
    res_ref,
    left_w_ref,
    right_w_ref,
    outer_ref,
    logits_w_ref,
    value_w_ref,
    gate_w_ref,
    output_w_ref,
    norm_all,
    rows_buf,
    masked_buf,
    block_buf,
    block_high,
    block_low,
    right_buf,
    left_ref,
    right_ref,
    gate_bd,
    wl_buf,
    w_buf,
    l_buf,
    r_buf,
    high_buf,
    low_buf,
    pair_ref,
    load_sem,
    left_send,
    left_recv,
    turn_sem,
    right_send,
    right_recv,
    share_send,
    share_recv,
    logits_send,
    logits_recv,
    norm_send,
    norm_recv,
    relay_send,
    relay_recv,
):
    row, col = lax.axis_index("row"), lax.axis_index("col")
    barrier = pltpu.get_barrier_semaphore()
    loads = [
        pltpu.make_async_copy(source, target, load_sem.at[at])
        for at, (source, target) in enumerate(
            [
                (right_w_in, right_w_ref),
                (res_in, res_ref),
                (left_w_in, left_w_ref),
                (seq_in, seq_ref),
                (align_in, align_ref),
                (outer_in, outer_ref),
                (gate_w_in, gate_w_ref),
                (value_w_in, value_w_ref),
                (logits_w_in, logits_w_ref),
                (output_w_in, output_w_ref),
                (pair_in, pair_ref),
            ]
        )
    ]
    for load in loads:
        load.start()

    seqs, rows, width = align_ref.shape
    factor = right_w_ref.shape[0]
    ratio, k_col = n_row // n_col, factor * seqs
    half = n_row // 2
    chip, core = row // 2, lax.rem(row, 2)
    partner = 2 * chip + 1 - core
    cols, pair_width = pair_out.shape[1], pair_out.shape[2]
    heads = logits_w_ref.shape[0]
    quarter = rows * seqs // 4
    steps = rows // here
    parts = LANES // (here * heads)
    jrows = cols // parts
    group = LANES * heads // value_w_ref.shape[1]
    premixed = high_buf.shape[0] == rows
    depth = n_col * k_col

    def peer_row(k):
        return 2 * lax.rem(chip + k, half) + core

    relayed = n_col >= 4
    at_high, at_low = col == n_col - 2, col == 1
    relay = at_high | at_low
    far_src = jnp.where(at_low, n_col - 1, 0)
    far_dest = jnp.where(at_low, 0, n_col - 1)

    def is_far(other):
        return (other - col == n_col - 1) | (col - other == n_col - 1)

    def near(other, action):
        if relayed:
            pl.when(jnp.logical_not(is_far(other)))(action)
        else:
            action()

    def unless_relayed(src, action):
        if relayed:
            pl.when(jnp.logical_not(relay & (src == far_src)))(action)
        else:
            action()

    dest = row // ratio
    spot = col * ratio + lax.rem(row, ratio)
    away = dest != col

    def meet(action):
        for k in range(1, n_col):
            other = lax.rem(col + k, n_col)
            near(other, functools.partial(action, row, other))
        for k in range(1, half):
            action(peer_row(k), col)
        action(partner, col)
        pl.when(away)(functools.partial(action, spot, dest))

    def greet(other_row, other_col):
        pl.semaphore_signal(
            barrier, inc=1, device_id=(other_row, other_col), device_id_type=MESH
        )

    greeters = half + n_col - 1 + jnp.where(away, 1, 0)
    if relayed:
        greeters = greeters - jnp.where((col == 0) | (col == n_col - 1), 1, 0)
    meet(greet)
    for at in range(4):
        loads[at].wait()
    res_row = res_ref[...].astype(F32)
    diag = iota((rows, rows), 0) == iota((rows, rows), 1)

    def column(values):
        return jnp.sum(
            jnp.where(diag, jnp.broadcast_to(values, (rows, rows)), 0.0), axis=1, keepdims=True
        )

    res_col = column(res_row)
    spread = jnp.broadcast_to(right_w_ref[...][:, None, :], (factor, seqs, width))
    row_seq = iota((factor, seqs, width), 1)
    for s in range(seqs):
        block_buf[:, s * width : (s + 1) * width] = jnp.where(row_seq == s, spread, 0.0).reshape(
            factor * seqs, width
        )
    wr_high, wr_low = split(block_buf[...])
    block_high[...] = wr_high
    block_low[...] = wr_low
    wl_high, wl_low = split(left_w_ref[...])
    norm_all[row, rows : rows + 8, 0:rows] = jnp.broadcast_to(res_row, (8, rows))
    norm_all[row, rows : rows + 8, rows:] = jnp.zeros((8, seqs * width - rows), F32)
    loads[4].wait()
    seq_sum = 0.0
    for s in range(seqs):
        normed = layer_norm(align_ref[s])
        norm_all[row, 0:rows, s * width : (s + 1) * width] = normed
        live = seq_ref[s].astype(F32)
        seq_sum = seq_sum + live
        masked_buf[:, s * width : (s + 1) * width] = normed * (res_col * live)
    right_buf[...] = dot_split(masked_buf[...], block_high[...], block_low[...], dot_t)
    pl.semaphore_wait(barrier, greeters)
    turn = pltpu.make_async_remote_copy(
        right_buf,
        right_ref.at[spot],
        turn_sem.at[0],
        turn_sem.at[1],
        device_id=(spot, dest),
        device_id_type=MESH,
    )
    stay = pltpu.make_async_copy(right_buf, right_ref.at[spot], turn_sem.at[1])

    @pl.when(away)
    def _():
        turn.start()

    @pl.when(jnp.logical_not(away))
    def _():
        stay.start()

    for s in range(seqs):
        rows_buf[pl.ds(s, rows, stride=seqs), :] = masked_buf[:, s * width : (s + 1) * width]
    left = dot_split(rows_buf[...], wl_high, wl_low, dot_t)
    for g in range(4):
        left_ref[col, 0:quarter, g * factor : (g + 1) * factor] = left[
            g * quarter : (g + 1) * quarter
        ]
    left_ref[col, quarter : quarter + 8, :] = jnp.full((8, left_ref.shape[2]), seq_sum, F32)

    def left_copy(k):
        return pltpu.make_async_remote_copy(
            left_ref.at[col],
            left_ref.at[col],
            left_send.at[k],
            left_recv.at[col],
            device_id=(row, lax.rem(col + k, n_col)),
            device_id_type=MESH,
        )

    def left_forward():
        return pltpu.make_async_remote_copy(
            left_ref.at[far_src],
            left_ref.at[far_src],
            left_send.at[0],
            left_recv.at[far_src],
            device_id=(row, far_dest),
            device_id_type=MESH,
        )

    def left_wait(src):
        pltpu.make_async_copy(left_ref.at[src], left_ref.at[src], left_recv.at[src]).wait()

    def right_copy(k):
        return pltpu.make_async_remote_copy(
            right_ref.at[row],
            right_ref.at[row],
            right_send,
            right_recv.at[half - k - 1],
            device_id=(peer_row(k), col),
            device_id_type=MESH,
        )

    def share_copy(k):
        src = peer_row(k)
        return pltpu.make_async_remote_copy(
            right_ref.at[src],
            right_ref.at[src],
            share_send,
            share_recv,
            device_id=(partner, col),
            device_id_type=MESH,
        )

    def norm_copy(k):
        return pltpu.make_async_remote_copy(
            norm_all.at[row],
            norm_all.at[row],
            norm_send,
            norm_recv,
            device_id=(peer_row(k), col),
            device_id_type=MESH,
        )

    def relay_copy(k):
        return pltpu.make_async_remote_copy(
            norm_all.at[peer_row(k)],
            norm_all.at[peer_row(k)],
            relay_send,
            relay_recv,
            device_id=(partner, col),
            device_id_type=MESH,
        )

    loads[5].wait()
    for b in range(factor):
        high, low = split(outer_ref[pl.ds(b, factor, stride=factor), :])
        lanes = slice(b * pair_width, (b + 1) * pair_width)
        w_buf[0:factor, lanes] = high
        w_buf[factor : 2 * factor, lanes] = low
        w_buf[2 * factor : 3 * factor, lanes] = high

    def left_rows(c, at):
        packed = left_ref[c, 0:quarter, :]
        high = packed.astype(BF16).astype(F32)
        low = packed - high
        for g in range(4):
            lanes = slice(g * factor, (g + 1) * factor)
            pieces = [high[:, lanes], high[:, lanes], low[:, lanes]]
            l_buf[at, g * quarter : (g + 1) * quarter, :] = jnp.concatenate(
                pieces, axis=1
            ).astype(BF16)

    def mix(l_rows, c, count):
        for nb in range(factor // 2):
            mixed = dot(l_rows, w_buf[:, nb * 2 * pair_width : (nb + 1) * 2 * pair_width])
            tiles = jnp.concatenate(
                [
                    mixed[:, :pair_width].reshape(count, seqs, pair_width),
                    mixed[:, pair_width:].reshape(count, seqs, pair_width),
                ],
                axis=1,
            )
            high, low = split(tiles)
            high_buf[:, c, nb] = high
            low_buf[:, c, nb] = low

    def prepare():
        for at in range(6, 11):
            loads[at].wait()

        def keep_value(h, block):
            value_bd[h] = block

        def keep_gate(h, block):
            gate_bd[h] = block

        spread_heads(gate_w_ref[...], heads, group, keep_gate)
        spread_heads(value_w_ref[...], heads, group, keep_value)
        groups = seqs // group
        own = jnp.concatenate(
            [
                norm_all[row, 0:rows, g * group * width : (g + 1) * group * width]
                for g in range(groups)
            ],
            axis=0,
        )
        for h in range(heads):
            gate = jax.nn.sigmoid(stacked_dot(own, gate_bd[h]))
            for g in range(groups):
                gate_out[g, h] = gate[g * rows : (g + 1) * rows]
        channels = output_w_ref.shape[1]
        head_width = channels // heads
        lanes = iota((width, group * width), 1)
        pick = jnp.where(iota((width, group * width), 0) == lanes % width, 1.0, 0.0).astype(BF16)
        own = (iota((2 * group * head_width, group * width), 0) // head_width) % group == iota(
            (2 * group * head_width, group * width), 1
        ) // width
        for t, half_w in enumerate(split(output_w_ref[...])):
            tiled = t_dot(half_w, pick)
            for hp in range(heads // 2):
                pieces = []
                for hh in range(2):
                    first = (2 * hp + hh) * head_width
                    pieces += [tiled[first : first + head_width]] * group
                output_bd[t, hp] = jnp.where(own, jnp.concatenate(pieces, axis=0), 0.0).astype(BF16)
        lanes = iota((heads, 2 * LANES), 1)
        low_half = iota((pair_width, 2 * LANES), 1) >= LANES
        w_high, w_low = split(logits_w_ref[...])
        for i in range(here):
            pick = jnp.where(
                ((lanes // here) % heads == iota((heads, 2 * LANES), 0)) & (lanes % here == i),
                1.0,
                0.0,
            ).astype(BF16)
            block = jnp.where(low_half, t_dot(w_low, pick), t_dot(w_high, pick))
            wl_buf[i // 2, (i % 2) * pair_width : (i % 2 + 1) * pair_width, :] = block.astype(BF16)

    low_end = col < (n_col + 1) // 2
    spot_in = jnp.where(low_end, col, n_col - 1 - col)

    def stage(k, carry):
        order = jnp.where(k - 1 < spot_in, k - 1, k)
        src = jnp.where(low_end, order, n_col - 1 - order)
        src = jnp.where(k == 0, col, src)

        @pl.when(k == 1)
        def _():
            for k2 in sorted(range(1, n_col), key=lambda d: min(d, n_col - d)):
                near(lax.rem(col + k2, n_col), left_copy(k2).start)
            prepare()
            pltpu.make_async_copy(right_buf, right_ref.at[row], turn_sem.at[1]).wait()
            odd = lax.rem(chip, 2)
            right_copy(half - 1 - odd * (half - 2)).start()
            right_copy(1 + odd * (half - 2)).start()
            for k2 in range(2, half - 1):
                right_copy(k2).start()
            share_copy(0).start()
            if relayed:

                @pl.when(relay)
                def _():
                    left_wait(far_src)
                    left_forward().start()

        @pl.when(k == n_col - 1)
        def _():
            for k2 in range(1, half):
                pltpu.make_async_copy(
                    right_buf, right_ref.at[peer_row(k2)], right_recv.at[k2 - 1]
                ).wait()
                share_copy(k2).start()

        @pl.when(k > 0)
        def _():
            unless_relayed(src, lambda: left_wait(src))

        at = 0 if premixed else src
        left_rows(src, at)
        if premixed:
            mix(l_buf[0], src, rows)
        return carry

    lax.fori_loop(0, n_col, stage, 0)
    def blocks(ref, number, sem):
        pltpu.make_async_copy(ref.at[pl.ds(0, number)], ref.at[pl.ds(0, number)], sem).wait()

    blocks(right_ref, half, share_recv)
    count = left_ref[0, quarter : quarter + 1, 0:1]
    for c in range(1, n_col):
        count = count + left_ref[c, quarter : quarter + 1, 0:1]
    scale = 1.0 / jnp.maximum(count, 1.0)
    for c in range(n_col):
        for t in range(ratio):
            high_r, low_r = split(right_ref[c * ratio + t])
            lanes = slice(c * k_col, (c + 1) * k_col)
            r_buf[t * rows : (t + 1) * rows, lanes] = high_r
            r_buf[cols + t * rows : cols + (t + 1) * rows, lanes] = low_r
    part_of = iota((jrows, LANES), 1) // (here * heads)

    def chunk(at):
        return pl.ds(pl.multiple_of(at * jrows, jrows), jrows)

    lag, direct = 2, 1
    first = steps - direct

    def logits_copy(k, at):
        other = lax.rem(col + k, n_col)
        sem = jnp.where(at < early, col, n_col + col)
        if relayed:
            passed = (at < first) & (
                ((col == 0) & (other == n_col - 2)) | ((col == n_col - 1) & (other == 1))
            )
            sem = jnp.where(passed, 2 * n_col + at, sem)
        return pltpu.make_async_remote_copy(
            slots.at[col, chunk(at)],
            slots.at[col, chunk(at)],
            logits_send.at[k],
            logits_recv.at[sem],
            device_id=(row, other),
            device_id_type=MESH,
        )

    def logits_forward(at):
        return pltpu.make_async_remote_copy(
            slots.at[far_src, chunk(at)],
            slots.at[far_src, chunk(at)],
            logits_send.at[0],
            logits_recv.at[jnp.where(at < early, far_src, n_col + far_src)],
            device_id=(row, far_dest),
            device_id_type=MESH,
        )

    def chunks(src, number, sem):
        part = slots.at[src, pl.ds(0, number * jrows)]
        pltpu.make_async_copy(part, part, sem).wait()

    def pass_on(at):
        @pl.when(relay)
        def _():
            chunks(far_src, 1, logits_recv.at[2 * n_col + at])
            logits_forward(at).start()

    def body(step, carry):
        first_row = pl.multiple_of(step * here, here)
        if not premixed:
            size = here * seqs
            for c in range(n_col):
                mix(l_buf[c, pl.ds(pl.multiple_of(step * size, size), size), :], c, here)
        r_both = r_buf[...]
        for p in range(here // 2):
            at = [2 * p + t + (first_row if premixed else 0) for t in range(2)]
            right_high = jnp.concatenate(
                [high_buf[i].reshape(depth, pair_width) for i in at], axis=1
            )
            right_low = jnp.concatenate([low_buf[i].reshape(depth, pair_width) for i in at], axis=1)
            product = dot(r_both, right_high)
            sums = product[:cols] + (product[cols:] + dot(r_both[:cols], right_low))
            for t in range(2):
                i = first_row + 2 * p + t
                pair_out[i] = pair_ref[i] + sums[:, t * pair_width : (t + 1) * pair_width] * scale
        total = None
        batch = here // 2
        for g in range(0, here, batch):
            pairs = pair_out[pl.ds(first_row + g, batch)].reshape(batch * cols, pair_width)
            high, low = split(layer_norm(pairs))
            for p in range(batch // 2):
                both = jnp.concatenate(
                    [
                        jnp.concatenate(
                            [
                                half_x[(2 * p + t) * cols : (2 * p + t + 1) * cols]
                                for t in range(2)
                            ],
                            axis=1,
                        )
                        for half_x in (high, low)
                    ],
                    axis=0,
                )
                out = dot(both, wl_buf[g // 2 + p])
                out = out[:, :LANES] + out[:, LANES:]
                out = out[:cols] + out[cols:]
                total = out if total is None else total + out
        logits = total[:jrows]
        for p in range(1, parts):
            logits = jnp.where(part_of == p, total[p * jrows : (p + 1) * jrows], logits)
        slots[col, chunk(step), :] = logits
        for k in range(1, n_col):
            other = lax.rem(col + k, n_col)
            if relayed:
                pl.when(jnp.logical_not(is_far(other)) | (step >= steps - direct))(
                    logits_copy(k, step).start
                )
            else:
                logits_copy(k, step).start()
        if relayed:

            @pl.when(step >= lag)
            def _():
                pass_on(step - lag)

        @pl.when(step == steps - 2)
        def _():
            blocks(norm_all, half - 1, norm_recv)
            for k in range(1, half):
                relay_copy(k).start()

        return carry

    relay_copy(0).start()
    for k in range(1, half):
        norm_copy(k).start()
    lax.fori_loop(0, steps, body, 0)
    if relayed:
        for at in range(steps - lag, first):
            pass_on(at)
    blocks(norm_all, half, relay_recv)
    for r in range(n_row):
        high, low = split(norm_all[r, 0:rows, :])
        norm_high[r] = high
        norm_low[r] = low
    for c in range(n_col):
        res_cols = jnp.concatenate(
            [column(norm_all[c * ratio + t, rows : rows + 1, 0:rows]) for t in range(ratio)],
            axis=0,
        )
        mask = jnp.zeros((jrows, LANES), F32)
        for p in range(parts):
            dead = (res_cols[p * jrows : (p + 1) * jrows] - 1.0) * 1000000000.0
            mask = jnp.where(part_of == p, dead, mask)
        mask_out[c] = mask
    for k in range(1, n_col):
        other = lax.rem(col + k, n_col)
        unless_relayed(other, lambda: chunks(other, early, logits_recv.at[other]))

    def keep(s, values):
        early_out[s] = values

    average_rows(
        here,
        range(early),
        slots,
        mask_out,
        norm_high[...].reshape(n_row * rows, seqs * width),
        norm_low[...].reshape(n_row * rows, seqs * width),
        gate_out,
        value_bd,
        output_bd,
        align_ref,
        keep,
    )
    blocks(right_ref, half, share_send)
    blocks(right_ref, half - 1, right_send)
    for k in range(1, n_col):
        near(lax.rem(col + k, n_col), left_copy(k).wait_send)

    @pl.when(away)
    def _():
        turn.wait_send()

    if relayed:

        @pl.when(relay)
        def _():
            left_forward().wait_send()
            chunks(far_src, first, logits_send.at[0])

    blocks(norm_all, half - 1, norm_send)
    blocks(norm_all, half, relay_send)
    for k in range(1, n_col):
        other = lax.rem(col + k, n_col)
        if relayed:
            near(other, lambda: chunks(col, steps, logits_send.at[k]))
            pl.when(is_far(other))(lambda: chunks(col, direct, logits_send.at[k]))
        else:
            chunks(col, steps, logits_send.at[k])
        last = logits_recv.at[n_col + other]
        unless_relayed(other, lambda: chunks(other, steps - early, last))
        if relayed:
            pl.when(relay & (other == far_src))(lambda: chunks(other, direct, last))


def average_rows(
    here, taken, slots, mask_ref, norm_high, norm_low, gate_ref, value_bd, output_bd, align_ref, store
):
    seqs, rows, width = align_ref.shape
    n_col, total_rows, _ = slots.shape
    groups, heads = gate_ref.shape[0], gate_ref.shape[1]
    group = seqs // groups
    jrows = total_rows // (rows // here)
    wide = here * heads
    parts = LANES // wide
    own_rows = slice(taken[0] * here, (taken[-1] + 1) * here)
    part_of = iota((jrows, LANES), 1) // wide

    def over_parts(values, combine):
        out = values
        for p in range(1, parts):
            out = combine(out, pltpu.roll(values, p * wide, 1))
        return out

    weights = []
    for t in taken:
        pieces = [
            slots[c, t * jrows : (t + 1) * jrows, :] + mask_ref[c] for c in range(n_col)
        ]
        top = pieces[0]
        for piece in pieces[1:]:
            top = jnp.maximum(top, piece)
        top = over_parts(jnp.max(top, axis=0, keepdims=True), jnp.maximum)
        pieces = [jnp.exp(piece - top) for piece in pieces]
        total = pieces[0]
        for piece in pieces[1:]:
            total = total + piece
        inverse = 1.0 / over_parts(jnp.sum(total, axis=0, keepdims=True), jnp.add)
        weights.append([piece * inverse for piece in pieces])
    turned = []
    for t in range(0, len(taken), parts):
        blocks = []
        for c in range(n_col):
            for p in range(parts):
                block = None
                for q in range(parts):
                    value = weights[t + q][c]
                    shift = (q - p) % parts * wide
                    if shift:
                        value = pltpu.roll(value, shift, 1)
                    block = value if block is None else jnp.where(part_of == q, value, block)
                blocks.append(block)
        turned.append(jnp.concatenate(blocks, axis=0).T)
    mixed = dot_split(jnp.concatenate(turned, axis=0), norm_high, norm_low)
    count = len(taken) * here
    gated = []
    for h in range(heads):
        own = jnp.concatenate(
            [
                mixed[
                    t * wide + h * here : t * wide + (h + 1) * here,
                    g * group * width : (g + 1) * group * width,
                ]
                for g in range(groups)
                for t in range(len(taken))
            ],
            axis=0,
        )
        gate = jnp.concatenate([gate_ref[g, h, own_rows, :] for g in range(groups)], axis=0)
        gated.append(stacked_dot(own, value_bd[h]) * gate)
    out = None
    for hp in range(heads // 2):
        part = dot_split(
            jnp.concatenate(gated[2 * hp : 2 * hp + 2], axis=1),
            output_bd[0, hp],
            output_bd[1, hp],
        )
        out = part if out is None else out + part
    for g in range(groups):
        for s in range(group):
            at = g * group + s
            change = out[g * count : (g + 1) * count, s * width : (s + 1) * width]
            store(at, align_ref[at, own_rows, :] + change)


def average_kernel(
    here,
    early,
    slots,
    mask_ref,
    norm_high,
    norm_low,
    gate_ref,
    value_bd,
    output_bd,
    align_ref,
    early_ref,
    pair_ref,
    out_any,
    pair_any,
    out_buf,
    sems,
):
    rows = align_ref.shape[1]
    steps = rows // here
    first = early * here
    copies = [
        pltpu.make_async_copy(pair_ref, pair_any, sems.at[0]),
        pltpu.make_async_copy(early_ref, out_any.at[:, pl.ds(0, first), :], sems.at[1]),
        pltpu.make_async_copy(out_buf, out_any.at[:, pl.ds(first, rows - first), :], sems.at[2]),
    ]
    copies[0].start()
    copies[1].start()

    def keep(s, values):
        out_buf[s] = values

    average_rows(
        here,
        range(early, steps),
        slots,
        mask_ref,
        norm_high[...],
        norm_low[...],
        gate_ref,
        value_bd,
        output_bd,
        align_ref,
        keep,
    )
    copies[2].start()
    for copy in copies:
        copy.wait()


def per_device(
    n_row,
    n_col,
    alignment,
    pair_rep,
    seq_mask,
    res_mask,
    left_weight,
    right_weight,
    w_outer,
    w_logits,
    value_weight,
    gate_weight,
    output_weight,
):
    seqs, rows, width = alignment.shape
    cols, pair_width = pair_rep.shape[1], pair_rep.shape[2]
    factor = left_weight.shape[1]
    heads = w_logits.shape[1]
    channels = value_weight.shape[1]
    k_col = factor * seqs
    quarter = rows * seqs // 4
    half = n_row // 2
    here = 8
    steps = rows // here
    early = LANES // (here * heads)
    jrows = cols * here * heads // LANES
    group = LANES * heads // channels
    groups = seqs // group
    vmem = pl.BlockSpec(memory_space=pltpu.VMEM)
    anywhere = pl.BlockSpec(memory_space=pl.ANY)
    dma = pltpu.SemaphoreType.DMA
    left_shape = (quarter + 8, 4 * factor)
    right_shape = (rows, k_col)
    mix_row = (n_col, factor // 2, 2 * seqs, pair_width)
    row_bytes = 4 * n_col * k_col * pair_width
    premixed = rows * row_bytes <= MIX_BYTES
    held = rows if premixed else here
    pair_new, slots, mask, norm_high, norm_low, gate, value_bd, output_bd, align, started = pl.pallas_call(
        functools.partial(pair_kernel, n_row, n_col, here, early),
        out_shape=(
            pltpu.VMEM(pair_rep.shape, F32),
            pltpu.VMEM((n_col, steps * jrows, LANES), F32),
            pltpu.VMEM((n_col, jrows, LANES), F32),
            pltpu.VMEM((n_row, rows, seqs * width), BF16),
            pltpu.VMEM((n_row, rows, seqs * width), BF16),
            pltpu.VMEM((groups, heads, rows, LANES), F32),
            pltpu.VMEM((heads, group * width, 2 * LANES), BF16),
            pltpu.VMEM((2, heads // 2, 2 * LANES, group * width), BF16),
            pltpu.VMEM(alignment.shape, F32),
            pltpu.VMEM((seqs, early * here, width), F32),
        ),
        in_specs=[anywhere] * 11,
        out_specs=(vmem,) * 10,
        scratch_shapes=[
            pltpu.SMEM((seqs,), jnp.int32),
            pltpu.VMEM((1, rows), jnp.int32),
            pltpu.VMEM((factor, width), F32),
            pltpu.VMEM((factor, width), F32),
            pltpu.VMEM(w_outer.shape, F32),
            pltpu.VMEM((heads, pair_width), F32),
            pltpu.VMEM(value_weight.shape, F32),
            pltpu.VMEM(gate_weight.shape, F32),
            pltpu.VMEM((width, channels), F32),
            pltpu.VMEM((n_row, rows + 8, seqs * width), F32),
            pltpu.VMEM((rows * seqs, width), F32),
            pltpu.VMEM((rows, seqs * width), F32),
            pltpu.VMEM((k_col, seqs * width), F32),
            pltpu.VMEM((k_col, seqs * width), BF16),
            pltpu.VMEM((k_col, seqs * width), BF16),
            pltpu.VMEM(right_shape, F32),
            pltpu.VMEM((n_col,) + left_shape, F32),
            pltpu.VMEM((n_row,) + right_shape, F32),
            pltpu.VMEM((heads, group * width, 2 * LANES), BF16),
            pltpu.VMEM((here // 2, 2 * pair_width, 2 * LANES), BF16),
            pltpu.VMEM((3 * factor, factor * pair_width), BF16),
            pltpu.VMEM((1 if premixed else n_col, rows * seqs, 3 * factor), BF16),
            pltpu.VMEM((2 * cols, n_col * k_col), BF16),
            pltpu.VMEM((held,) + mix_row, BF16),
            pltpu.VMEM((held,) + mix_row, BF16),
            pltpu.VMEM(pair_rep.shape, F32),
            dma((11,)),
            dma((n_col,)),
            dma((n_col,)),
            dma((2,)),
            dma,
            dma((half - 1,)),
            dma,
            dma,
            dma((n_col,)),
            dma((2 * n_col + steps,)),
            dma,
            dma,
            dma,
            dma,
        ],
        compiler_params=pltpu.CompilerParams(
            collective_id=0, has_side_effects=True, vmem_limit_bytes=PAIR_VMEM
        ),
        name="pair",
    )(
        seq_mask,
        res_mask.reshape(1, rows),
        alignment,
        left_weight.T,
        right_weight.T,
        w_outer,
        w_logits.T,
        value_weight,
        gate_weight,
        output_weight.T,
        pair_rep,
    )
    alignment_out, pair_final = pl.pallas_call(
        functools.partial(average_kernel, here, early),
        out_shape=(
            jax.ShapeDtypeStruct(alignment.shape, F32),
            jax.ShapeDtypeStruct(pair_rep.shape, F32),
        ),
        in_specs=[vmem] * 10,
        out_specs=(anywhere, anywhere),
        scratch_shapes=[pltpu.VMEM((seqs, (steps - early) * here, width), F32), dma((3,))],
        compiler_params=pltpu.CompilerParams(vmem_limit_bytes=AVERAGE_VMEM),
        name="average",
    )(
        slots,
        mask,
        norm_high.reshape(n_row * rows, seqs * width),
        norm_low.reshape(n_row * rows, seqs * width),
        gate,
        value_bd,
        output_bd,
        align,
        started,
        pair_new,
    )
    return (alignment_out, pair_final)


def solution(mesh):
    in_specs = (P("col", "row", None), P("row", "col", None), P("col"), P("row")) + (P(),) * 7
    out_specs = (P("col", "row", None), P("row", "col", None))
    return jax.shard_map(
        functools.partial(per_device, mesh.shape["row"], mesh.shape["col"]),
        mesh=mesh,
        in_specs=in_specs,
        out_specs=out_specs,
        check_vma=False,
    )
```

```python
import functools

import jax
import jax.numpy as jnp
from jax import lax
from jax.experimental import pallas as pl
from jax.experimental.pallas import tpu as pltpu
from jax.sharding import PartitionSpec as P

MESH = pl.DeviceIdType.MESH
F32 = jnp.float32
BF16 = jnp.bfloat16
epsilon = 1e-05
PAIR_VMEM = 48 * 1024 * 1024
AVERAGE_VMEM = 24 * 1024 * 1024
MIX_BYTES = 30 * 1024 * 1024
LANES = 128


def layer_norm(values):
    center = jnp.mean(values, axis=-1, keepdims=True)
    centred = values - center
    return centred * lax.rsqrt(jnp.mean(centred * centred, axis=-1, keepdims=True) + epsilon)


def split(values):
    high = values.astype(BF16)
    return high, (values - high.astype(F32)).astype(BF16)


def dot(left, right):
    return jnp.dot(left, right, preferred_element_type=F32)


def dot_t(left, right):
    return lax.dot_general(left, right, (((1,), (1,)), ((), ())), preferred_element_type=F32)


def t_dot(left, right):
    return lax.dot_general(left, right, (((0,), (0,)), ((), ())), preferred_element_type=F32)


def dot_split(left, right_high, right_low, multiply=dot):
    high, low = split(left)
    return multiply(high, right_high) + (multiply(low, right_high) + multiply(high, right_low))


def iota(shape, axis):
    return lax.broadcasted_iota(jnp.int32, shape, axis)


def stacked_dot(values, weights):
    count, half = values.shape[0], weights.shape[1] // 2
    high, low = split(values)
    out = dot(jnp.concatenate([high, low], axis=0), weights)
    out = out[:, :half] + out[:, half:]
    return out[:count] + out[count:]


def spread_heads(weight, heads, group, store):
    width, channels = weight.shape
    head_width = channels // heads
    both = jnp.concatenate(split(weight), axis=0)
    rows, lanes = iota((channels, LANES), 0), iota((channels, LANES), 1)
    own = iota((group * width, LANES), 0) // width == iota((group * width, LANES), 1) // head_width
    for h in range(heads):
        pick = jnp.where(rows == h * head_width + lanes % head_width, 1.0, 0.0).astype(BF16)
        tiled = dot(both, pick)
        parts = []
        for t in range(2):
            piece = jnp.concatenate([tiled[t * width : (t + 1) * width]] * group, axis=0)
            parts.append(jnp.where(own, piece, 0.0))
        store(h, jnp.concatenate(parts, axis=1).astype(BF16))


def pair_kernel(
    n_row,
    n_col,
    here,
    early,
    seq_in,
    res_in,
    align_in,
    left_w_in,
    right_w_in,
    outer_in,
    logits_w_in,
    value_w_in,
    gate_w_in,
    output_w_in,
    pair_in,
    pair_out,
    slots,
    mask_out,
    norm_high,
    norm_low,
    gate_out,
    value_bd,
    output_bd,
    align_ref,
    early_out,
    seq_ref,
    res_ref,
    left_w_ref,
    right_w_ref,
    outer_ref,
    logits_w_ref,
    value_w_ref,
    gate_w_ref,
    output_w_ref,
    norm_all,
    rows_buf,
    masked_buf,
    block_buf,
    block_high,
    block_low,
    right_buf,
    left_ref,
    right_ref,
    gate_bd,
    wl_buf,
    w_buf,
    l_buf,
    r_buf,
    high_buf,
    low_buf,
    pair_ref,
    load_sem,
    left_send,
    left_recv,
    turn_sem,
    right_send,
    right_recv,
    share_send,
    share_recv,
    logits_send,
    logits_recv,
    norm_send,
    norm_recv,
    relay_send,
    relay_recv,
):
    row, col = lax.axis_index("row"), lax.axis_index("col")
    barrier = pltpu.get_barrier_semaphore()
    loads = [
        pltpu.make_async_copy(source, target, load_sem.at[at])
        for at, (source, target) in enumerate(
            [
                (right_w_in, right_w_ref),
                (res_in, res_ref),
                (left_w_in, left_w_ref),
                (seq_in, seq_ref),
                (align_in, align_ref),
                (outer_in, outer_ref),
                (gate_w_in, gate_w_ref),
                (value_w_in, value_w_ref),
                (logits_w_in, logits_w_ref),
                (output_w_in, output_w_ref),
                (pair_in, pair_ref),
            ]
        )
    ]
    for load in loads:
        load.start()

    seqs, rows, width = align_ref.shape
    factor = right_w_ref.shape[0]
    ratio, k_col = n_row // n_col, factor * seqs
    half = n_row // 2
    chip, core = row // 2, lax.rem(row, 2)
    partner = 2 * chip + 1 - core
    cols, pair_width = pair_out.shape[1], pair_out.shape[2]
    heads = logits_w_ref.shape[0]
    quarter = rows * seqs // 4
    steps = rows // here
    parts = LANES // (here * heads)
    jrows = cols // parts
    group = LANES * heads // value_w_ref.shape[1]
    premixed = high_buf.shape[0] == rows
    depth = n_col * k_col

    def peer_row(k):
        return 2 * lax.rem(chip + k, half) + core

    relayed = n_col >= 4
    at_high, at_low = col == n_col - 2, col == 1
    relay = at_high | at_low
    far_src = jnp.where(at_low, n_col - 1, 0)
    far_dest = jnp.where(at_low, 0, n_col - 1)

    def is_far(other):
        return (other - col == n_col - 1) | (col - other == n_col - 1)

    def near(other, action):
        if relayed:
            pl.when(jnp.logical_not(is_far(other)))(action)
        else:
            action()

    def unless_relayed(src, action):
        if relayed:
            pl.when(jnp.logical_not(relay & (src == far_src)))(action)
        else:
            action()

    dest = row // ratio
    spot = col * ratio + lax.rem(row, ratio)
    away = dest != col

    def meet(action):
        for k in range(1, n_col):
            other = lax.rem(col + k, n_col)
            near(other, functools.partial(action, row, other))
        for k in range(1, half):
            action(peer_row(k), col)
        action(partner, col)
        pl.when(away)(functools.partial(action, spot, dest))

    def greet(other_row, other_col):
        pl.semaphore_signal(
            barrier, inc=1, device_id=(other_row, other_col), device_id_type=MESH
        )

    greeters = half + n_col - 1 + jnp.where(away, 1, 0)
    if relayed:
        greeters = greeters - jnp.where((col == 0) | (col == n_col - 1), 1, 0)
    meet(greet)
    for at in range(4):
        loads[at].wait()
    res_row = res_ref[...].astype(F32)
    diag = iota((rows, rows), 0) == iota((rows, rows), 1)

    def column(values):
        return jnp.sum(
            jnp.where(diag, jnp.broadcast_to(values, (rows, rows)), 0.0), axis=1, keepdims=True
        )

    res_col = column(res_row)
    spread = jnp.broadcast_to(right_w_ref[...][:, None, :], (factor, seqs, width))
    row_seq = iota((factor, seqs, width), 1)
    for s in range(seqs):
        block_buf[:, s * width : (s + 1) * width] = jnp.where(row_seq == s, spread, 0.0).reshape(
            factor * seqs, width
        )
    wr_high, wr_low = split(block_buf[...])
    block_high[...] = wr_high
    block_low[...] = wr_low
    wl_high, wl_low = split(left_w_ref[...])
    norm_all[row, rows : rows + 8, 0:rows] = jnp.broadcast_to(res_row, (8, rows))
    norm_all[row, rows : rows + 8, rows:] = jnp.zeros((8, seqs * width - rows), F32)
    loads[4].wait()
    seq_sum = 0.0
    for s in range(seqs):
        normed = layer_norm(align_ref[s])
        norm_all[row, 0:rows, s * width : (s + 1) * width] = normed
        live = seq_ref[s].astype(F32)
        seq_sum = seq_sum + live
        masked_buf[:, s * width : (s + 1) * width] = normed * (res_col * live)
    right_buf[...] = dot_split(masked_buf[...], block_high[...], block_low[...], dot_t)
    pl.semaphore_wait(barrier, greeters)
    turn = pltpu.make_async_remote_copy(
        right_buf,
        right_ref.at[spot],
        turn_sem.at[0],
        turn_sem.at[1],
        device_id=(spot, dest),
        device_id_type=MESH,
    )
    stay = pltpu.make_async_copy(right_buf, right_ref.at[spot], turn_sem.at[1])

    @pl.when(away)
    def _():
        turn.start()

    @pl.when(jnp.logical_not(away))
    def _():
        stay.start()

    for s in range(seqs):
        rows_buf[pl.ds(s, rows, stride=seqs), :] = masked_buf[:, s * width : (s + 1) * width]
    left = dot_split(rows_buf[...], wl_high, wl_low, dot_t)
    for g in range(4):
        left_ref[col, 0:quarter, g * factor : (g + 1) * factor] = left[
            g * quarter : (g + 1) * quarter
        ]
    left_ref[col, quarter : quarter + 8, :] = jnp.full((8, left_ref.shape[2]), seq_sum, F32)

    def left_copy(k):
        return pltpu.make_async_remote_copy(
            left_ref.at[col],
            left_ref.at[col],
            left_send.at[k],
            left_recv.at[col],
            device_id=(row, lax.rem(col + k, n_col)),
            device_id_type=MESH,
        )

    def left_forward():
        return pltpu.make_async_remote_copy(
            left_ref.at[far_src],
            left_ref.at[far_src],
            left_send.at[0],
            left_recv.at[far_src],
            device_id=(row, far_dest),
            device_id_type=MESH,
        )

    def left_wait(src):
        pltpu.make_async_copy(left_ref.at[src], left_ref.at[src], left_recv.at[src]).wait()

    def right_copy(k):
        return pltpu.make_async_remote_copy(
            right_ref.at[row],
            right_ref.at[row],
            right_send,
            right_recv.at[half - k - 1],
            device_id=(peer_row(k), col),
            device_id_type=MESH,
        )

    def share_copy(k):
        src = peer_row(k)
        return pltpu.make_async_remote_copy(
            right_ref.at[src],
            right_ref.at[src],
            share_send,
            share_recv,
            device_id=(partner, col),
            device_id_type=MESH,
        )

    def norm_copy(k):
        return pltpu.make_async_remote_copy(
            norm_all.at[row],
            norm_all.at[row],
            norm_send,
            norm_recv,
            device_id=(peer_row(k), col),
            device_id_type=MESH,
        )

    def relay_copy(k):
        return pltpu.make_async_remote_copy(
            norm_all.at[peer_row(k)],
            norm_all.at[peer_row(k)],
            relay_send,
            relay_recv,
            device_id=(partner, col),
            device_id_type=MESH,
        )

    loads[5].wait()
    for b in range(factor):
        high, low = split(outer_ref[pl.ds(b, factor, stride=factor), :])
        lanes = slice(b * pair_width, (b + 1) * pair_width)
        w_buf[0:factor, lanes] = high
        w_buf[factor : 2 * factor, lanes] = low
        w_buf[2 * factor : 3 * factor, lanes] = high

    def left_rows(c, at):
        packed = left_ref[c, 0:quarter, :]
        high = packed.astype(BF16).astype(F32)
        low = packed - high
        for g in range(4):
            lanes = slice(g * factor, (g + 1) * factor)
            pieces = [high[:, lanes], high[:, lanes], low[:, lanes]]
            l_buf[at, g * quarter : (g + 1) * quarter, :] = jnp.concatenate(
                pieces, axis=1
            ).astype(BF16)

    def mix(l_rows, c, count):
        for nb in range(factor // 2):
            mixed = dot(l_rows, w_buf[:, nb * 2 * pair_width : (nb + 1) * 2 * pair_width])
            tiles = jnp.concatenate(
                [
                    mixed[:, :pair_width].reshape(count, seqs, pair_width),
                    mixed[:, pair_width:].reshape(count, seqs, pair_width),
                ],
                axis=1,
            )
            high, low = split(tiles)
            high_buf[:, c, nb] = high
            low_buf[:, c, nb] = low

    def prepare():
        for at in range(6, 11):
            loads[at].wait()

        def keep_value(h, block):
            value_bd[h] = block

        def keep_gate(h, block):
            gate_bd[h] = block

        spread_heads(gate_w_ref[...], heads, group, keep_gate)
        spread_heads(value_w_ref[...], heads, group, keep_value)
        groups = seqs // group
        own = jnp.concatenate(
            [
                norm_all[row, 0:rows, g * group * width : (g + 1) * group * width]
                for g in range(groups)
            ],
            axis=0,
        )
        for h in range(heads):
            gate = jax.nn.sigmoid(stacked_dot(own, gate_bd[h]))
            for g in range(groups):
                gate_out[g, h] = gate[g * rows : (g + 1) * rows]
        channels = output_w_ref.shape[1]
        head_width = channels // heads
        lanes = iota((width, group * width), 1)
        pick = jnp.where(iota((width, group * width), 0) == lanes % width, 1.0, 0.0).astype(BF16)
        own = (iota((2 * group * head_width, group * width), 0) // head_width) % group == iota(
            (2 * group * head_width, group * width), 1
        ) // width
        for t, half_w in enumerate(split(output_w_ref[...])):
            tiled = t_dot(half_w, pick)
            for hp in range(heads // 2):
                pieces = []
                for hh in range(2):
                    first = (2 * hp + hh) * head_width
                    pieces += [tiled[first : first + head_width]] * group
                output_bd[t, hp] = jnp.where(own, jnp.concatenate(pieces, axis=0), 0.0).astype(BF16)
        lanes = iota((heads, 2 * LANES), 1)
        low_half = iota((pair_width, 2 * LANES), 1) >= LANES
        w_high, w_low = split(logits_w_ref[...])
        for i in range(here):
            pick = jnp.where(
                ((lanes // here) % heads == iota((heads, 2 * LANES), 0)) & (lanes % here == i),
                1.0,
                0.0,
            ).astype(BF16)
            block = jnp.where(low_half, t_dot(w_low, pick), t_dot(w_high, pick))
            wl_buf[i // 2, (i % 2) * pair_width : (i % 2 + 1) * pair_width, :] = block.astype(BF16)

    low_end = col < (n_col + 1) // 2
    spot_in = jnp.where(low_end, col, n_col - 1 - col)

    def stage(k, carry):
        order = jnp.where(k - 1 < spot_in, k - 1, k)
        src = jnp.where(low_end, order, n_col - 1 - order)
        src = jnp.where(k == 0, col, src)

        @pl.when(k == 1)
        def _():
            for k2 in sorted(range(1, n_col), key=lambda d: min(d, n_col - d)):
                near(lax.rem(col + k2, n_col), left_copy(k2).start)
            prepare()
            pltpu.make_async_copy(right_buf, right_ref.at[row], turn_sem.at[1]).wait()
            odd = lax.rem(chip, 2)
            right_copy(half - 1 - odd * (half - 2)).start()
            right_copy(1 + odd * (half - 2)).start()
            for k2 in range(2, half - 1):
                right_copy(k2).start()
            share_copy(0).start()
            if relayed:

                @pl.when(relay)
                def _():
                    left_wait(far_src)
                    left_forward().start()

        @pl.when(k == n_col - 1)
        def _():
            for k2 in range(1, half):
                pltpu.make_async_copy(
                    right_buf, right_ref.at[peer_row(k2)], right_recv.at[k2 - 1]
                ).wait()
                share_copy(k2).start()

        @pl.when(k > 0)
        def _():
            unless_relayed(src, lambda: left_wait(src))

        at = 0 if premixed else src
        left_rows(src, at)
        if premixed:
            mix(l_buf[0], src, rows)
        return carry

    lax.fori_loop(0, n_col, stage, 0)
    def blocks(ref, number, sem):
        pltpu.make_async_copy(ref.at[pl.ds(0, number)], ref.at[pl.ds(0, number)], sem).wait()

    blocks(right_ref, half, share_recv)
    count = left_ref[0, quarter : quarter + 1, 0:1]
    for c in range(1, n_col):
        count = count + left_ref[c, quarter : quarter + 1, 0:1]
    scale = 1.0 / jnp.maximum(count, 1.0)
    for c in range(n_col):
        for t in range(ratio):
            high_r, low_r = split(right_ref[c * ratio + t])
            lanes = slice(c * k_col, (c + 1) * k_col)
            r_buf[t * rows : (t + 1) * rows, lanes] = high_r
            r_buf[cols + t * rows : cols + (t + 1) * rows, lanes] = low_r
    part_of = iota((jrows, LANES), 1) // (here * heads)

    def chunk(at):
        return pl.ds(pl.multiple_of(at * jrows, jrows), jrows)

    lag, direct = 2, 1
    first = steps - direct

    def logits_copy(k, at):
        other = lax.rem(col + k, n_col)
        sem = jnp.where(at < early, col, n_col + col)
        if relayed:
            passed = (at < first) & (
                ((col == 0) & (other == n_col - 2)) | ((col == n_col - 1) & (other == 1))
            )
            sem = jnp.where(passed, 2 * n_col + at, sem)
        return pltpu.make_async_remote_copy(
            slots.at[col, chunk(at)],
            slots.at[col, chunk(at)],
            logits_send.at[k],
            logits_recv.at[sem],
            device_id=(row, other),
            device_id_type=MESH,
        )

    def logits_forward(at):
        return pltpu.make_async_remote_copy(
            slots.at[far_src, chunk(at)],
            slots.at[far_src, chunk(at)],
            logits_send.at[0],
            logits_recv.at[jnp.where(at < early, far_src, n_col + far_src)],
            device_id=(row, far_dest),
            device_id_type=MESH,
        )

    def chunks(src, number, sem):
        part = slots.at[src, pl.ds(0, number * jrows)]
        pltpu.make_async_copy(part, part, sem).wait()

    def pass_on(at):
        @pl.when(relay)
        def _():
            chunks(far_src, 1, logits_recv.at[2 * n_col + at])
            logits_forward(at).start()

    def body(step, carry):
        first_row = pl.multiple_of(step * here, here)
        if not premixed:
            size = here * seqs
            for c in range(n_col):
                mix(l_buf[c, pl.ds(pl.multiple_of(step * size, size), size), :], c, here)
        r_both = r_buf[...]
        for p in range(here // 2):
            at = [2 * p + t + (first_row if premixed else 0) for t in range(2)]
            right_high = jnp.concatenate(
                [high_buf[i].reshape(depth, pair_width) for i in at], axis=1
            )
            right_low = jnp.concatenate([low_buf[i].reshape(depth, pair_width) for i in at], axis=1)
            product = dot(r_both, right_high)
            sums = product[:cols] + (product[cols:] + dot(r_both[:cols], right_low))
            for t in range(2):
                i = first_row + 2 * p + t
                pair_out[i] = pair_ref[i] + sums[:, t * pair_width : (t + 1) * pair_width] * scale
        total = None
        batch = here
        for g in range(0, here, batch):
            pairs = pair_out[pl.ds(first_row + g, batch)].reshape(batch * cols, pair_width)
            high, low = split(layer_norm(pairs))
            for p in range(batch // 2):
                both = jnp.concatenate(
                    [
                        jnp.concatenate(
                            [
                                half_x[(2 * p + t) * cols : (2 * p + t + 1) * cols]
                                for t in range(2)
                            ],
                            axis=1,
                        )
                        for half_x in (high, low)
                    ],
                    axis=0,
                )
                out = dot(both, wl_buf[g // 2 + p])
                out = out[:, :LANES] + out[:, LANES:]
                out = out[:cols] + out[cols:]
                total = out if total is None else total + out
        logits = total[:jrows]
        for p in range(1, parts):
            logits = jnp.where(part_of == p, total[p * jrows : (p + 1) * jrows], logits)
        slots[col, chunk(step), :] = logits
        for k in range(1, n_col):
            other = lax.rem(col + k, n_col)
            if relayed:
                pl.when(jnp.logical_not(is_far(other)) | (step >= steps - direct))(
                    logits_copy(k, step).start
                )
            else:
                logits_copy(k, step).start()
        if relayed:

            @pl.when(step >= lag)
            def _():
                pass_on(step - lag)

        @pl.when(step == steps - 2)
        def _():
            blocks(norm_all, half - 1, norm_recv)
            for k in range(1, half):
                relay_copy(k).start()

        return carry

    relay_copy(0).start()
    for k in range(1, half):
        norm_copy(k).start()
    lax.fori_loop(0, steps, body, 0)
    if relayed:
        for at in range(steps - lag, first):
            pass_on(at)
    blocks(norm_all, half, relay_recv)
    for r in range(n_row):
        high, low = split(norm_all[r, 0:rows, :])
        norm_high[r] = high
        norm_low[r] = low
    for c in range(n_col):
        res_cols = jnp.concatenate(
            [column(norm_all[c * ratio + t, rows : rows + 1, 0:rows]) for t in range(ratio)],
            axis=0,
        )
        mask = jnp.zeros((jrows, LANES), F32)
        for p in range(parts):
            dead = (res_cols[p * jrows : (p + 1) * jrows] - 1.0) * 1000000000.0
            mask = jnp.where(part_of == p, dead, mask)
        mask_out[c] = mask
    for k in range(1, n_col):
        other = lax.rem(col + k, n_col)
        unless_relayed(other, lambda: chunks(other, early, logits_recv.at[other]))

    def keep(s, values):
        early_out[s] = values

    average_rows(
        here,
        range(early),
        slots,
        mask_out,
        norm_high[...].reshape(n_row * rows, seqs * width),
        norm_low[...].reshape(n_row * rows, seqs * width),
        gate_out,
        value_bd,
        output_bd,
        align_ref,
        keep,
    )
    blocks(right_ref, half, share_send)
    blocks(right_ref, half - 1, right_send)
    for k in range(1, n_col):
        near(lax.rem(col + k, n_col), left_copy(k).wait_send)

    @pl.when(away)
    def _():
        turn.wait_send()

    if relayed:

        @pl.when(relay)
        def _():
            left_forward().wait_send()
            chunks(far_src, first, logits_send.at[0])

    blocks(norm_all, half - 1, norm_send)
    blocks(norm_all, half, relay_send)
    for k in range(1, n_col):
        other = lax.rem(col + k, n_col)
        if relayed:
            near(other, lambda: chunks(col, steps, logits_send.at[k]))
            pl.when(is_far(other))(lambda: chunks(col, direct, logits_send.at[k]))
        else:
            chunks(col, steps, logits_send.at[k])
        last = logits_recv.at[n_col + other]
        unless_relayed(other, lambda: chunks(other, steps - early, last))
        if relayed:
            pl.when(relay & (other == far_src))(lambda: chunks(other, direct, last))


def average_rows(
    here, taken, slots, mask_ref, norm_high, norm_low, gate_ref, value_bd, output_bd, align_ref, store
):
    seqs, rows, width = align_ref.shape
    n_col, total_rows, _ = slots.shape
    groups, heads = gate_ref.shape[0], gate_ref.shape[1]
    group = seqs // groups
    jrows = total_rows // (rows // here)
    wide = here * heads
    parts = LANES // wide
    own_rows = slice(taken[0] * here, (taken[-1] + 1) * here)
    part_of = iota((jrows, LANES), 1) // wide

    def over_parts(values, combine):
        out = values
        for p in range(1, parts):
            out = combine(out, pltpu.roll(values, p * wide, 1))
        return out

    weights = []
    for t in taken:
        pieces = [
            slots[c, t * jrows : (t + 1) * jrows, :] + mask_ref[c] for c in range(n_col)
        ]
        top = pieces[0]
        for piece in pieces[1:]:
            top = jnp.maximum(top, piece)
        top = over_parts(jnp.max(top, axis=0, keepdims=True), jnp.maximum)
        pieces = [jnp.exp(piece - top) for piece in pieces]
        total = pieces[0]
        for piece in pieces[1:]:
            total = total + piece
        inverse = 1.0 / over_parts(jnp.sum(total, axis=0, keepdims=True), jnp.add)
        weights.append([piece * inverse for piece in pieces])
    turned = []
    for t in range(0, len(taken), parts):
        blocks = []
        for c in range(n_col):
            for p in range(parts):
                block = None
                for q in range(parts):
                    value = weights[t + q][c]
                    shift = (q - p) % parts * wide
                    if shift:
                        value = pltpu.roll(value, shift, 1)
                    block = value if block is None else jnp.where(part_of == q, value, block)
                blocks.append(block)
        turned.append(jnp.concatenate(blocks, axis=0).T)
    mixed = dot_split(jnp.concatenate(turned, axis=0), norm_high, norm_low)
    count = len(taken) * here
    gated = []
    for h in range(heads):
        own = jnp.concatenate(
            [
                mixed[
                    t * wide + h * here : t * wide + (h + 1) * here,
                    g * group * width : (g + 1) * group * width,
                ]
                for g in range(groups)
                for t in range(len(taken))
            ],
            axis=0,
        )
        gate = jnp.concatenate([gate_ref[g, h, own_rows, :] for g in range(groups)], axis=0)
        gated.append(stacked_dot(own, value_bd[h]) * gate)
    out = None
    for hp in range(heads // 2):
        part = dot_split(
            jnp.concatenate(gated[2 * hp : 2 * hp + 2], axis=1),
            output_bd[0, hp],
            output_bd[1, hp],
        )
        out = part if out is None else out + part
    for g in range(groups):
        for s in range(group):
            at = g * group + s
            change = out[g * count : (g + 1) * count, s * width : (s + 1) * width]
            store(at, align_ref[at, own_rows, :] + change)


def average_kernel(
    here,
    early,
    slots,
    mask_ref,
    norm_high,
    norm_low,
    gate_ref,
    value_bd,
    output_bd,
    align_ref,
    early_ref,
    pair_ref,
    out_any,
    pair_any,
    out_buf,
    sems,
):
    rows = align_ref.shape[1]
    steps = rows // here
    first = early * here
    copies = [
        pltpu.make_async_copy(pair_ref, pair_any, sems.at[0]),
        pltpu.make_async_copy(early_ref, out_any.at[:, pl.ds(0, first), :], sems.at[1]),
        pltpu.make_async_copy(out_buf, out_any.at[:, pl.ds(first, rows - first), :], sems.at[2]),
    ]
    copies[0].start()
    copies[1].start()

    def keep(s, values):
        out_buf[s] = values

    average_rows(
        here,
        range(early, steps),
        slots,
        mask_ref,
        norm_high[...],
        norm_low[...],
        gate_ref,
        value_bd,
        output_bd,
        align_ref,
        keep,
    )
    copies[2].start()
    for copy in copies:
        copy.wait()


def per_device(
    n_row,
    n_col,
    alignment,
    pair_rep,
    seq_mask,
    res_mask,
    left_weight,
    right_weight,
    w_outer,
    w_logits,
    value_weight,
    gate_weight,
    output_weight,
):
    seqs, rows, width = alignment.shape
    cols, pair_width = pair_rep.shape[1], pair_rep.shape[2]
    factor = left_weight.shape[1]
    heads = w_logits.shape[1]
    channels = value_weight.shape[1]
    k_col = factor * seqs
    quarter = rows * seqs // 4
    half = n_row // 2
    here = 8
    steps = rows // here
    early = LANES // (here * heads)
    jrows = cols * here * heads // LANES
    group = LANES * heads // channels
    groups = seqs // group
    vmem = pl.BlockSpec(memory_space=pltpu.VMEM)
    anywhere = pl.BlockSpec(memory_space=pl.ANY)
    dma = pltpu.SemaphoreType.DMA
    left_shape = (quarter + 8, 4 * factor)
    right_shape = (rows, k_col)
    mix_row = (n_col, factor // 2, 2 * seqs, pair_width)
    row_bytes = 4 * n_col * k_col * pair_width
    premixed = rows * row_bytes <= MIX_BYTES
    held = rows if premixed else here
    pair_new, slots, mask, norm_high, norm_low, gate, value_bd, output_bd, align, started = pl.pallas_call(
        functools.partial(pair_kernel, n_row, n_col, here, early),
        out_shape=(
            pltpu.VMEM(pair_rep.shape, F32),
            pltpu.VMEM((n_col, steps * jrows, LANES), F32),
            pltpu.VMEM((n_col, jrows, LANES), F32),
            pltpu.VMEM((n_row, rows, seqs * width), BF16),
            pltpu.VMEM((n_row, rows, seqs * width), BF16),
            pltpu.VMEM((groups, heads, rows, LANES), F32),
            pltpu.VMEM((heads, group * width, 2 * LANES), BF16),
            pltpu.VMEM((2, heads // 2, 2 * LANES, group * width), BF16),
            pltpu.VMEM(alignment.shape, F32),
            pltpu.VMEM((seqs, early * here, width), F32),
        ),
        in_specs=[anywhere] * 11,
        out_specs=(vmem,) * 10,
        scratch_shapes=[
            pltpu.SMEM((seqs,), jnp.int32),
            pltpu.VMEM((1, rows), jnp.int32),
            pltpu.VMEM((factor, width), F32),
            pltpu.VMEM((factor, width), F32),
            pltpu.VMEM(w_outer.shape, F32),
            pltpu.VMEM((heads, pair_width), F32),
            pltpu.VMEM(value_weight.shape, F32),
            pltpu.VMEM(gate_weight.shape, F32),
            pltpu.VMEM((width, channels), F32),
            pltpu.VMEM((n_row, rows + 8, seqs * width), F32),
            pltpu.VMEM((rows * seqs, width), F32),
            pltpu.VMEM((rows, seqs * width), F32),
            pltpu.VMEM((k_col, seqs * width), F32),
            pltpu.VMEM((k_col, seqs * width), BF16),
            pltpu.VMEM((k_col, seqs * width), BF16),
            pltpu.VMEM(right_shape, F32),
            pltpu.VMEM((n_col,) + left_shape, F32),
            pltpu.VMEM((n_row,) + right_shape, F32),
            pltpu.VMEM((heads, group * width, 2 * LANES), BF16),
            pltpu.VMEM((here // 2, 2 * pair_width, 2 * LANES), BF16),
            pltpu.VMEM((3 * factor, factor * pair_width), BF16),
            pltpu.VMEM((1 if premixed else n_col, rows * seqs, 3 * factor), BF16),
            pltpu.VMEM((2 * cols, n_col * k_col), BF16),
            pltpu.VMEM((held,) + mix_row, BF16),
            pltpu.VMEM((held,) + mix_row, BF16),
            pltpu.VMEM(pair_rep.shape, F32),
            dma((11,)),
            dma((n_col,)),
            dma((n_col,)),
            dma((2,)),
            dma,
            dma((half - 1,)),
            dma,
            dma,
            dma((n_col,)),
            dma((2 * n_col + steps,)),
            dma,
            dma,
            dma,
            dma,
        ],
        compiler_params=pltpu.CompilerParams(
            collective_id=0, has_side_effects=True, vmem_limit_bytes=PAIR_VMEM
        ),
        name="pair",
    )(
        seq_mask,
        res_mask.reshape(1, rows),
        alignment,
        left_weight.T,
        right_weight.T,
        w_outer,
        w_logits.T,
        value_weight,
        gate_weight,
        output_weight.T,
        pair_rep,
    )
    alignment_out, pair_final = pl.pallas_call(
        functools.partial(average_kernel, here, early),
        out_shape=(
            jax.ShapeDtypeStruct(alignment.shape, F32),
            jax.ShapeDtypeStruct(pair_rep.shape, F32),
        ),
        in_specs=[vmem] * 10,
        out_specs=(anywhere, anywhere),
        scratch_shapes=[pltpu.VMEM((seqs, (steps - early) * here, width), F32), dma((3,))],
        compiler_params=pltpu.CompilerParams(vmem_limit_bytes=AVERAGE_VMEM),
        name="average",
    )(
        slots,
        mask,
        norm_high.reshape(n_row * rows, seqs * width),
        norm_low.reshape(n_row * rows, seqs * width),
        gate,
        value_bd,
        output_bd,
        align,
        started,
        pair_new,
    )
    return (alignment_out, pair_final)


def solution(mesh):
    in_specs = (P("col", "row", None), P("row", "col", None), P("col"), P("row")) + (P(),) * 7
    out_specs = (P("col", "row", None), P("row", "col", None))
    return jax.shard_map(
        functools.partial(per_device, mesh.shape["row"], mesh.shape["col"]),
        mesh=mesh,
        in_specs=in_specs,
        out_specs=out_specs,
        check_vma=False,
    )
```
